32 devices in a mesh: dp: 8 (over z, x), feat: 4 (over y, core).
Axes of the slice: x: 2, y: 2, z: 4, core: 2. Of those that a mesh axis runs over, the one named last changes fastest.
Arguments:
- tokens: bfloat16 [4096, 1024], P('dp', 'feat'), may hold values from -6 to 6
- doc_lengths: int32 [16, 3], P('dp'), may hold values from 1 to 128, 256 in all within a row
- norm_gain: bfloat16 [1024], P('feat'), may hold values from 0.5 to 1.5
- norm_shift: bfloat16 [1024], P('feat'), may hold values from -1.25 to 1.25
- qkv_weight: bfloat16 [1024, 3, 1024], P('dp', None, 'feat'), may hold values from -0.1875 to 0.1875
- qkv_bias: bfloat16 [3, 1024], P(None, 'feat'), may hold values from -1.75 to 1.75
- omega: float32 [64, 64], replicated, may hold values from -4 to 4
- qmc_weights: float32 [64], replicated, may hold values from 0.5 to 2
- out_weight: bfloat16 [1024, 1024], P('feat', 'dp'), may hold values from -1.5 to 1.5
- out_bias: bfloat16 [1024], P('feat'), may hold values from -1.75 to 1.75
- up_weight: bfloat16 [1024, 4096], P('dp', 'feat'), may hold values from -0.1875 to 0.1875
- up_bias: bfloat16 [4096], P('feat'), may hold values from -1.75 to 1.75
- down_weight: bfloat16 [4096, 1024], P('feat', 'dp'), may hold values from -0.09375 to 0.09375
- out_grad: bfloat16 [4096, 1024], P('dp', 'feat'), may hold values from -6 to 6
Outputs:
- block_out: bfloat16 [4096, 1024], P('dp', 'feat')
- input_grad: bfloat16 [4096, 1024], P('dp', 'feat')
- gain_grad: float32 [1024], P('feat')
- shift_grad: float32 [1024], P('feat')
- qkv_weight_grad: float32 [1024, 3, 1024], P('dp', None, 'feat')
- qkv_bias_grad: float32 [3, 1024], P(None, 'feat')
- out_weight_grad: float32 [1024, 1024], P('feat', 'dp')
- out_bias_grad: float32 [1024], P('feat')
- up_weight_grad: float32 [1024, 4096], P('dp', 'feat')
- up_bias_grad: float32 [4096], P('feat')
- down_weight_grad: float32 [4096, 1024], P('feat', 'dp')
The draws below stay inside these ranges and needn't reach their ends.
Inputs may be any that keep to these rules, and one draw needn't show every extreme that they name: `doc_lengths`: each row lists the lengths of the 3 sequences of one micro-batch; they sum to 256, and the longest is exactly 128.
All inputs are finite; a program needn't handle non-finite values.
Results may differ from the reference program's by a relative error of at most 0.013.
The reference program's roundings to bfloat16 on the way count: a program that leaves them out, or rounds other values in their place, can miss the bound.
Values may be sent and summed in bfloat16 or wider, within the bound.
A program may use at most 128 MiB of HBM per device.

```python
import math
import jax
import jax.numpy as jnp
import numpy as np
from jax import lax

D = 1024
H = 16
HD = 64
FF = 4096
ROT = 16
M = 64
SPAN = 64
SEQS = 3
MB = 2
MB_TOK = 256
TOKENS = 4096
N_DP = 8


def shard_levels(rng, shape, shards, least, largest):
    def one(dim, blocks):
        heights = jax.random.uniform(jax.random.fold_in(jax.random.fold_in(rng, 6), dim), (blocks,), jnp.float32, least / len(shards), largest / len(shards))
        return jnp.repeat(jnp.exp(heights), shape[dim] // blocks).reshape((-1,) + (1,) * (len(shape) - dim - 1))

    factor_of = one(*shards[0])
    for cut in shards[1:]:
        factor_of = factor_of * one(*cut)
    return factor_of


def profile(amount, total, reach, lean):
    weights = [(1 << 20) // math.isqrt(rank ** lean) + 1 for rank in range(2, amount + 1)]
    surplus, given = total - reach - (amount - 1), [1] * (amount - 1)
    while surplus > 0:
        movable = [i for i in range(amount - 1) if given[i] < reach]
        whole, budget = sum([weights[i] for i in movable]), surplus
        for i in movable:
            addition = min(reach - given[i], max(1, budget * weights[i] // whole), surplus)
            given[i] = given[i] + addition
            surplus = surplus - addition
    return np.array([reach] + given)


def uneven_parts(stream_key, count, total, limit, lean):
    if count == 2:
        one = jax.random.randint(stream_key, (), max(1, total - limit), min(limit, total - 1) + 1)
        return jnp.stack([one, total - one])
    sizes = jnp.asarray(profile(count, total, limit, lean), jnp.int32)
    couples = (count - 1) // 2
    donor, taker = sizes[1:1 + 2 * couples:2], sizes[2:2 + 2 * couples:2]
    margin = jnp.minimum(donor - 1, limit - taker)
    moved = jax.random.randint(jax.random.fold_in(stream_key, 1), (couples,), 0, 1 << 20) % (margin + 1)
    sizes = sizes.at[1:1 + 2 * couples:2].set(donor - moved).at[2:2 + 2 * couples:2].set(taker + moved)
    return sizes[jax.random.permutation(jax.random.fold_in(stream_key, 2), count)]


def bell_draw(rng, shape, scale, most, shards=(), kind=jnp.bfloat16):
    gain = shard_levels(rng, shape, shards, -0.22, 0.18) if shards else 1.0
    result = jax.random.normal(rng, shape, jnp.float32) * scale * gain
    return jnp.minimum(jnp.maximum(result, -most), most).astype(kind)


def setup_inputs(seed: int = 0) -> dict:
    arg_keys = jax.random.split(jax.random.key(seed), 15)
    tokens = bell_draw(arg_keys[0], (TOKENS, D), 1.0, 6.0, ((0, 8), (1, 4)))
    doc_lengths = jax.vmap(lambda own: uneven_parts(own, SEQS, MB_TOK, MB_TOK // 2, 2))(jax.random.split(arg_keys[1], (N_DP * MB))).reshape((N_DP * MB, SEQS)).astype(jnp.int32)
    norm_gain = jnp.clip(1.0 + 0.1 * jax.random.normal(arg_keys[2], (D,), jnp.float32), 0.5, 1.5).astype(jnp.bfloat16)
    norm_shift = bell_draw(arg_keys[3], (D,), 0.2, 1.25, ((0, 4),))
    qkv_weight = bell_draw(arg_keys[4], (D, 3, D), D ** -0.5, 0.1875, ((0, 8), (2, 4)))
    qkv_bias = bell_draw(arg_keys[5], (3, D), 0.3, 1.75, ((1, 4),))
    omega = bell_draw(arg_keys[6], (HD, M), 1.0, 4.0, (), jnp.float32)
    qmc_weights = jnp.clip(jnp.exp(jax.random.uniform(arg_keys[7], (M,), jnp.float32, math.log(0.5), math.log(2.0))), 0.5, 2.0)
    out_weight = bell_draw(arg_keys[8], (D, D), 16 ** -0.5, 1.5, ((0, 4), (1, 8)))
    out_bias = bell_draw(arg_keys[9], (D,), 0.3, 1.75, ((0, 4),))
    up_weight = bell_draw(arg_keys[10], (D, FF), D ** -0.5, 0.1875, ((0, 8), (1, 4)))
    up_bias = bell_draw(arg_keys[11], (FF,), 0.3, 1.75, ((0, 4),))
    down_weight = bell_draw(arg_keys[12], (FF, D), FF ** -0.5, 0.09375, ((0, 4), (1, 8)))
    out_grad = bell_draw(arg_keys[13], (TOKENS, D), 1.0, 6.0, ((0, 8), (1, 4)))
    return dict(tokens=tokens, doc_lengths=doc_lengths, norm_gain=norm_gain, norm_shift=norm_shift, qkv_weight=qkv_weight, qkv_bias=qkv_bias, omega=omega, qmc_weights=qmc_weights, out_weight=out_weight, out_bias=out_bias, up_weight=up_weight, up_bias=up_bias, down_weight=down_weight, out_grad=out_grad)


epsilon = 1e-05
highest = lax.Precision.HIGHEST

@jax.custom_vjp
def low(v):
    return lax.optimization_barrier(v.astype(jnp.bfloat16)).astype(jnp.float32)

@jax.custom_vjp
def low_back(v):
    return v

def low_keep(v):
    return (low(v), None)

def low_pass(kept, grad):
    return (grad,)

def back_keep(v):
    return (v, None)

def back_low(kept, grad):
    return (low(grad),)
low.defvjp(low_keep, low_pass)
low_back.defvjp(back_keep, back_low)

def row_layout(lengths, row_count):
    seq_ends = jnp.cumsum(lengths).astype(jnp.int32)
    starts = (seq_ends - lengths).astype(jnp.int32)
    row_ids = jnp.arange(row_count, dtype=jnp.int32)
    segment = lax.optimization_barrier(jnp.sum((row_ids[:, None] >= seq_ends[None, :]).astype(jnp.int32), 1)).astype(jnp.int32)
    belongs = segment[:, None] == jnp.arange(lengths.shape[0], dtype=jnp.int32)[None, :]
    row_begin = lax.optimization_barrier(jnp.sum(jnp.where(belongs, starts[None, :], 0), 1)).astype(jnp.int32)
    return (segment, (row_ids - row_begin).astype(jnp.float32))

def rotate(vectors, positions):
    half_rot = ROT // 2
    inv_freq = jnp.exp(-jnp.arange(half_rot, dtype=jnp.float32) * (2.0 / ROT) * math.log(10000.0))
    angles = positions[:, None] * inv_freq[None, :]
    cosine = jnp.cos(angles)[:, None, :]
    sine = jnp.sin(angles)[:, None, :]
    lower_part = vectors[..., :half_rot]
    upper_part = vectors[..., half_rot:ROT]
    return jnp.concatenate([lower_part * cosine - upper_part * sine, upper_part * cosine + lower_part * sine, vectors[..., ROT:]], -1)

def dct_table():
    ramp_vals = jnp.arange(HD, dtype=jnp.float32)
    weights_row = jnp.where(ramp_vals == 0.0, jnp.sqrt(1.0 / HD), jnp.sqrt(2.0 / HD))
    return jnp.cos(math.pi * (2.0 * ramp_vals[None, :] + 1.0) * ramp_vals[:, None] / (2.0 * HD)) * weights_row[:, None]

def feature_map(vectors, positions, omega):
    turned = rotate(vectors, positions) * HD ** (-0.25)
    spectrum = jnp.einsum('rhn,kn->rhk', turned, dct_table(), precision=highest)
    scores = jnp.einsum('rhk,kj->rhj', spectrum, omega, precision=highest)
    return jnp.exp(scores - 0.5 * lax.optimization_barrier(jnp.sum(turned * turned, -1, keepdims=True)))

def attend(query_feat, key_feat, extended, segment):
    nblocks = MB_TOK // SPAN
    head_count = query_feat.shape[1]
    blocks = segment.reshape(nblocks, SPAN)
    head_seg = blocks[:, 0]
    following = jnp.concatenate([head_seg[1:], jnp.full((1,), -1, jnp.int32)])
    offsets_in = jnp.arange(SPAN, dtype=jnp.int32)
    causal = offsets_in[:, None] >= offsets_in[None, :]

    def one_block(state_run, pieces):
        block_q, block_k, block_v, block_seg, first_seg, next_seg = pieces
        block_mask = (causal & (block_seg[:, None] == block_seg[None, :])).astype(jnp.float32)
        scores = jnp.einsum('thj,shj->hts', block_q, block_k, precision=highest) * block_mask[None]
        inside = jnp.einsum('hts,she->the', scores, block_v, precision=highest)
        row_gate = (block_seg == first_seg).astype(jnp.float32)
        outside = jnp.einsum('thj,hje->the', block_q * row_gate[:, None, None], state_run, precision=highest)
        chosen = (block_seg == next_seg).astype(jnp.float32)
        carry_keep = (first_seg == next_seg).astype(jnp.float32)
        state_run = carry_keep * state_run + jnp.einsum('shj,she->hje', block_k * chosen[:, None, None], block_v, precision=highest)
        return (state_run, inside + outside)
    initial = jnp.zeros((head_count, query_feat.shape[2], extended.shape[2]), jnp.float32)
    pieces = (query_feat.reshape(nblocks, SPAN, head_count, -1), key_feat.reshape(nblocks, SPAN, head_count, -1), extended.reshape(nblocks, SPAN, head_count, -1), blocks, head_seg, following)
    _, results = lax.scan(jax.checkpoint(one_block), initial, pieces)
    return results.reshape(MB_TOK, head_count, -1)

def layer_rows(inputs, lengths, gain_vec, shift_vec, wqkv, bqkv, omega, qmc, wout, bout, wup, bup, wdown):
    row_count = inputs.shape[0]
    center = lax.optimization_barrier(jnp.mean(inputs, -1, keepdims=True))
    spread = lax.optimization_barrier(jnp.mean(inputs * inputs, -1, keepdims=True)) - center * center
    standard = (inputs - center) * lax.rsqrt(spread + epsilon)
    normed = low(standard * gain_vec + shift_vec)
    projected = low(low_back(jnp.einsum('rd,dcf->rcf', normed, wqkv, precision=highest) + bqkv))
    heads_view = projected.reshape(row_count, 3, H, HD)
    segment, positions = row_layout(lengths, row_count)
    query_feat = low(qmc * feature_map(heads_view[:, 0], positions, omega))
    key_feat = low(feature_map(heads_view[:, 1], positions, omega))
    extended = jnp.concatenate([heads_view[:, 2], jnp.ones((row_count, H, 1), jnp.float32)], 2)
    mixed = attend(query_feat, key_feat, extended, segment)
    numerator = low_back(mixed[..., :HD])
    denominator = low_back(mixed[..., HD])
    attended = low((numerator / denominator[..., None]).reshape(row_count, D))
    pre_act = low_back(jnp.dot(normed, wup, precision=highest, preferred_element_type=jnp.float32) + bup)
    hidden = low(jax.nn.gelu(pre_act, approximate=False))
    branch = jnp.dot(attended, wout, precision=highest, preferred_element_type=jnp.float32)
    branch = branch + jnp.dot(hidden, wdown, precision=highest, preferred_element_type=jnp.float32)
    return inputs + branch + bout

def reference(tokens, doc_lengths, norm_gain, norm_shift, qkv_weight, qkv_bias, omega, qmc_weights, out_weight, out_bias, up_weight, up_bias, down_weight, out_grad):
    stacked = tokens.astype(jnp.float32).reshape(N_DP * MB, MB_TOK, D)
    omega_f = omega.astype(jnp.float32)
    qmc_f = qmc_weights.astype(jnp.float32)

    def forward(inputs, gain_vec, shift_vec, wqkv, bqkv, wout, bout, wup, bup, wdown):

        def per_micro(pair):
            return layer_rows(pair[0], pair[1], gain_vec, shift_vec, wqkv, bqkv, omega_f, qmc_f, wout, bout, wup, bup, wdown)
        return lax.map(jax.checkpoint(per_micro), (inputs, doc_lengths))
    primals = (stacked, norm_gain.astype(jnp.float32), norm_shift.astype(jnp.float32), qkv_weight.astype(jnp.float32), qkv_bias.astype(jnp.float32), out_weight.astype(jnp.float32), out_bias.astype(jnp.float32), up_weight.astype(jnp.float32), up_bias.astype(jnp.float32), down_weight.astype(jnp.float32))
    results, pullback = jax.vjp(forward, *primals)
    grads = pullback(out_grad.astype(jnp.float32).reshape(N_DP * MB, MB_TOK, D))
    return (results.reshape(TOKENS, D).astype(jnp.bfloat16), grads[0].reshape(TOKENS, D).astype(jnp.bfloat16), grads[1], grads[2], grads[3], grads[4], grads[5], grads[6], grads[7], grads[8], grads[9])
```

```python
import functools
import math

import jax
import jax.numpy as jnp
import ml_dtypes
import numpy as np
from jax import lax
from jax.experimental import pallas as pl
from jax.experimental.pallas import tpu as pltpu
from jax.sharding import PartitionSpec as P

D = 1024
HD = 64
ROT = 16
M = 64
SPAN = 64
MB = 2
SEQS = 3


epsilon = 1e-05
highest = lax.Precision.HIGHEST


def row_layout(lengths, row_count):
    seq_ends = jnp.cumsum(lengths)
    starts = seq_ends - lengths
    row_ids = jnp.arange(row_count, dtype=jnp.int32)
    segment = jnp.sum((row_ids[:, None] >= seq_ends[None, :]).astype(jnp.int32), 1)
    belongs = segment[:, None] == jnp.arange(lengths.shape[0], dtype=jnp.int32)[None, :]
    row_begin = jnp.sum(jnp.where(belongs, starts[None, :], 0), 1)
    return (segment, (row_ids - row_begin).astype(jnp.float32))


def rotate(vectors, positions):
    half_rot = ROT // 2
    inv_freq = jnp.exp(-jnp.arange(half_rot, dtype=jnp.float32) * (2.0 / ROT) * math.log(10000.0))
    angles = positions[:, None] * inv_freq[None, :]
    cosine = jnp.cos(angles)[:, None, :]
    sine = jnp.sin(angles)[:, None, :]
    lower_part = vectors[..., :half_rot]
    upper_part = vectors[..., half_rot:ROT]
    return jnp.concatenate(
        [
            lower_part * cosine - upper_part * sine,
            upper_part * cosine + lower_part * sine,
            vectors[..., ROT:],
        ],
        -1,
    )


def dct_table():
    ramp_vals = jnp.arange(HD, dtype=jnp.float32)
    weights_row = jnp.where(ramp_vals == 0.0, jnp.sqrt(1.0 / HD), jnp.sqrt(2.0 / HD))
    return (
        jnp.cos(math.pi * (2.0 * ramp_vals[None, :] + 1.0) * ramp_vals[:, None] / (2.0 * HD))
        * weights_row[:, None]
    )


def feature_map(vectors, positions, omega):
    turned = rotate(vectors, positions) * HD ** (-0.25)
    spectrum = jnp.einsum("rhn,kn->rhk", turned, dct_table(), precision=highest)
    scores = jnp.einsum("rhk,kj->rhj", spectrum, omega, precision=highest)
    return jnp.exp(scores - 0.5 * jnp.sum(turned * turned, -1, keepdims=True))


def both_maps(queries, keys_raw, positions, omega_used, weights_used):
    return (
        weights_used * feature_map(queries, positions, omega_used),
        feature_map(keys_raw, positions, omega_used),
    )


def gelu_exact(pre_act):
    return jax.nn.gelu(pre_act, approximate=False)


def block_masks(segment):
    nblocks = segment.shape[0] // SPAN
    blocks = segment.reshape(nblocks, SPAN)
    head_seg = blocks[:, 0]
    following = jnp.concatenate([head_seg[1:], jnp.full((1,), -1, jnp.int32)])
    carry_keep = (head_seg == following).astype(jnp.float32)
    row_gate = (blocks == head_seg[:, None]).astype(jnp.float32)
    chosen = (blocks == following[:, None]).astype(jnp.float32)
    offsets_in = jnp.arange(SPAN, dtype=jnp.int32)
    causal = offsets_in[:, None] >= offsets_in[None, :]
    same_seq = blocks[:, :, None] == blocks[:, None, :]
    block_mask = (causal[None] & same_seq).astype(jnp.float32)
    return (carry_keep, row_gate, chosen, block_mask)


def carry_chain(carry_keep, increments):

    def combine(earlier, latter):
        return (earlier[0] * latter[0], latter[0] * earlier[1] + latter[1])

    factors = jnp.broadcast_to(carry_keep[:, None, None, None], increments.shape)
    return lax.associative_scan(combine, (factors, increments))[1]


def block_states(carry_keep, picked, block_v):
    increments = jnp.einsum("bshj,bshe->bhje", picked, block_v, precision=highest)
    totals = carry_chain(carry_keep, increments)
    return jnp.concatenate([jnp.zeros_like(totals[:1]), totals[:-1]], 0)


def attend(query_feat, key_feat, extended, masks):
    carry_keep, row_gate, chosen, block_mask = masks
    nblocks, span_len = row_gate.shape
    head_count = query_feat.shape[1]
    block_q = query_feat.reshape(nblocks, span_len, head_count, -1)
    block_k = key_feat.reshape(nblocks, span_len, head_count, -1)
    block_v = extended.reshape(nblocks, span_len, head_count, -1)
    scores = (
        jnp.einsum("bthj,bshj->bhts", block_q, block_k, precision=highest) * block_mask[:, None]
    )
    inside = jnp.einsum("bhts,bshe->bthe", scores, block_v, precision=highest)
    states = block_states(carry_keep, block_k * chosen[:, :, None, None], block_v)
    outside = jnp.einsum(
        "bthj,bhje->bthe", block_q * row_gate[:, :, None, None], states, precision=highest
    )
    return (inside + outside).reshape(nblocks * span_len, head_count, -1)


def attend_back(query_feat, key_feat, extended, masks, upstream):
    carry_keep, row_gate, chosen, block_mask = masks
    nblocks, span_len = row_gate.shape
    head_count = query_feat.shape[1]
    block_q = query_feat.reshape(nblocks, span_len, head_count, -1)
    block_k = key_feat.reshape(nblocks, span_len, head_count, -1)
    block_v = extended.reshape(nblocks, span_len, head_count, -1)
    block_g = upstream.reshape(nblocks, span_len, head_count, -1)
    picked = block_k * chosen[:, :, None, None]
    gated = block_q * row_gate[:, :, None, None]
    scores = (
        jnp.einsum("bthj,bshj->bhts", block_q, block_k, precision=highest) * block_mask[:, None]
    )
    states = block_states(carry_keep, picked, block_v)
    score_grad = (
        jnp.einsum("bthe,bshe->bhts", block_g, block_v, precision=highest) * block_mask[:, None]
    )
    query_grad = jnp.einsum("bhts,bshj->bthj", score_grad, block_k, precision=highest)
    query_grad = query_grad + row_gate[:, :, None, None] * jnp.einsum(
        "bthe,bhje->bthj", block_g, states, precision=highest
    )
    key_grad = jnp.einsum("bhts,bthj->bshj", score_grad, block_q, precision=highest)
    value_grad = jnp.einsum("bhts,bthe->bshe", scores, block_g, precision=highest)
    state_grad = jnp.einsum("bthj,bthe->bhje", gated, block_g, precision=highest)
    later_total = jnp.flip(carry_chain(jnp.flip(carry_keep, 0), jnp.flip(state_grad, 0)), 0)
    incr_grad = jnp.concatenate([later_total[1:], jnp.zeros_like(later_total[:1])], 0)
    key_grad = key_grad + chosen[:, :, None, None] * jnp.einsum(
        "bhje,bshe->bshj", incr_grad, block_v, precision=highest
    )
    value_grad = value_grad + jnp.einsum("bshj,bhje->bshe", picked, incr_grad, precision=highest)
    row_total = nblocks * span_len
    return (
        query_grad.reshape(row_total, head_count, -1),
        key_grad.reshape(row_total, head_count, -1),
        value_grad.reshape(row_total, head_count, -1),
    )


def on_device(
    tokens,
    doc_lengths,
    norm_gain,
    norm_shift,
    qkv_weight,
    qkv_bias,
    omega,
    qmc_weights,
    out_weight,
    out_bias,
    up_weight,
    up_bias,
    down_weight,
    out_grad,
):
    feat_parts = lax.axis_size("feat")
    feat_index = lax.axis_index("feat")
    qkv_full, up_full, out_rows, down_rows = (
        lax.all_gather(qkv_weight, "dp", axis=0, tiled=True),
        lax.all_gather(up_weight, "dp", axis=0, tiled=True),
        lax.all_gather(out_weight, "dp", axis=1, tiled=True),
        lax.all_gather(down_weight, "dp", axis=1, tiled=True),
    )
    gain_vec = norm_gain.astype(jnp.float32)
    shift_vec = norm_shift.astype(jnp.float32)
    inputs = tokens.astype(jnp.float32)
    row_sums = lax.psum((jnp.sum(inputs, 1), jnp.sum(inputs * inputs, 1)), "feat")
    center = row_sums[0] / D
    spread = row_sums[1] / D - center * center
    inv_root = lax.rsqrt(spread + epsilon)
    standard = (inputs - center[:, None]) * inv_root[:, None]
    normed_all = lax.all_gather(
        (standard * gain_vec + shift_vec).astype(jnp.bfloat16), "feat", axis=1, tiled=True
    )
    local_width = tokens.shape[1]
    local_heads = local_width // HD
    feat_count = M // feat_parts
    omega_used = lax.dynamic_slice_in_dim(omega, feat_index * feat_count, feat_count, 1)
    weights_used = lax.dynamic_slice_in_dim(qmc_weights, feat_index * feat_count, feat_count, 0)
    row_count = tokens.shape[0] // MB
    qkv_bias_f = qkv_bias.astype(jnp.float32)
    up_bias_f = up_bias.astype(jnp.float32)
    out_bias_f = out_bias.astype(jnp.float32)
    block_outs = []
    saved_state = []
    for micro_idx in range(MB):
        offset = micro_idx * row_count
        normed_rows = normed_all[offset : offset + row_count]
        segment, positions = row_layout(doc_lengths[micro_idx], row_count)
        masks = block_masks(segment)
        projected = (
            jnp.einsum("rd,dcf->rcf", normed_rows, qkv_full, preferred_element_type=jnp.float32)
            + qkv_bias_f
        ).astype(jnp.bfloat16)
        pre_act = jnp.dot(normed_rows, up_full, preferred_element_type=jnp.float32) + up_bias_f
        hidden = gelu_exact(pre_act).astype(jnp.bfloat16)
        projected_used = lax.all_gather(projected, "feat", axis=2, tiled=True)
        heads_used = projected_used.shape[2] // HD
        heads_view = projected_used.astype(jnp.float32).reshape(row_count, 3, heads_used, HD)
        queries = heads_view[:, 0]
        keys_raw = heads_view[:, 1]
        query_map, key_map = both_maps(queries, keys_raw, positions, omega_used, weights_used)
        query_feat = query_map.astype(jnp.bfloat16).astype(jnp.float32)
        key_feat = key_map.astype(jnp.bfloat16).astype(jnp.float32)
        extended = jnp.concatenate(
            [heads_view[:, 2], jnp.ones((row_count, heads_used, 1), jnp.float32)], 2
        )
        mixed = attend(query_feat, key_feat, extended, masks)
        numerator = mixed[..., :HD]
        denominator = mixed[..., HD]
        numerator, denominator = (
            lax.psum_scatter(numerator, "feat", scatter_dimension=1, tiled=True),
            lax.psum_scatter(denominator, "feat", scatter_dimension=1, tiled=True),
        )
        attended = (
            (numerator / denominator[..., None])
            .reshape(row_count, local_width)
            .astype(jnp.bfloat16)
        )
        branch = jnp.dot(attended, out_rows, preferred_element_type=jnp.float32)
        branch = branch + jnp.dot(hidden, down_rows, preferred_element_type=jnp.float32)
        summed = lax.psum_scatter(
            branch.astype(jnp.bfloat16), "feat", scatter_dimension=1, tiled=True
        ).astype(jnp.float32)
        block_outs.append(
            (inputs[offset : offset + row_count] + summed + out_bias_f).astype(jnp.bfloat16)
        )
        saved_state.append(
            (
                normed_rows,
                positions,
                masks,
                pre_act,
                hidden,
                queries,
                keys_raw,
                extended,
                query_feat,
                key_feat,
                numerator,
                denominator,
                attended,
            )
        )
    qkv_acc = jnp.zeros(qkv_full.shape, jnp.float32)
    up_acc = jnp.zeros(up_full.shape, jnp.float32)
    outw_acc = jnp.zeros(out_rows.shape, jnp.float32)
    down_acc = jnp.zeros(down_rows.shape, jnp.float32)
    qkv_bias_acc = jnp.zeros((3, local_width), jnp.float32)
    up_bias_acc = jnp.zeros((up_full.shape[1],), jnp.float32)
    normed_grads = []
    for micro_idx in range(MB):
        offset = micro_idx * row_count
        (
            normed_rows,
            positions,
            masks,
            pre_act,
            hidden,
            queries,
            keys_raw,
            extended,
            query_feat,
            key_feat,
            numerator,
            denominator,
            attended,
        ) = saved_state[micro_idx]
        cotangent = lax.all_gather(
            out_grad[offset : offset + row_count], "feat", axis=1, tiled=True
        )
        outw_acc = outw_acc + jnp.einsum(
            "rk,rd->kd", attended, cotangent, preferred_element_type=jnp.float32
        )
        down_acc = down_acc + jnp.einsum(
            "rk,rd->kd", hidden, cotangent, preferred_element_type=jnp.float32
        )
        att_grad = jnp.einsum("rd,kd->rk", cotangent, out_rows, preferred_element_type=jnp.float32)
        hidden_grad = jnp.einsum(
            "rd,kd->rk", cotangent, down_rows, preferred_element_type=jnp.float32
        )
        _, gelu_pull = jax.vjp(gelu_exact, pre_act)
        pre_grad = gelu_pull(hidden_grad)[0].astype(jnp.bfloat16)
        up_acc = up_acc + jnp.einsum(
            "rd,rk->dk", normed_rows, pre_grad, preferred_element_type=jnp.float32
        )
        up_bias_acc = up_bias_acc + jnp.sum(pre_grad.astype(jnp.float32), 0)
        att_grad = att_grad.reshape(row_count, local_heads, HD)
        numer_grad = (att_grad / denominator[..., None]).astype(jnp.bfloat16)
        denom_grad = (-jnp.sum(att_grad * numerator, 2) / (denominator * denominator)).astype(
            jnp.bfloat16
        )
        numer_grad, denom_grad = (
            lax.all_gather(numer_grad, "feat", axis=1, tiled=True),
            lax.all_gather(denom_grad, "feat", axis=1, tiled=True),
        )
        upstream = jnp.concatenate(
            [numer_grad.astype(jnp.float32), denom_grad.astype(jnp.float32)[..., None]], 2
        )
        query_feat_grad, key_feat_grad, extended_grad = attend_back(
            query_feat, key_feat, extended, masks, upstream
        )

        def map_local(query_in, key_in):
            return both_maps(query_in, key_in, positions, omega_used, weights_used)

        _, map_pull = jax.vjp(map_local, queries, keys_raw)
        query_grad, key_grad = map_pull((query_feat_grad, key_feat_grad))
        proj_rows = jnp.stack([query_grad, key_grad, extended_grad[..., :HD]], 1).reshape(
            row_count, 3, -1
        )
        proj_rows = lax.psum_scatter(proj_rows, "feat", scatter_dimension=2, tiled=True)
        proj_grad = proj_rows.astype(jnp.bfloat16)
        qkv_acc = qkv_acc + jnp.einsum(
            "rd,rcf->dcf", normed_rows, proj_grad, preferred_element_type=jnp.float32
        )
        qkv_bias_acc = qkv_bias_acc + jnp.sum(proj_grad.astype(jnp.float32), 0)
        normed_part = jnp.einsum(
            "rcf,dcf->rd", proj_grad, qkv_full, preferred_element_type=jnp.float32
        )
        normed_part = normed_part + jnp.einsum(
            "rk,dk->rd", pre_grad, up_full, preferred_element_type=jnp.float32
        )
        normed_grads.append(
            lax.psum_scatter(
                normed_part.astype(jnp.bfloat16), "feat", scatter_dimension=1, tiled=True
            ).astype(jnp.float32)
        )
    normed_grad = jnp.concatenate(normed_grads, 0)
    scaled = normed_grad * gain_vec
    grad_sums = lax.psum((jnp.sum(scaled, 1), jnp.sum(scaled * standard, 1)), "feat")
    out_grad_f = out_grad.astype(jnp.float32)
    input_grad = out_grad_f + inv_root[:, None] * (
        scaled - grad_sums[0][:, None] / D - standard * grad_sums[1][:, None] / D
    )
    gain_part = jnp.sum(normed_grad * standard, 0)
    shift_part = jnp.sum(normed_grad, 0)
    out_bias_part = jnp.sum(out_grad_f, 0)
    qkv_grad, up_grad, outw_grad, down_grad = (
        lax.psum_scatter(
            qkv_acc.astype(jnp.bfloat16), "dp", scatter_dimension=0, tiled=True
        ).astype(jnp.float32),
        lax.psum_scatter(up_acc.astype(jnp.bfloat16), "dp", scatter_dimension=0, tiled=True).astype(
            jnp.float32
        ),
        lax.psum_scatter(
            outw_acc.astype(jnp.bfloat16), "dp", scatter_dimension=1, tiled=True
        ).astype(jnp.float32),
        lax.psum_scatter(
            down_acc.astype(jnp.bfloat16), "dp", scatter_dimension=1, tiled=True
        ).astype(jnp.float32),
    )
    gain_grad, shift_grad, qkv_bias_grad, out_bias_grad, up_bias_grad = lax.psum(
        (gain_part, shift_part, qkv_bias_acc, out_bias_part, up_bias_acc), "dp"
    )
    return (
        jnp.concatenate(block_outs, 0),
        input_grad.astype(jnp.bfloat16),
        gain_grad,
        shift_grad,
        qkv_grad,
        qkv_bias_grad,
        outw_grad,
        out_bias_grad,
        up_grad,
        up_bias_grad,
        down_grad,
    )


MESH = pl.DeviceIdType.MESH
f32, bf16 = jnp.float32, jnp.bfloat16
NT = ((1,), (1,))
TN = ((0,), (0,))
EXTRA = 16


def dot(a, b, dims=((1,), (0,)), precision=None):
    return lax.dot_general(
        a, b, (dims, ((), ())), precision=precision, preferred_element_type=f32
    )


def rotary_table(longest):
    half_rot = ROT // 2
    inv_freq = np.exp(
        -np.arange(half_rot, dtype=np.float32)
        * np.float32(2.0 / ROT)
        * np.float32(math.log(10000.0))
    ).astype(np.float32)
    angles = np.arange(longest, dtype=np.float32)[:, None] * inv_freq[None, :]
    cosine = np.ones((longest, HD), np.float32)
    sine = np.zeros((longest, HD), np.float32)
    for part in range(2):
        cosine[:, part * half_rot : (part + 1) * half_rot] = np.cos(angles)
        sine[:, part * half_rot : (part + 1) * half_rot] = np.sin(angles)
    rest = np.concatenate([cosine, cosine, sine, sine], 1).astype(np.float32)
    terms = []
    for _ in range(3):
        term = rest.astype(ml_dtypes.bfloat16)
        terms.append(term)
        rest = rest - term.astype(np.float32)
    return np.concatenate(terms, 0)


def rotary_swap():
    half_rot = ROT // 2
    one = np.zeros((HD, HD), np.float32)
    for i in range(half_rot):
        one[i + half_rot, i] = -1.0
        one[i, i + half_rot] = 1.0
    return np.kron(np.eye(4, dtype=np.float32), one).astype(ml_dtypes.bfloat16)


def dct_rows():
    ramp = np.arange(HD, dtype=np.float32)
    scale = np.where(ramp == 0.0, np.sqrt(1.0 / HD), np.sqrt(2.0 / HD))
    table = np.cos(math.pi * (2.0 * ramp[None, :] + 1.0) * ramp[:, None] / (2.0 * HD)) * scale[:, None]
    return np.tile(table.T, (4, 1)).astype(np.float32)


class Sizes:
    def __init__(self, rows, width, hidden, dp_count, feat_count):
        self.rows = rows
        self.width = width
        self.model = width * feat_count
        self.span = rows // MB
        self.total = 2 * rows
        self.micro = 2 * MB
        self.half = width // 2
        self.hidden = hidden // 2
        self.block = self.model // dp_count
        self.planes = dp_count // 2


def scratch_list(s):
    pl_, bl, hf, hd, tt, md = s.planes, s.block, s.half, s.hidden, s.total, s.model
    grads = {
        "qkv": (3, bl, hf),
        "out": (hf, bl),
        "up": (bl, hd),
        "down": (hd, bl),
    }
    shapes = dict(
        XG=((2, s.rows + EXTRA, md), bf16),
        G=((tt, md), bf16),
        WQ=((3, md, hf), bf16),
        WU=((md, hd), bf16),
        WO=((hf, md), bf16),
        WD=((hd, md), bf16),
        NB=((tt, md), bf16),
        MU=((tt, 1), f32),
        IV=((tt, 1), f32),
        A2=((2 * s.width // 2, s.width), f32),
        WB=((tt, 2 * hf), bf16),
        VB=((tt, hf), bf16),
        PHF=((tt, 2 * hf), f32),
        PHB=((tt, 2 * hf), bf16),
        ROTV=((tt, 2 * hf), f32),
        CSB=((tt, 2 * hf), f32),
        SB=((s.micro, 2, s.span, s.span), bf16),
        ND=((tt, 2 * hf), f32),
        AT=((tt, hf), bf16),
        PG=((tt, 3 * hf), bf16),
        HB=((tt, hd), bf16),
        GP=((tt, hd), f32),
        PRE=((tt, hd), bf16),
        QBG=((1, 3 * hf), f32),
        UBG=((1, hd), f32),
        NGF=((s.rows, s.width), f32),
        ST=((16, s.rows), f32),
        STR=((3, 16, s.rows), f32),
        SV=((24, 128), f32),
        SVR=((7, 24, 128), f32),
    )
    for name, shape in grads.items():
        shapes["SX" + name] = ((pl_,) + shape, bf16)
        shapes["RX" + name] = ((pl_,) + shape, bf16)
        shapes["KX" + name] = ((pl_,) + shape, f32)
        shapes["ZS" + name] = ((3,) + shape, bf16)
        shapes["ZR" + name] = ((3,) + shape, bf16)
    for name in ("blk", "nrm"):
        shapes["CS" + name] = ((tt, 2 * s.width), bf16)
        shapes["CR" + name] = ((tt, 2 * s.width), bf16)
        shapes["KC" + name] = ((tt, 2 * s.width), f32)
        shapes["KY" + name] = ((tt, s.width), f32)
        shapes["YS" + name] = ((tt, s.width), bf16)
        shapes["YR" + name] = ((tt, s.width), bf16)
        shapes["AS" + name] = ((s.rows, s.width), bf16)
        shapes["AR" + name] = ((s.rows, s.width), bf16)
    return shapes


N_LOCAL = 7
N_REMOTE = 120


def fused_kernel(s, names, *refs):
    (tok, grd, ext, wq_in, wu_in, wo_in, wd_in, small, tab, swap, ones16, dct, rep, omega) = refs[:14]
    o_blk, o_inp, o_qkv, o_up, o_out, o_down, o_small = refs[14:21]
    m_ = dict(zip(names, refs[21:]))
    lsem, ssem, rsem = m_["lsem"], m_["ssem"], m_["rsem"]
    XG, G, WQ, WU, WO, WD = (m_[k] for k in ("XG", "G", "WQ", "WU", "WO", "WD"))
    NB, MU, IV = m_["NB"], m_["MU"], m_["IV"]

    dp = lax.axis_index("dp")
    ft = lax.axis_index("feat")
    z, x = dp // 2, dp % 2
    zl = z % 2
    y, c = ft // 2, ft % 2
    zd = (z, z + 1 - 2 * zl, z + 2 - 4 * (z // 2), 3 - z)
    zd = (z, z + 1 - 2 * zl, (z + 2) % 4, z + 1 - 2 * zl + 2 - 4 * (z // 2))
    hl = (zl, 1 - zl, zl, 1 - zl)
    counter = [0]

    def new(n=1):
        counter[0] += n
        return counter[0] - n

    def device(d=0, fx=False, fy=False, fc=False):
        return {
            "dp": zd[d] * 2 + (1 - x if fx else x),
            "feat": (1 - y if fy else y) * 2 + (1 - c if fc else c),
        }

    def send(src, dst, sem, where):
        copy = pltpu.make_async_remote_copy(
            src_ref=src,
            dst_ref=dst,
            send_sem=ssem.at[sem],
            recv_sem=rsem.at[sem],
            device_id=where,
            device_id_type=MESH,
        )
        return copy

    sent = []

    def go(src, dst, sem, where):
        copy = send(src, dst, sem, where)
        copy.start()
        sent.append(copy)

    def arrived(ref, sem, where):
        send(ref, ref, sem, where).wait_recv()

    mo = pl.multiple_of

    def lanes(index, size):
        return pl.ds(mo(index * size, size), size)

    def tok_at(b, f):
        return XG.at[b, :, lanes(f, s.width)]

    def grd_at(b, f):
        return G.at[lanes(b, s.rows), lanes(f, s.width)]

    def own_half(w, h):
        if w == "qkv":
            return wq_in.at[:, :, lanes(h, s.half)]
        if w == "up":
            return wu_in.at[:, lanes(h, s.hidden)]
        if w == "out":
            return wo_in.at[lanes(h, s.half), :]
        return wd_in.at[lanes(h, s.hidden), :]

    def weight_at(w, block):
        if w == "qkv":
            return WQ.at[:, lanes(block, s.block), :]
        if w == "up":
            return WU.at[lanes(block, s.block), :]
        if w == "out":
            return WO.at[:, lanes(block, s.block)]
        return WD.at[:, lanes(block, s.block)]

    ws = ("qkv", "out", "up", "down")

    local = [
        pltpu.make_async_copy(tok, XG.at[zl, pl.ds(0, s.rows), lanes(ft, s.width)], lsem.at[0]),
        pltpu.make_async_copy(ext, XG.at[zl, pl.ds(s.rows, EXTRA), lanes(ft, s.width)], lsem.at[1]),
        pltpu.make_async_copy(grd, grd_at(zl, ft), lsem.at[2]),
    ]
    for i, w in enumerate(ws):
        local.append(pltpu.make_async_copy(own_half(w, zl), weight_at(w, dp), lsem.at[3 + i]))
    for copy in local:
        copy.start()

    barrier = pltpu.get_barrier_semaphore()
    partners = [device(d) for d in (1, 2, 3)] + [device(d, fx=True) for d in (0, 1, 2, 3)]
    partners += [device(fy=True), device(fc=True), device(fy=True, fc=True)]
    for where in partners:
        pl.semaphore_signal(barrier, inc=1, device_id=where, device_id_type=MESH)
    pl.semaphore_wait(barrier, len(partners))
    for copy in local:
        copy.wait()

    sem_act = {"tok": new(7), "grd": new(7)}

    def act_first(name, at):
        base = sem_act[name]
        go(at(zl, ft), at(zl, ft), base + 1, device(fy=True))
        go(at(zl, ft), at(zl, ft), base + 2, device(1))
        go(at(zl, ft), at(zl, ft), base + 0, device(fc=True))

    def act_forward(name, at):
        base = sem_act[name]
        fy = (1 - y) * 2 + c
        zb = 1 - zl
        arrived(at(zb, ft), base + 2, device(1))
        go(at(zb, ft), at(zb, ft), base + 3, device(fy=True))
        go(at(zb, ft), at(zb, ft), base + 4, device(fc=True))
        arrived(at(zl, fy), base + 1, device(fy=True))
        go(at(zl, fy), at(zl, fy), base + 5, device(fc=True))
        arrived(at(zb, fy), base + 3, device(fy=True))
        go(at(zb, fy), at(zb, fy), base + 6, device(fc=True))

    def act_rest(name, at):
        base = sem_act[name]
        fc = y * 2 + 1 - c
        fyc = (1 - y) * 2 + 1 - c
        for k, b, f in ((0, zl, fc), (4, 1 - zl, fc), (5, zl, fyc), (6, 1 - zl, fyc)):
            arrived(at(b, f), base + k, device(fc=True))

    sem_z = {w: new(3) for w in ws}
    sem_x = {w: new(4) for w in ws}

    def w_z(w):
        for d in (3, 2, 1):
            go(own_half(w, hl[d]), weight_at(w, dp), sem_z[w] + d - 1, device(d))

    def w_own(w):
        go(weight_at(w, dp), weight_at(w, dp), sem_x[w], device(fx=True))

    def w_forward(w, d):
        block = zd[d] * 2 + x
        arrived(weight_at(w, block), sem_z[w] + d - 1, device(d))
        go(weight_at(w, block), weight_at(w, block), sem_x[w] + d, device(fx=True))

    def w_rest(w):
        for d in range(4):
            arrived(weight_at(w, zd[d] * 2 + 1 - x), sem_x[w] + d, device(fx=True))

    sem_gx = {w: new(4) for w in ws}
    sem_gz = {w: new(3) for w in ws}

    def put_grad(w, zp, mine, theirs):
        m_["KX" + w][zp] = mine
        m_["SX" + w][zp] = theirs.astype(bf16)
        src, dst = m_["SX" + w].at[zp], m_["RX" + w].at[zp]
        send(src, dst, sem_gx[w] + zp, device(fx=True)).start()

    def grad_z(w):
        for d in (3, 2, 1, 0):
            zp = zd[d]
            arrived(m_["RX" + w].at[zp], sem_gx[w] + zp, device(fx=True))
            both = m_["KX" + w][zp] + m_["RX" + w][zp].astype(f32)
            if d == 0:
                m_["KX" + w][zp] = both
            else:
                m_["ZS" + w][d - 1] = both.astype(bf16)
                go(m_["ZS" + w].at[d - 1], m_["ZR" + w].at[d - 1], sem_gz[w] + d - 1, device(d))

    def grad_last(w):
        for d in (1, 2, 3):
            arrived(m_["ZR" + w].at[d - 1], sem_gz[w] + d - 1, device(d))
        got = m_["ZR" + w]
        same = m_["KX" + w][z] + got[1].astype(f32)
        other = got[0].astype(f32) + got[2].astype(f32)
        if w == "qkv":
            o_qkv[:, :, lanes(zl, s.half)] = same
            o_qkv[:, :, lanes(1 - zl, s.half)] = other
        elif w == "up":
            o_up[:, lanes(zl, s.hidden)] = same
            o_up[:, lanes(1 - zl, s.hidden)] = other
        elif w == "out":
            o_out[lanes(zl, s.half), :] = same
            o_out[lanes(1 - zl, s.half), :] = other
        else:
            o_down[lanes(zl, s.hidden), :] = same
            o_down[lanes(1 - zl, s.hidden), :] = other
        for zp in range(4):
            send(m_["SX" + w].at[zp], m_["RX" + w].at[zp], sem_gx[w] + zp, device(fx=True)).wait_send()

    def pick(flag, a, b):
        return jnp.where(flag == 0, a, b)

    def halves(value, axis):
        n = value.shape[axis] // 2
        lo, hi = lax.slice_in_dim(value, 0, n, axis=axis), lax.slice_in_dim(value, n, 2 * n, axis=axis)
        return pick(x, lo, hi), pick(x, hi, lo)

    sem_c = {k: new(4) for k in ("blk", "nrm")}
    sem_y = {k: new(4) for k in ("blk", "nrm")}
    sem_a = {k: new(2) for k in ("blk", "nrm")}

    def rows_of(i):
        block = (1 - zl) + (i // MB) * (2 * zl - 1)
        return pl.ds(mo(block * s.rows + (i % MB) * s.span, s.span), s.span)

    def act_put(name, i, value):
        r = rows_of(i)
        w_ = s.width
        v = [value[:, k * w_ : (k + 1) * w_] for k in range(4)]
        m_["KC" + name][r, 0:w_] = pick(c, v[0], v[1])
        m_["KC" + name][r, w_ : 2 * w_] = pick(c, v[2], v[3])
        m_["CS" + name][r, 0:w_] = pick(c, v[1], v[0]).astype(bf16)
        m_["CS" + name][r, w_ : 2 * w_] = pick(c, v[3], v[2]).astype(bf16)
        send(m_["CS" + name].at[r], m_["CR" + name].at[r], sem_c[name] + i, device(fc=True)).start()

    def act_y(name, i):
        r = rows_of(i)
        w_ = s.width
        arrived(m_["CR" + name].at[r], sem_c[name] + i, device(fc=True))
        both = m_["KC" + name][r, :] + m_["CR" + name][r, :].astype(f32)
        lo, hi = both[:, :w_], both[:, w_:]
        m_["KY" + name][r, :] = pick(y, lo, hi)
        m_["YS" + name][r, :] = pick(y, hi, lo).astype(bf16)
        send(m_["YS" + name].at[r], m_["YR" + name].at[r], sem_y[name] + i, device(fy=True)).start()

    def act_z(name, i):
        r = rows_of(i)
        q = pl.ds(i * s.span, s.span)
        arrived(m_["YR" + name].at[r], sem_y[name] + i, device(fy=True))
        both = m_["KY" + name][r, :] + m_["YR" + name][r, :].astype(f32)
        m_["AS" + name][q, :] = both.astype(bf16)
        go(m_["AS" + name].at[q], m_["AR" + name].at[q], sem_a[name] + i, device(1))

    def act_last(name, i):
        r = rows_of(MB + i)
        q = pl.ds(i * s.span, s.span)
        arrived(m_["YR" + name].at[r], sem_y[name] + MB + i, device(fy=True))
        arrived(m_["AR" + name].at[q], sem_a[name] + i, device(1))
        return (
            m_["KY" + name][r, :]
            + m_["YR" + name][r, :].astype(f32)
            + m_["AR" + name][q, :].astype(f32)
        )

    def act_sent(name):
        for i in range(4):
            r = rows_of(i)
            send(m_["CS" + name].at[r], m_["CR" + name].at[r], sem_c[name] + i, device(fc=True)).wait_send()
            send(m_["YS" + name].at[r], m_["YR" + name].at[r], sem_y[name] + i, device(fy=True)).wait_send()

    def loop(n, body):
        lax.fori_loop(0, n, lambda i, carry: (body(i), carry)[1], 0)

    def at_micro(m):
        return pl.ds(mo(m * s.span, s.span), s.span)

    def norm_phase():
        extra = XG[0, s.rows : s.rows + EXTRA, :].astype(f32)
        gain, shift = extra[0:1], extra[1:2]

        def body(m):
            xv = XG[m // MB, pl.ds(mo((m % MB) * s.span, s.span), s.span), :].astype(f32)
            mu = jnp.sum(xv, 1, keepdims=True) * (1.0 / s.model)
            var = jnp.sum(xv * xv, 1, keepdims=True) * (1.0 / s.model) - mu * mu
            inv = lax.rsqrt(var + epsilon)
            r = at_micro(m)
            MU[r, :] = mu
            IV[r, :] = inv
            NB[r, :] = ((xv - mu) * inv * gain + shift).astype(bf16)

        loop(s.micro, body)

    def masks(m):
        extra = XG[m // MB, s.rows : s.rows + EXTRA, 0 : s.span].astype(f32)
        row_id = lax.broadcasted_iota(jnp.int32, extra.shape, 0)
        first = 2 + SEQS * (m % MB)

        def length(k):
            return jnp.sum(jnp.where(row_id == first + k, extra, 0.0), 0, keepdims=True)

        end0 = length(0)
        end1 = end0 + length(1)
        t = lax.broadcasted_iota(jnp.int32, (s.span, s.span), 0).astype(f32)
        u = lax.broadcasted_iota(jnp.int32, (s.span, s.span), 1).astype(f32)
        start = jnp.where(t >= end1, end1, jnp.where(t >= end0, end0, 0.0))
        return jnp.logical_and(u <= t, u >= start), t, u, start

    def head_rows():
        lane = lax.broadcasted_iota(jnp.int32, (1, s.half), 1)
        return [jnp.where(lane // HD == h, 1.0, 0.0).astype(bf16) for h in range(2)], [
            jnp.where(lane == h * HD, 1.0, 0.0).astype(bf16) for h in range(2)
        ]

    HIGH = lax.Precision.HIGH
    HIGHEST = lax.Precision.HIGHEST
    hf = s.half

    def table_phase():
        wide = dot(dot(dct[...], omega[...], precision=HIGHEST), rep[...], precision=HIGHEST)
        m_["A2"][...] = wide * (ones16[...].astype(f32) * (16.0 * HD ** (-0.25)))

    def fwd_phase():
        def body(m):
            r = at_micro(m)
            wq = jnp.concatenate([WQ[0], WQ[1], WQ[2]], 1)
            bias = jnp.concatenate(
                [small[1:2, pl.ds(mo(k * s.width + zl * hf, hf), hf)] for k in range(3)], 1
            )
            p = (dot(NB[r, :], wq) + bias).astype(bf16)
            w, v = p[:, : 2 * hf], p[:, 2 * hf :]
            m_["VB"][r, :] = v
            mask, t, u, start = masks(m)
            pos = t[:, :hf] - start[:, :hf]
            hot = jnp.where(pos == u[:, :hf], 1.0, 0.0).astype(bf16)
            cs = dot(jnp.concatenate([hot, hot, hot], 1), tab[...])
            m_["CSB"][r, :] = cs
            cc = jnp.concatenate([cs[:, :hf], cs[:, :hf]], 1)
            ss = jnp.concatenate([cs[:, hf:], cs[:, hf:]], 1)
            wf = w.astype(f32)
            rot = wf * cc + dot(w, swap[...]) * ss
            m_["ROTV"][r, :] = rot
            score = dot(rot, m_["A2"][...], precision=HIGH)
            norm2 = dot(wf * wf, ones16[...].astype(f32), precision=HIGH)
            ph = jnp.exp(score - norm2) * small[2:3, 0 : 2 * hf]
            m_["PHF"][r, :] = ph
            pb = ph.astype(bf16)
            m_["PHB"][r, :] = pb
            hm, _ = head_rows()
            acc = jnp.zeros((s.span, 2 * hf), f32)
            for h in range(2):
                sc = dot(pb[:, :hf] * hm[h], pb[:, hf:], NT)
                sm = jnp.where(mask, sc, 0.0).astype(bf16)
                m_["SB"][m, h] = sm
                rhs = jnp.concatenate([v * hm[h], jnp.broadcast_to(hm[h], v.shape)], 1)
                acc = acc + dot(sm, rhs)
            m_["ND"][r, :] = acc
            m_["AT"][r, :] = (acc[:, :hf] / acc[:, hf:]).astype(bf16)

        loop(s.micro, body)

    def bwd_phase():
        m_["QBG"][...] = jnp.zeros_like(m_["QBG"])

        def body(m):
            r = at_micro(m)
            mask = masks(m)[0]
            hm, hot = head_rows()
            ag = dot(G[r, :], WO[...], NT)
            nd = m_["ND"][r, :]
            num, den = nd[:, :hf], nd[:, hf:]
            ng = (ag / den).astype(bf16)
            sums = dot(ag * num, ones16[0:hf, 0:hf].astype(f32), precision=HIGH) * 16.0
            dg = (-sums / (den * den)).astype(bf16)
            v = m_["VB"][r, :]
            pb = m_["PHB"][r, :]
            v1 = jnp.concatenate([v, jnp.ones(v.shape, bf16)], 1)
            dq = dk = dv = jnp.zeros((s.span, hf), f32)
            for h in range(2):
                e = dot(jnp.concatenate([ng * hm[h], dg * hot[h]], 1), v1, NT)
                em = jnp.where(mask, e, 0.0).astype(bf16)
                dq = dq + dot(em, pb[:, hf:] * hm[h])
                dk = dk + dot(em, pb[:, :hf] * hm[h], TN)
                dv = dv + dot(m_["SB"][m, h], ng * hm[h], TN)
            dph = jnp.concatenate([dq, dk], 1) * m_["PHF"][r, :]
            rot = m_["ROTV"][r, :]
            both = dot(dph, ones16[...].astype(f32), precision=HIGH) * 2.0
            drot = dot(dph, m_["A2"][...], NT, precision=HIGH) - rot * both
            cs = m_["CSB"][r, :]
            cc = jnp.concatenate([cs[:, :hf], cs[:, :hf]], 1)
            ss = jnp.concatenate([cs[:, hf:], cs[:, hf:]], 1)
            dw = drot * cc + dot(drot * ss, swap[...].astype(f32), NT, precision=HIGH)
            pg = jnp.concatenate([dw, dv], 1).astype(bf16)
            m_["PG"][r, :] = pg
            m_["QBG"][...] += jnp.sum(pg.astype(f32), 0, keepdims=True)

        loop(s.micro, body)

    def up_phase():
        bias = small[0:1, lanes(zl, s.hidden)]

        def body(m):
            r = at_micro(m)
            pre = dot(NB[r, :], WU[...]) + bias
            cdf = 0.5 * (1.0 + lax.erf(pre * math.sqrt(0.5)))
            m_["HB"][r, :] = (pre * cdf).astype(bf16)
            m_["GP"][r, :] = cdf + pre * jnp.exp(-0.5 * pre * pre) * (1.0 / math.sqrt(2.0 * math.pi))

        loop(s.micro, body)

    def pre_phase():
        m_["UBG"][...] = jnp.zeros_like(m_["UBG"])

        def body(m):
            r = at_micro(m)
            pre = (dot(G[r, :], WD[...], NT) * m_["GP"][r, :]).astype(bf16)
            m_["PRE"][r, :] = pre
            m_["UBG"][...] += jnp.sum(pre.astype(f32), 0, keepdims=True)

        loop(s.micro, body)

    def nrm_phase():
        def body(i):
            r = rows_of(i)
            wq = jnp.concatenate([WQ[0], WQ[1], WQ[2]], 1)
            act_put("nrm", i, dot(m_["PG"][r, :], wq, NT) + dot(m_["PRE"][r, :], WU[...], NT))

        loop(4, body)

    def blk_phase():
        def body(i):
            r = rows_of(i)
            act_put("blk", i, dot(m_["AT"][r, :], WO[...]) + dot(m_["HB"][r, :], WD[...]))

        loop(4, body)

    two = 2 * s.block

    def grad_phase(w):
        def body(zp):
            cols = lanes(zp, two)
            if w == "qkv":
                value = dot(NB[:, cols], m_["PG"][...], TN)
                mine, theirs = halves(value, 0)
                mine = jnp.stack([mine[:, k * hf : (k + 1) * hf] for k in range(3)], 0)
                theirs = jnp.stack([theirs[:, k * hf : (k + 1) * hf] for k in range(3)], 0)
            elif w == "up":
                mine, theirs = halves(dot(NB[:, cols], m_["PRE"][...], TN), 0)
            elif w == "out":
                mine, theirs = halves(dot(m_["AT"][...], G[:, cols], TN), 1)
            else:
                mine, theirs = halves(dot(m_["HB"][...], G[:, cols], TN), 1)
            put_grad(w, zp, mine, theirs)

        loop(s.planes, body)

    def out_rows(i):
        return pl.ds(i * s.span, s.span)

    def blk_last():
        for i in range(MB):
            own = XG[zl, i * s.span : (i + 1) * s.span, lanes(ft, s.width)].astype(f32)
            bias = small[1:2, 3 * s.width : 4 * s.width]
            o_blk[out_rows(i), :] = (own + act_last("blk", i) + bias).astype(bf16)

    sem_st = new(3)
    stat_where = [device(fc=True), device(fy=True), device(fy=True, fc=True)]

    def own_parts():
        extra = XG[0, s.rows : s.rows + EXTRA, lanes(ft, s.width)].astype(f32)
        r = lanes(zl, s.rows)
        own = XG[zl, 0 : s.rows, lanes(ft, s.width)].astype(f32)
        xhat = (own - MU[r, :]) * IV[r, :]
        return extra[0:1], xhat

    def nrm_last():
        for i in range(MB):
            m_["NGF"][out_rows(i), :] = act_last("nrm", i)
        gain, xhat = own_parts()
        ngrad = m_["NGF"][...]
        scaled = ngrad * gain
        ones = jnp.ones((8, s.width), f32)
        m_["ST"][0:8, :] = dot(ones, scaled, NT, precision=HIGHEST)
        m_["ST"][8:16, :] = dot(ones, scaled * xhat, NT, precision=HIGHEST)
        for k, where in enumerate(stat_where):
            go(m_["ST"], m_["STR"].at[k], sem_st + k, where)
        own_g = G[lanes(zl, s.rows), lanes(ft, s.width)].astype(f32)
        rows = [
            jnp.sum(ngrad * xhat, 0, keepdims=True),
            jnp.sum(ngrad, 0, keepdims=True),
            jnp.sum(own_g, 0, keepdims=True),
        ]
        sv = m_["SV"]
        sv[...] = jnp.zeros_like(sv)
        for k, row in enumerate(rows):
            for j in range(2):
                sv[2 * k + j : 2 * k + j + 1, :] = row[:, j * 128 : (j + 1) * 128]
        for k in range(3):
            sv[pl.ds(6 + 2 * k + zl, 1), :] = m_["QBG"][0:1, k * hf : (k + 1) * hf]
        for j in range(s.hidden // 128):
            sv[pl.ds(12 + zl * (s.hidden // 128) + j, 1), :] = m_["UBG"][0:1, j * 128 : (j + 1) * 128]

    sem_sv = new(7)
    sv_where = [device(d) for d in (1, 2, 3)] + [device(d, fx=True) for d in (0, 1, 2, 3)]

    def small_send():
        for k, where in enumerate(sv_where):
            go(m_["SV"], m_["SVR"].at[k], sem_sv + k, where)

    def small_last():
        total = m_["SV"][...]
        for k, where in enumerate(sv_where):
            arrived(m_["SVR"].at[k], sem_sv + k, where)
            total = total + m_["SVR"][k]
        o_small[...] = total

    def input_last():
        total = m_["ST"][...]
        for k, where in enumerate(stat_where):
            arrived(m_["STR"].at[k], sem_st + k, where)
            total = total + m_["STR"][k]
        spread = jnp.full((8, s.width), 1.0 / (8.0 * s.model), f32)
        mean1 = dot(total[0:8, :], spread, TN, precision=HIGHEST)
        mean2 = dot(total[8:16, :], spread, TN, precision=HIGHEST)
        gain, xhat = own_parts()
        own_g = G[lanes(zl, s.rows), lanes(ft, s.width)].astype(f32)
        scaled = m_["NGF"][...] * gain
        inv = IV[lanes(zl, s.rows), :]
        o_inp[...] = (own_g + inv * (scaled - mean1 - xhat * mean2)).astype(bf16)

    act_first("tok", tok_at)
    w_own("qkv")
    w_z("qkv")
    w_own("out")
    table_phase()
    act_forward("tok", tok_at)
    act_first("grd", grd_at)
    w_z("out")
    w_z("up")
    w_z("down")
    for d in (1, 2, 3):
        w_forward("qkv", d)
    w_own("up")
    w_own("down")
    act_rest("tok", tok_at)
    norm_phase()
    act_forward("grd", grd_at)
    for d in (1, 2, 3):
        w_forward("out", d)
    w_rest("qkv")
    fwd_phase()
    act_rest("grd", grd_at)
    for d in (1, 2, 3):
        w_forward("up", d)
    w_rest("out")
    bwd_phase()
    grad_phase("out")
    grad_phase("qkv")
    for d in (1, 2, 3):
        w_forward("down", d)
    w_rest("up")
    up_phase()
    grad_z("out")
    grad_z("qkv")
    w_rest("down")
    pre_phase()
    nrm_phase()
    blk_phase()
    for i in range(4):
        act_y("nrm", i)
    grad_phase("up")
    for i in range(4):
        act_y("blk", i)
    for i in range(2):
        act_z("nrm", i)
    grad_phase("down")
    for i in range(2):
        act_z("blk", i)
    grad_z("up")
    nrm_last()
    small_send()
    grad_z("down")
    blk_last()
    input_last()
    small_last()
    for w in ws:
        grad_last(w)
    for copy in sent:
        copy.wait_send()
    for name in ("blk", "nrm"):
        act_sent(name)
    assert counter[0] <= N_REMOTE


def on_device_fused(
    dp_count,
    feat_count,
    tokens,
    doc_lengths,
    norm_gain,
    norm_shift,
    qkv_weight,
    qkv_bias,
    omega,
    qmc_weights,
    out_weight,
    out_bias,
    up_weight,
    up_bias,
    down_weight,
    out_grad,
):
    rows, width = tokens.shape
    s = Sizes(rows, width, up_weight.shape[1], dp_count, feat_count)
    lens = jnp.broadcast_to(doc_lengths.reshape(-1, 1).astype(bf16), (doc_lengths.size, width))
    extra = jnp.concatenate(
        [
            norm_gain[None],
            norm_shift[None],
            lens,
            jnp.zeros((EXTRA - 2 - doc_lengths.size, width), bf16),
        ],
        0,
    )
    full = up_bias.shape[0]
    lane_gain = jnp.concatenate([qmc_weights, qmc_weights, jnp.ones((width // 2,), f32)])
    small = jnp.stack(
        [
            up_bias.astype(f32),
            jnp.concatenate([qkv_bias.reshape(-1), out_bias]).astype(f32),
            jnp.concatenate([lane_gain, jnp.zeros((full - lane_gain.shape[0],), f32)]),
        ],
        0,
    )
    ones16 = np.kron(np.eye(4), np.full((HD, HD), 1.0 / 16.0)).astype(ml_dtypes.bfloat16)
    rep = np.tile(np.eye(HD, dtype=np.float32), (1, 4))
    shapes = scratch_list(s)
    names = list(shapes) + ["lsem", "ssem", "rsem"]
    scratch = [pltpu.VMEM(shape, kind) for shape, kind in shapes.values()]
    scratch += [
        pltpu.SemaphoreType.DMA((N_LOCAL,)),
        pltpu.SemaphoreType.DMA((N_REMOTE,)),
        pltpu.SemaphoreType.DMA((N_REMOTE,)),
    ]
    raw = pl.BlockSpec(memory_space=pl.ANY)
    vm = pl.BlockSpec(memory_space=pltpu.VMEM)
    outs = pl.pallas_call(
        functools.partial(fused_kernel, s, names),
        out_shape=(
            jax.ShapeDtypeStruct((rows, width), bf16),
            jax.ShapeDtypeStruct((rows, width), bf16),
            jax.ShapeDtypeStruct((3, s.block, width), f32),
            jax.ShapeDtypeStruct(up_weight.shape, f32),
            jax.ShapeDtypeStruct(out_weight.shape, f32),
            jax.ShapeDtypeStruct(down_weight.shape, f32),
            jax.ShapeDtypeStruct((24, 128), f32),
        ),
        in_specs=[raw] * 7 + [vm] * 7,
        out_specs=[vm] * 7,
        scratch_shapes=scratch,
        compiler_params=pltpu.CompilerParams(
            collective_id=0, has_side_effects=True, vmem_limit_bytes=63 * 2**20
        ),
    )(
        tokens,
        out_grad,
        extra,
        jnp.transpose(qkv_weight, (1, 0, 2)),
        up_weight,
        out_weight,
        down_weight,
        small,
        jnp.asarray(rotary_table(rows // MB // 2)),
        jnp.asarray(rotary_swap()),
        jnp.asarray(ones16),
        jnp.asarray(dct_rows()),
        jnp.asarray(rep),
        omega,
    )
    o_blk, o_inp, o_qkv, o_up, o_out, o_down, o_small = outs
    flat = o_small.reshape(-1)
    return (
        o_blk,
        o_inp,
        flat[0:width],
        flat[width : 2 * width],
        jnp.transpose(o_qkv, (1, 0, 2)),
        flat[3 * width : 6 * width].reshape(3, width),
        o_out,
        flat[2 * width : 3 * width],
        o_up,
        flat[6 * width : 6 * width + full],
        o_down,
    )


def solution(mesh):
    in_specs = (
        P("dp", "feat"),
        P("dp", None),
        P("feat"),
        P("feat"),
        P("dp", None, "feat"),
        P(None, "feat"),
        P(),
        P(),
        P("feat", "dp"),
        P("feat"),
        P("dp", "feat"),
        P("feat"),
        P("feat", "dp"),
        P("dp", "feat"),
    )
    out_specs = (
        P("dp", "feat"),
        P("dp", "feat"),
        P("feat"),
        P("feat"),
        P("dp", None, "feat"),
        P(None, "feat"),
        P("feat", "dp"),
        P("feat"),
        P("dp", "feat"),
        P("feat"),
        P("feat", "dp"),
    )
    dp_count, feat_count = mesh.shape["dp"], mesh.shape["feat"]
    if (dp_count, feat_count) == (8, 4):
        per_device = functools.partial(on_device_fused, dp_count, feat_count)
    else:
        per_device = on_device
    return jax.shard_map(
        per_device, mesh=mesh, in_specs=in_specs, out_specs=out_specs, check_vma=False
    )
```

```python
import functools
import math

import jax
import jax.numpy as jnp
import ml_dtypes
import numpy as np
from jax import lax
from jax.experimental import pallas as pl
from jax.experimental.pallas import tpu as pltpu
from jax.sharding import PartitionSpec as P

D = 1024
HD = 64
ROT = 16
M = 64
SPAN = 64
MB = 2
SEQS = 3


FEAT = "feat"
DP = "dp"
QKV = "qkv"
OUT = "out"
UP = "up"
DOWN = "down"
TOK = "tok"
GRD = "grd"
NRM = "nrm"
BLK = "blk"


epsilon = 1e-05
highest = lax.Precision.HIGHEST


def row_layout(lengths, row_count):
    seq_ends = jnp.cumsum(lengths)
    starts = seq_ends - lengths
    row_ids = jnp.arange(row_count, dtype=jnp.int32)
    segment = jnp.sum((row_ids[:, None] >= seq_ends[None, :]).astype(jnp.int32), 1)
    belongs = segment[:, None] == jnp.arange(lengths.shape[0], dtype=jnp.int32)[None, :]
    row_begin = jnp.sum(jnp.where(belongs, starts[None, :], 0), 1)
    return (segment, (row_ids - row_begin).astype(jnp.float32))


def rotate(vectors, positions):
    half_rot = ROT // 2
    inv_freq = jnp.exp(-jnp.arange(half_rot, dtype=jnp.float32) * (2.0 / ROT) * math.log(10000.0))
    angles = positions[:, None] * inv_freq[None, :]
    cosine = jnp.cos(angles)[:, None, :]
    sine = jnp.sin(angles)[:, None, :]
    lower_part = vectors[..., :half_rot]
    upper_part = vectors[..., half_rot:ROT]
    return jnp.concatenate(
        [
            lower_part * cosine - upper_part * sine,
            upper_part * cosine + lower_part * sine,
            vectors[..., ROT:],
        ],
        -1,
    )


def dct_table():
    ramp_vals = jnp.arange(HD, dtype=jnp.float32)
    weights_row = jnp.where(ramp_vals == 0.0, jnp.sqrt(1.0 / HD), jnp.sqrt(2.0 / HD))
    return (
        jnp.cos(math.pi * (2.0 * ramp_vals[None, :] + 1.0) * ramp_vals[:, None] / (2.0 * HD))
        * weights_row[:, None]
    )


def feature_map(vectors, positions, omega):
    turned = rotate(vectors, positions) * HD ** (-0.25)
    spectrum = jnp.einsum("rhn,kn->rhk", turned, dct_table(), precision=highest)
    scores = jnp.einsum("rhk,kj->rhj", spectrum, omega, precision=highest)
    return jnp.exp(scores - 0.5 * jnp.sum(turned * turned, -1, keepdims=True))


def both_maps(queries, keys_raw, positions, omega_used, weights_used):
    return (
        weights_used * feature_map(queries, positions, omega_used),
        feature_map(keys_raw, positions, omega_used),
    )


def gelu_exact(pre_act):
    return jax.nn.gelu(pre_act, approximate=False)


def block_masks(segment):
    nblocks = segment.shape[0] // SPAN
    blocks = segment.reshape(nblocks, SPAN)
    head_seg = blocks[:, 0]
    following = jnp.concatenate([head_seg[1:], jnp.full((1,), -1, jnp.int32)])
    carry_keep = (head_seg == following).astype(jnp.float32)
    row_gate = (blocks == head_seg[:, None]).astype(jnp.float32)
    chosen = (blocks == following[:, None]).astype(jnp.float32)
    offsets_in = jnp.arange(SPAN, dtype=jnp.int32)
    causal = offsets_in[:, None] >= offsets_in[None, :]
    same_seq = blocks[:, :, None] == blocks[:, None, :]
    block_mask = (causal[None] & same_seq).astype(jnp.float32)
    return (carry_keep, row_gate, chosen, block_mask)


def carry_chain(carry_keep, increments):

    def combine(earlier, latter):
        return (earlier[0] * latter[0], latter[0] * earlier[1] + latter[1])

    factors = jnp.broadcast_to(carry_keep[:, None, None, None], increments.shape)
    return lax.associative_scan(combine, (factors, increments))[1]


def block_states(carry_keep, picked, block_v):
    increments = jnp.einsum("bshj,bshe->bhje", picked, block_v, precision=highest)
    totals = carry_chain(carry_keep, increments)
    return jnp.concatenate([jnp.zeros_like(totals[:1]), totals[:-1]], 0)


def attend(query_feat, key_feat, extended, masks):
    carry_keep, row_gate, chosen, block_mask = masks
    nblocks, span_len = row_gate.shape
    head_count = query_feat.shape[1]
    block_q = query_feat.reshape(nblocks, span_len, head_count, -1)
    block_k = key_feat.reshape(nblocks, span_len, head_count, -1)
    block_v = extended.reshape(nblocks, span_len, head_count, -1)
    scores = (
        jnp.einsum("bthj,bshj->bhts", block_q, block_k, precision=highest) * block_mask[:, None]
    )
    inside = jnp.einsum("bhts,bshe->bthe", scores, block_v, precision=highest)
    states = block_states(carry_keep, block_k * chosen[:, :, None, None], block_v)
    outside = jnp.einsum(
        "bthj,bhje->bthe", block_q * row_gate[:, :, None, None], states, precision=highest
    )
    return (inside + outside).reshape(nblocks * span_len, head_count, -1)


def attend_back(query_feat, key_feat, extended, masks, upstream):
    carry_keep, row_gate, chosen, block_mask = masks
    nblocks, span_len = row_gate.shape
    head_count = query_feat.shape[1]
    block_q = query_feat.reshape(nblocks, span_len, head_count, -1)
    block_k = key_feat.reshape(nblocks, span_len, head_count, -1)
    block_v = extended.reshape(nblocks, span_len, head_count, -1)
    block_g = upstream.reshape(nblocks, span_len, head_count, -1)
    picked = block_k * chosen[:, :, None, None]
    gated = block_q * row_gate[:, :, None, None]
    scores = (
        jnp.einsum("bthj,bshj->bhts", block_q, block_k, precision=highest) * block_mask[:, None]
    )
    states = block_states(carry_keep, picked, block_v)
    score_grad = (
        jnp.einsum("bthe,bshe->bhts", block_g, block_v, precision=highest) * block_mask[:, None]
    )
    query_grad = jnp.einsum("bhts,bshj->bthj", score_grad, block_k, precision=highest)
    query_grad = query_grad + row_gate[:, :, None, None] * jnp.einsum(
        "bthe,bhje->bthj", block_g, states, precision=highest
    )
    key_grad = jnp.einsum("bhts,bthj->bshj", score_grad, block_q, precision=highest)
    value_grad = jnp.einsum("bhts,bthe->bshe", scores, block_g, precision=highest)
    state_grad = jnp.einsum("bthj,bthe->bhje", gated, block_g, precision=highest)
    later_total = jnp.flip(carry_chain(jnp.flip(carry_keep, 0), jnp.flip(state_grad, 0)), 0)
    incr_grad = jnp.concatenate([later_total[1:], jnp.zeros_like(later_total[:1])], 0)
    key_grad = key_grad + chosen[:, :, None, None] * jnp.einsum(
        "bhje,bshe->bshj", incr_grad, block_v, precision=highest
    )
    value_grad = value_grad + jnp.einsum("bshj,bhje->bshe", picked, incr_grad, precision=highest)
    row_total = nblocks * span_len
    return (
        query_grad.reshape(row_total, head_count, -1),
        key_grad.reshape(row_total, head_count, -1),
        value_grad.reshape(row_total, head_count, -1),
    )


def on_device(
    tokens,
    doc_lengths,
    norm_gain,
    norm_shift,
    qkv_weight,
    qkv_bias,
    omega,
    qmc_weights,
    out_weight,
    out_bias,
    up_weight,
    up_bias,
    down_weight,
    out_grad,
):
    feat_parts = lax.axis_size(FEAT)
    feat_index = lax.axis_index(FEAT)
    qkv_full, up_full, out_rows, down_rows = (
        lax.all_gather(qkv_weight, DP, axis=0, tiled=True),
        lax.all_gather(up_weight, DP, axis=0, tiled=True),
        lax.all_gather(out_weight, DP, axis=1, tiled=True),
        lax.all_gather(down_weight, DP, axis=1, tiled=True),
    )
    gain_vec = norm_gain.astype(jnp.float32)
    shift_vec = norm_shift.astype(jnp.float32)
    inputs = tokens.astype(jnp.float32)
    row_sums = lax.psum((jnp.sum(inputs, 1), jnp.sum(inputs * inputs, 1)), FEAT)
    center = row_sums[0] / D
    spread = row_sums[1] / D - center * center
    inv_root = lax.rsqrt(spread + epsilon)
    standard = (inputs - center[:, None]) * inv_root[:, None]
    normed_all = lax.all_gather(
        (standard * gain_vec + shift_vec).astype(jnp.bfloat16), FEAT, axis=1, tiled=True
    )
    local_width = tokens.shape[1]
    local_heads = local_width // HD
    feat_count = M // feat_parts
    omega_used = lax.dynamic_slice_in_dim(omega, feat_index * feat_count, feat_count, 1)
    weights_used = lax.dynamic_slice_in_dim(qmc_weights, feat_index * feat_count, feat_count, 0)
    row_count = tokens.shape[0] // MB
    qkv_bias_f = qkv_bias.astype(jnp.float32)
    up_bias_f = up_bias.astype(jnp.float32)
    out_bias_f = out_bias.astype(jnp.float32)
    block_outs = []
    saved_state = []
    for micro_idx in range(MB):
        offset = micro_idx * row_count
        normed_rows = normed_all[offset : offset + row_count]
        segment, positions = row_layout(doc_lengths[micro_idx], row_count)
        masks = block_masks(segment)
        projected = (
            jnp.einsum("rd,dcf->rcf", normed_rows, qkv_full, preferred_element_type=jnp.float32)
            + qkv_bias_f
        ).astype(jnp.bfloat16)
        pre_act = jnp.dot(normed_rows, up_full, preferred_element_type=jnp.float32) + up_bias_f
        hidden = gelu_exact(pre_act).astype(jnp.bfloat16)
        projected_used = lax.all_gather(projected, FEAT, axis=2, tiled=True)
        heads_used = projected_used.shape[2] // HD
        heads_view = projected_used.astype(jnp.float32).reshape(row_count, 3, heads_used, HD)
        queries = heads_view[:, 0]
        keys_raw = heads_view[:, 1]
        query_map, key_map = both_maps(queries, keys_raw, positions, omega_used, weights_used)
        query_feat = query_map.astype(jnp.bfloat16).astype(jnp.float32)
        key_feat = key_map.astype(jnp.bfloat16).astype(jnp.float32)
        extended = jnp.concatenate(
            [heads_view[:, 2], jnp.ones((row_count, heads_used, 1), jnp.float32)], 2
        )
        mixed = attend(query_feat, key_feat, extended, masks)
        numerator = mixed[..., :HD]
        denominator = mixed[..., HD]
        numerator, denominator = (
            lax.psum_scatter(numerator, FEAT, scatter_dimension=1, tiled=True),
            lax.psum_scatter(denominator, FEAT, scatter_dimension=1, tiled=True),
        )
        attended = (
            (numerator / denominator[..., None])
            .reshape(row_count, local_width)
            .astype(jnp.bfloat16)
        )
        branch = jnp.dot(attended, out_rows, preferred_element_type=jnp.float32)
        branch = branch + jnp.dot(hidden, down_rows, preferred_element_type=jnp.float32)
        summed = lax.psum_scatter(
            branch.astype(jnp.bfloat16), FEAT, scatter_dimension=1, tiled=True
        ).astype(jnp.float32)
        block_outs.append(
            (inputs[offset : offset + row_count] + summed + out_bias_f).astype(jnp.bfloat16)
        )
        saved_state.append(
            (
                normed_rows,
                positions,
                masks,
                pre_act,
                hidden,
                queries,
                keys_raw,
                extended,
                query_feat,
                key_feat,
                numerator,
                denominator,
                attended,
            )
        )
    qkv_acc = jnp.zeros(qkv_full.shape, jnp.float32)
    up_acc = jnp.zeros(up_full.shape, jnp.float32)
    outw_acc = jnp.zeros(out_rows.shape, jnp.float32)
    down_acc = jnp.zeros(down_rows.shape, jnp.float32)
    qkv_bias_acc = jnp.zeros((3, local_width), jnp.float32)
    up_bias_acc = jnp.zeros((up_full.shape[1],), jnp.float32)
    normed_grads = []
    for micro_idx in range(MB):
        offset = micro_idx * row_count
        (
            normed_rows,
            positions,
            masks,
            pre_act,
            hidden,
            queries,
            keys_raw,
            extended,
            query_feat,
            key_feat,
            numerator,
            denominator,
            attended,
        ) = saved_state[micro_idx]
        cotangent = lax.all_gather(
            out_grad[offset : offset + row_count], FEAT, axis=1, tiled=True
        )
        outw_acc = outw_acc + jnp.einsum(
            "rk,rd->kd", attended, cotangent, preferred_element_type=jnp.float32
        )
        down_acc = down_acc + jnp.einsum(
            "rk,rd->kd", hidden, cotangent, preferred_element_type=jnp.float32
        )
        att_grad = jnp.einsum("rd,kd->rk", cotangent, out_rows, preferred_element_type=jnp.float32)
        hidden_grad = jnp.einsum(
            "rd,kd->rk", cotangent, down_rows, preferred_element_type=jnp.float32
        )
        _, gelu_pull = jax.vjp(gelu_exact, pre_act)
        pre_grad = gelu_pull(hidden_grad)[0].astype(jnp.bfloat16)
        up_acc = up_acc + jnp.einsum(
            "rd,rk->dk", normed_rows, pre_grad, preferred_element_type=jnp.float32
        )
        up_bias_acc = up_bias_acc + jnp.sum(pre_grad.astype(jnp.float32), 0)
        att_grad = att_grad.reshape(row_count, local_heads, HD)
        numer_grad = (att_grad / denominator[..., None]).astype(jnp.bfloat16)
        denom_grad = (-jnp.sum(att_grad * numerator, 2) / (denominator * denominator)).astype(
            jnp.bfloat16
        )
        numer_grad, denom_grad = (
            lax.all_gather(numer_grad, FEAT, axis=1, tiled=True),
            lax.all_gather(denom_grad, FEAT, axis=1, tiled=True),
        )
        upstream = jnp.concatenate(
            [numer_grad.astype(jnp.float32), denom_grad.astype(jnp.float32)[..., None]], 2
        )
        query_feat_grad, key_feat_grad, extended_grad = attend_back(
            query_feat, key_feat, extended, masks, upstream
        )

        def map_local(query_in, key_in):
            return both_maps(query_in, key_in, positions, omega_used, weights_used)

        _, map_pull = jax.vjp(map_local, queries, keys_raw)
        query_grad, key_grad = map_pull((query_feat_grad, key_feat_grad))
        proj_rows = jnp.stack([query_grad, key_grad, extended_grad[..., :HD]], 1).reshape(
            row_count, 3, -1
        )
        proj_rows = lax.psum_scatter(proj_rows, FEAT, scatter_dimension=2, tiled=True)
        proj_grad = proj_rows.astype(jnp.bfloat16)
        qkv_acc = qkv_acc + jnp.einsum(
            "rd,rcf->dcf", normed_rows, proj_grad, preferred_element_type=jnp.float32
        )
        qkv_bias_acc = qkv_bias_acc + jnp.sum(proj_grad.astype(jnp.float32), 0)
        normed_part = jnp.einsum(
            "rcf,dcf->rd", proj_grad, qkv_full, preferred_element_type=jnp.float32
        )
        normed_part = normed_part + jnp.einsum(
            "rk,dk->rd", pre_grad, up_full, preferred_element_type=jnp.float32
        )
        normed_grads.append(
            lax.psum_scatter(
                normed_part.astype(jnp.bfloat16), FEAT, scatter_dimension=1, tiled=True
            ).astype(jnp.float32)
        )
    normed_grad = jnp.concatenate(normed_grads, 0)
    scaled = normed_grad * gain_vec
    grad_sums = lax.psum((jnp.sum(scaled, 1), jnp.sum(scaled * standard, 1)), FEAT)
    out_grad_f = out_grad.astype(jnp.float32)
    input_grad = out_grad_f + inv_root[:, None] * (
        scaled - grad_sums[0][:, None] / D - standard * grad_sums[1][:, None] / D
    )
    gain_part = jnp.sum(normed_grad * standard, 0)
    shift_part = jnp.sum(normed_grad, 0)
    out_bias_part = jnp.sum(out_grad_f, 0)
    qkv_grad, up_grad, outw_grad, down_grad = (
        lax.psum_scatter(
            qkv_acc.astype(jnp.bfloat16), DP, scatter_dimension=0, tiled=True
        ).astype(jnp.float32),
        lax.psum_scatter(up_acc.astype(jnp.bfloat16), DP, scatter_dimension=0, tiled=True).astype(
            jnp.float32
        ),
        lax.psum_scatter(
            outw_acc.astype(jnp.bfloat16), DP, scatter_dimension=1, tiled=True
        ).astype(jnp.float32),
        lax.psum_scatter(
            down_acc.astype(jnp.bfloat16), DP, scatter_dimension=1, tiled=True
        ).astype(jnp.float32),
    )
    gain_grad, shift_grad, qkv_bias_grad, out_bias_grad, up_bias_grad = lax.psum(
        (gain_part, shift_part, qkv_bias_acc, out_bias_part, up_bias_acc), DP
    )
    return (
        jnp.concatenate(block_outs, 0),
        input_grad.astype(jnp.bfloat16),
        gain_grad,
        shift_grad,
        qkv_grad,
        qkv_bias_grad,
        outw_grad,
        out_bias_grad,
        up_grad,
        up_bias_grad,
        down_grad,
    )


MESH = pl.DeviceIdType.MESH
f32, bf16 = jnp.float32, jnp.bfloat16
NT = ((1,), (1,))
TN = ((0,), (0,))
EXTRA = 16


def dot(a, b, dims=((1,), (0,)), precision=None):
    return lax.dot_general(
        a, b, (dims, ((), ())), precision=precision, preferred_element_type=f32
    )


def rotary_table(longest):
    half_rot = ROT // 2
    inv_freq = np.exp(
        -np.arange(half_rot, dtype=np.float32)
        * np.float32(2.0 / ROT)
        * np.float32(math.log(10000.0))
    ).astype(np.float32)
    angles = np.arange(longest, dtype=np.float32)[:, None] * inv_freq[None, :]
    cosine = np.ones((longest, HD), np.float32)
    sine = np.zeros((longest, HD), np.float32)
    for part in range(2):
        cosine[:, part * half_rot : (part + 1) * half_rot] = np.cos(angles)
        sine[:, part * half_rot : (part + 1) * half_rot] = np.sin(angles)
    rest = np.concatenate([cosine, cosine, sine, sine], 1).astype(np.float32)
    terms = []
    for _ in range(3):
        term = rest.astype(ml_dtypes.bfloat16)
        terms.append(term)
        rest = rest - term.astype(np.float32)
    return np.concatenate(terms, 0)


def rotary_swap():
    half_rot = ROT // 2
    one = np.zeros((HD, HD), np.float32)
    for i in range(half_rot):
        one[i + half_rot, i] = -1.0
        one[i, i + half_rot] = 1.0
    return np.kron(np.eye(4, dtype=np.float32), one).astype(ml_dtypes.bfloat16)


def dct_rows():
    ramp = np.arange(HD, dtype=np.float32)
    scale = np.where(ramp == 0.0, np.sqrt(1.0 / HD), np.sqrt(2.0 / HD))
    table = np.cos(math.pi * (2.0 * ramp[None, :] + 1.0) * ramp[:, None] / (2.0 * HD)) * scale[:, None]
    return np.tile(table.T, (4, 1)).astype(np.float32)


class Sizes:
    def __init__(self, rows, width, hidden, dp_count, feat_count):
        self.rows = rows
        self.width = width
        self.model = width * feat_count
        self.span = rows // MB
        self.total = 2 * rows
        self.micro = 2 * MB
        self.half = width // 2
        self.hidden = hidden // 2
        self.block = self.model // dp_count
        self.planes = dp_count // 2


def scratch_list(s):
    pl_, bl, hf, hd, tt, md = s.planes, s.block, s.half, s.hidden, s.total, s.model
    grads = {
        QKV: (3, bl, hf),
        OUT: (hf, bl),
        UP: (bl, hd),
        DOWN: (hd, bl),
    }
    shapes = dict(
        XG=((2, s.rows + EXTRA, md), bf16),
        G=((tt, md), bf16),
        WQ=((3, md, hf), bf16),
        WU=((md, hd), bf16),
        WO=((hf, md), bf16),
        WD=((hd, md), bf16),
        NB=((tt, md), bf16),
        MU=((tt, 1), f32),
        IV=((tt, 1), f32),
        A2=((2 * s.width // 2, s.width), f32),
        WB=((tt, 2 * hf), bf16),
        VB=((tt, hf), bf16),
        PHF=((tt, 2 * hf), f32),
        PHB=((tt, 2 * hf), bf16),
        ROTV=((tt, 2 * hf), f32),
        CSB=((tt, 2 * hf), f32),
        SB=((s.micro, 2, s.span, s.span), bf16),
        ND=((tt, 2 * hf), f32),
        AT=((tt, hf), bf16),
        PG=((tt, 3 * hf), bf16),
        HB=((tt, hd), bf16),
        GP=((tt, hd), f32),
        PRE=((tt, hd), bf16),
        QBG=((1, 3 * hf), f32),
        UBG=((1, hd), f32),
        NGF=((s.rows, s.width), f32),
        ST=((16, s.rows), f32),
        STR=((3, 16, s.rows), f32),
        SV=((24, 128), f32),
        SMALL=((3, max(2 * hd, 4 * s.width)), f32),
        IN_lens=((MB, SEQS), jnp.int32),
        IN_gain=((s.width,), bf16),
        IN_shift=((s.width,), bf16),
        IN_qkv_bias=((3, s.width), bf16),
        IN_out_bias=((s.width,), bf16),
        IN_up_bias=((2 * hd,), bf16),
        IN_qmc=((M,), f32),
        IN_tab=((3 * (s.span // 2), 2 * hf), bf16),
        IN_swap=((2 * hf, 2 * hf), bf16),
        IN_ones16=((2 * hf, 2 * hf), bf16),
        IN_dct=((2 * hf, HD), f32),
        IN_rep=((HD, 2 * hf), f32),
        IN_omega=((HD, M), f32),
        SVR=((7, 24, 128), f32),
    )
    for name, shape in grads.items():
        shapes["SX" + name] = ((pl_,) + shape, bf16)
        shapes["RX" + name] = ((pl_,) + shape, bf16)
        shapes["KX" + name] = ((pl_,) + shape, f32)
        shapes["ZS" + name] = ((3,) + shape, bf16)
        shapes["ZR" + name] = ((3,) + shape, bf16)
    for name in (BLK, NRM):
        shapes["CS" + name] = ((tt, 2 * s.width), bf16)
        shapes["CR" + name] = ((tt, 2 * s.width), bf16)
        shapes["KC" + name] = ((tt, 2 * s.width), f32)
        shapes["KY" + name] = ((tt, s.width), f32)
        shapes["YS" + name] = ((tt, s.width), bf16)
        shapes["YR" + name] = ((tt, s.width), bf16)
        shapes["AS" + name] = ((s.rows, s.width), bf16)
        shapes["AR" + name] = ((s.rows, s.width), bf16)
    return shapes


SMALL = ("lens", "gain", "shift", "qkv_bias", "out_bias", "up_bias", "qmc", "tab", "swap", "ones16", "dct", "rep", "omega")
N_LOCAL = 6 + len(SMALL)
N_REMOTE = 120


def fused_kernel(s, names, *refs):
    (tok, grd, wq_in, wu_in, wo_in, wd_in) = refs[:6]
    small_in = refs[6 : 6 + len(SMALL)]
    o_blk, o_inp, o_qkv, o_up, o_out, o_down, o_small = refs[6 + len(SMALL) : 13 + len(SMALL)]
    m_ = dict(zip(names, refs[13 + len(SMALL) :]))
    small, tab, swap, ones16 = m_["SMALL"], m_["IN_tab"], m_["IN_swap"], m_["IN_ones16"]
    dct, rep, omega = m_["IN_dct"], m_["IN_rep"], m_["IN_omega"]
    lsem, ssem, rsem = m_["lsem"], m_["ssem"], m_["rsem"]
    XG, G, WQ, WU, WO, WD = (m_[k] for k in ("XG", "G", "WQ", "WU", "WO", "WD"))
    NB, MU, IV = m_["NB"], m_["MU"], m_["IV"]

    dp = lax.axis_index(DP)
    ft = lax.axis_index(FEAT)
    z, x = dp // 2, dp % 2
    zl = z % 2
    y, c = ft // 2, ft % 2
    zd = (z, z + 1 - 2 * zl, (z + 2) % 4, 3 - z)
    hl = (zl, 1 - zl, zl, 1 - zl)

    def partner(d):
        if isinstance(d, int):
            return zd[d]
        return (z // 2 + d // 2) % 2 * 2 + (z + d) % 2

    counter = [0]

    def new(n=1):
        counter[0] += n
        return counter[0] - n

    def device(d=0, fx=False, fy=False, fc=False):
        return {
            DP: partner(d) * 2 + (1 - x if fx else x),
            FEAT: (1 - y if fy else y) * 2 + (1 - c if fc else c),
        }

    def send(src, dst, sem, where):
        copy = pltpu.make_async_remote_copy(
            src_ref=src,
            dst_ref=dst,
            send_sem=ssem.at[sem],
            recv_sem=rsem.at[sem],
            device_id=where,
            device_id_type=MESH,
        )
        return copy

    def go(src, dst, sem, where):
        send(src, dst, sem, where).start()

    def arrived(ref, sem, where):
        send(ref, ref, sem, where).wait_recv()

    mo = pl.multiple_of

    def lanes(index, size):
        return pl.ds(mo(index * size, size), size)

    def tok_at(b, f):
        return XG.at[b, :, lanes(f, s.width)]

    def grd_at(b, f):
        return G.at[lanes(b, s.rows), lanes(f, s.width)]

    def own_half(w, h):
        if w == QKV:
            return wq_in.at[:, :, lanes(h, s.half)]
        if w == UP:
            return wu_in.at[:, lanes(h, s.hidden)]
        if w == OUT:
            return wo_in.at[lanes(h, s.half), :]
        return wd_in.at[lanes(h, s.hidden), :]

    def weight_at(w, block):
        if w == QKV:
            return WQ.at[:, lanes(block, s.block), :]
        if w == UP:
            return WU.at[lanes(block, s.block), :]
        if w == OUT:
            return WO.at[:, lanes(block, s.block)]
        return WD.at[:, lanes(block, s.block)]

    ws = (QKV, OUT, UP, DOWN)

    local = [
        pltpu.make_async_copy(tok, XG.at[zl, pl.ds(0, s.rows), lanes(ft, s.width)], lsem.at[0]),
        pltpu.make_async_copy(grd, grd_at(zl, ft), lsem.at[1]),
    ]
    for i, w in enumerate(ws):
        local.append(pltpu.make_async_copy(own_half(w, zl), weight_at(w, dp), lsem.at[2 + i]))
    for i, name in enumerate(SMALL):
        local.append(pltpu.make_async_copy(small_in[i], m_["IN_" + name], lsem.at[6 + i]))
    for copy in local:
        copy.start()

    barrier = pltpu.get_barrier_semaphore()
    partners = [device(d) for d in (1, 2, 3)] + [device(d, fx=True) for d in (0, 1, 2, 3)]
    partners += [device(fy=True), device(fc=True), device(fy=True, fc=True)]
    for where in partners:
        pl.semaphore_signal(barrier, inc=1, device_id=where, device_id_type=MESH)
    pl.semaphore_wait(barrier, len(partners))
    for copy in local:
        copy.wait()

    def row_of(name):
        value = m_["IN_" + name][...].astype(f32)
        return value.reshape(1, value.shape[0])

    lens = m_["IN_lens"][...].astype(f32)
    rows = [row_of("gain"), row_of("shift")]
    for i in range(MB):
        for j in range(SEQS):
            rows.append(jnp.broadcast_to(lens[i : i + 1, j : j + 1], (1, s.width)))
    rows.append(jnp.zeros((EXTRA - len(rows), s.width), f32))
    XG[zl, s.rows : s.rows + EXTRA, lanes(ft, s.width)] = jnp.concatenate(rows, 0).astype(bf16)
    small[0:1, 0 : 2 * s.hidden] = row_of("up_bias")
    for k in range(3):
        small[1:2, k * s.width : (k + 1) * s.width] = m_["IN_qkv_bias"][k : k + 1, :].astype(f32)
    small[1:2, 3 * s.width : 4 * s.width] = row_of("out_bias")
    qmc = row_of("qmc")
    small[2:3, 0 : 2 * s.half] = jnp.concatenate([qmc, qmc, jnp.ones((1, s.half), f32)], 1)

    sem_act = {TOK: new(7), GRD: new(7)}

    def act_own(name, at, axis):
        k, where = {"c": (0, device(fc=True)), "y": (1, device(fy=True)), "z": (2, device(1))}[axis]
        go(at(zl, ft), at(zl, ft), sem_act[name] + k, where)

    def act_arrive(name, at, k):
        base = sem_act[name]
        fy = (1 - y) * 2 + c
        zb = 1 - zl
        if k == 0:
            arrived(at(zb, ft), base + 2, device(1))
            go(at(zb, ft), at(zb, ft), base + 3, device(fy=True))
            go(at(zb, ft), at(zb, ft), base + 4, device(fc=True))
        elif k == 1:
            arrived(at(zl, fy), base + 1, device(fy=True))
            go(at(zl, fy), at(zl, fy), base + 5, device(fc=True))
        else:
            arrived(at(zb, fy), base + 3, device(fy=True))
            go(at(zb, fy), at(zb, fy), base + 6, device(fc=True))

    def act_rest(name, at):
        base = sem_act[name]
        fc = y * 2 + 1 - c
        fyc = (1 - y) * 2 + 1 - c
        for k, b, f in ((0, zl, fc), (4, 1 - zl, fc), (5, zl, fyc), (6, 1 - zl, fyc)):
            arrived(at(b, f), base + k, device(fc=True))

    def act_gathered(name, at):
        base = sem_act[name]
        fy = (1 - y) * 2 + c
        zb = 1 - zl
        to_c, to_y = device(fc=True), device(fy=True)
        for k, b, f, where in (
            (0, zl, ft, to_c),
            (1, zl, ft, to_y),
            (2, zl, ft, device(1)),
            (3, zb, ft, to_y),
            (4, zb, ft, to_c),
            (5, zl, fy, to_c),
            (6, zb, fy, to_c),
        ):
            send(at(b, f), at(b, f), base + k, where).wait_send()

    sem_z = {w: new(3) for w in ws}
    sem_x = {w: new(4) for w in ws}

    def w_z(w, d):
        go(own_half(w, hl[d]), weight_at(w, dp), sem_z[w] + d - 1, device(d))

    def w_own(w):
        go(weight_at(w, dp), weight_at(w, dp), sem_x[w], device(fx=True))

    def w_forward(w, d):
        at = weight_at(w, partner(d) * 2 + x)
        arrived(at, sem_z[w] + d - 1, device(d))
        go(at, at, sem_x[w] + d, device(fx=True))

    def w_sent(w):
        for d in range(4):
            at = weight_at(w, zd[d] * 2 + x)
            send(at, at, sem_x[w] + d, device(fx=True)).wait_send()
            if d > 0:
                send(own_half(w, hl[d]), weight_at(w, dp), sem_z[w] + d - 1, device(d)).wait_send()

    def w_rest(w):
        for d in range(4):
            arrived(weight_at(w, zd[d] * 2 + 1 - x), sem_x[w] + d, device(fx=True))

    sem_gx = {w: new(4) for w in ws}
    sem_gz = {w: new(3) for w in ws}

    def put_grad(w, zp, mine, theirs):
        m_["KX" + w][zp] = mine
        m_["SX" + w][zp] = theirs.astype(bf16)
        src, dst = m_["SX" + w].at[zp], m_["RX" + w].at[zp]
        send(src, dst, sem_gx[w] + zp, device(fx=True)).start()

    def grad_z(w, d):
        zp = zd[d]
        arrived(m_["RX" + w].at[zp], sem_gx[w] + zp, device(fx=True))
        both = m_["KX" + w][zp] + m_["RX" + w][zp].astype(f32)
        if d == 0:
            m_["KX" + w][zp] = both
        else:
            m_["ZS" + w][d - 1] = both.astype(bf16)
            go(m_["ZS" + w].at[d - 1], m_["ZR" + w].at[d - 1], sem_gz[w] + d - 1, device(d))

    def grad_last(w):
        for d in (1, 2, 3):
            arrived(m_["ZR" + w].at[d - 1], sem_gz[w] + d - 1, device(d))
        got = m_["ZR" + w]
        same = m_["KX" + w][z] + got[1].astype(f32)
        other = got[0].astype(f32) + got[2].astype(f32)
        if w == QKV:
            o_qkv[:, :, lanes(zl, s.half)] = same
            o_qkv[:, :, lanes(1 - zl, s.half)] = other
        elif w == UP:
            o_up[:, lanes(zl, s.hidden)] = same
            o_up[:, lanes(1 - zl, s.hidden)] = other
        elif w == OUT:
            o_out[lanes(zl, s.half), :] = same
            o_out[lanes(1 - zl, s.half), :] = other
        else:
            o_down[lanes(zl, s.hidden), :] = same
            o_down[lanes(1 - zl, s.hidden), :] = other

    def grad_sent(w):
        for zp in range(4):
            send(m_["SX" + w].at[zp], m_["RX" + w].at[zp], sem_gx[w] + zp, device(fx=True)).wait_send()
        for d in (1, 2, 3):
            send(m_["ZS" + w].at[d - 1], m_["ZR" + w].at[d - 1], sem_gz[w] + d - 1, device(d)).wait_send()

    def pick(flag, a, b):
        return jnp.where(flag == 0, a, b)

    def halves(value, axis):
        n = value.shape[axis] // 2
        lo, hi = lax.slice_in_dim(value, 0, n, axis=axis), lax.slice_in_dim(value, n, 2 * n, axis=axis)
        return pick(x, lo, hi), pick(x, hi, lo)

    sem_c = {k: new(4) for k in (BLK, NRM)}
    sem_y = {k: new(4) for k in (BLK, NRM)}
    sem_a = {k: new(2) for k in (BLK, NRM)}

    def rows_of(i):
        block = (1 - zl) + (i // MB) * (2 * zl - 1)
        return pl.ds(mo(block * s.rows + (i % MB) * s.span, s.span), s.span)

    def act_put(name, i, value):
        r = rows_of(i)
        w_ = s.width
        v = [value[:, k * w_ : (k + 1) * w_] for k in range(4)]
        m_["KC" + name][r, 0:w_] = pick(c, v[0], v[1])
        m_["KC" + name][r, w_ : 2 * w_] = pick(c, v[2], v[3])
        m_["CS" + name][r, 0:w_] = pick(c, v[1], v[0]).astype(bf16)
        m_["CS" + name][r, w_ : 2 * w_] = pick(c, v[3], v[2]).astype(bf16)
        send(m_["CS" + name].at[r], m_["CR" + name].at[r], sem_c[name] + i, device(fc=True)).start()

    def act_y(name, i):
        r = rows_of(i)
        w_ = s.width
        arrived(m_["CR" + name].at[r], sem_c[name] + i, device(fc=True))
        both = m_["KC" + name][r, :] + m_["CR" + name][r, :].astype(f32)
        lo, hi = both[:, :w_], both[:, w_:]
        m_["KY" + name][r, :] = pick(y, lo, hi)
        m_["YS" + name][r, :] = pick(y, hi, lo).astype(bf16)
        send(m_["YS" + name].at[r], m_["YR" + name].at[r], sem_y[name] + i, device(fy=True)).start()

    def act_z(name, i):
        r = rows_of(i)
        q = pl.ds(i * s.span, s.span)
        arrived(m_["YR" + name].at[r], sem_y[name] + i, device(fy=True))
        both = m_["KY" + name][r, :] + m_["YR" + name][r, :].astype(f32)
        m_["AS" + name][q, :] = both.astype(bf16)
        go(m_["AS" + name].at[q], m_["AR" + name].at[q], sem_a[name] + i, device(1))

    def act_last(name, i):
        r = rows_of(MB + i)
        q = pl.ds(i * s.span, s.span)
        arrived(m_["YR" + name].at[r], sem_y[name] + MB + i, device(fy=True))
        arrived(m_["AR" + name].at[q], sem_a[name] + i, device(1))
        return (
            m_["KY" + name][r, :]
            + m_["YR" + name][r, :].astype(f32)
            + m_["AR" + name][q, :].astype(f32)
        )

    def act_sent(name):
        for i in range(4):
            r = rows_of(i)
            send(m_["CS" + name].at[r], m_["CR" + name].at[r], sem_c[name] + i, device(fc=True)).wait_send()
            send(m_["YS" + name].at[r], m_["YR" + name].at[r], sem_y[name] + i, device(fy=True)).wait_send()
        for i in range(MB):
            q = pl.ds(i * s.span, s.span)
            send(m_["AS" + name].at[q], m_["AR" + name].at[q], sem_a[name] + i, device(1)).wait_send()

    def beside(*steps):
        def side(i):
            for at in sorted(set(step[0] for step in steps)):

                @pl.when(i == at)
                def _():
                    for when, do, *args in steps:
                        if when == at:
                            do(*args)

        return side

    def loop(n, body, side=None):
        def step(i, carry):
            if side is not None:
                side(i)
            body(i)
            return carry

        lax.fori_loop(0, n, step, 0)

    def at_micro(m):
        return pl.ds(mo(m * s.span, s.span), s.span)

    def norm_phase(side=None):
        extra = XG[0, s.rows : s.rows + EXTRA, :].astype(f32)
        gain, shift = extra[0:1], extra[1:2]

        def body(m):
            xv = XG[m // MB, pl.ds(mo((m % MB) * s.span, s.span), s.span), :].astype(f32)
            mu = jnp.sum(xv, 1, keepdims=True) * (1.0 / s.model)
            var = jnp.sum(xv * xv, 1, keepdims=True) * (1.0 / s.model) - mu * mu
            inv = lax.rsqrt(var + epsilon)
            r = at_micro(m)
            MU[r, :] = mu
            IV[r, :] = inv
            NB[r, :] = ((xv - mu) * inv * gain + shift).astype(bf16)

        loop(s.micro, body, side)

    def masks(m):
        extra = XG[m // MB, s.rows : s.rows + EXTRA, 0 : s.span].astype(f32)
        row_id = lax.broadcasted_iota(jnp.int32, extra.shape, 0)
        first = 2 + SEQS * (m % MB)

        def length(k):
            return jnp.sum(jnp.where(row_id == first + k, extra, 0.0), 0, keepdims=True)

        end0 = length(0)
        end1 = end0 + length(1)
        t = lax.broadcasted_iota(jnp.int32, (s.span, s.span), 0).astype(f32)
        u = lax.broadcasted_iota(jnp.int32, (s.span, s.span), 1).astype(f32)
        start = jnp.where(t >= end1, end1, jnp.where(t >= end0, end0, 0.0))
        return jnp.logical_and(u <= t, u >= start), t, u, start

    def head_rows():
        lane = lax.broadcasted_iota(jnp.int32, (1, s.half), 1)
        return [jnp.where(lane // HD == h, 1.0, 0.0).astype(bf16) for h in range(2)], [
            jnp.where(lane == h * HD, 1.0, 0.0).astype(bf16) for h in range(2)
        ]

    HIGH = lax.Precision.HIGH
    HIGHEST = lax.Precision.HIGHEST
    hf = s.half

    def table_phase():
        wide = dot(dot(dct[...], omega[...], precision=HIGHEST), rep[...], precision=HIGHEST)
        m_["A2"][...] = wide * (ones16[...].astype(f32) * (16.0 * HD ** (-0.25)))

    def fwd_phase(side=None):
        def body(m):
            r = at_micro(m)
            wq = jnp.concatenate([WQ[0], WQ[1], WQ[2]], 1)
            bias = jnp.concatenate(
                [small[1:2, pl.ds(mo(k * s.width + zl * hf, hf), hf)] for k in range(3)], 1
            )
            p = (dot(NB[r, :], wq) + bias).astype(bf16)
            w, v = p[:, : 2 * hf], p[:, 2 * hf :]
            m_["VB"][r, :] = v
            mask, t, u, start = masks(m)
            pos = t[:, :hf] - start[:, :hf]
            hot = jnp.where(pos == u[:, :hf], 1.0, 0.0).astype(bf16)
            cs = dot(jnp.concatenate([hot, hot, hot], 1), tab[...])
            m_["CSB"][r, :] = cs
            cc = jnp.concatenate([cs[:, :hf], cs[:, :hf]], 1)
            ss = jnp.concatenate([cs[:, hf:], cs[:, hf:]], 1)
            wf = w.astype(f32)
            rot = wf * cc + dot(w, swap[...]) * ss
            m_["ROTV"][r, :] = rot
            score = dot(rot, m_["A2"][...], precision=HIGH)
            norm2 = dot(wf * wf, ones16[...].astype(f32), precision=HIGH)
            ph = jnp.exp(score - norm2) * small[2:3, 0 : 2 * hf]
            m_["PHF"][r, :] = ph
            pb = ph.astype(bf16)
            m_["PHB"][r, :] = pb
            hm, _ = head_rows()
            acc = jnp.zeros((s.span, 2 * hf), f32)
            for h in range(2):
                sc = dot(pb[:, :hf] * hm[h], pb[:, hf:], NT)
                sm = jnp.where(mask, sc, 0.0).astype(bf16)
                m_["SB"][m, h] = sm
                rhs = jnp.concatenate([v * hm[h], jnp.broadcast_to(hm[h], v.shape)], 1)
                acc = acc + dot(sm, rhs)
            m_["ND"][r, :] = acc
            m_["AT"][r, :] = (acc[:, :hf] / acc[:, hf:]).astype(bf16)

        loop(s.micro, body, side)

    def bwd_phase(side=None):
        m_["QBG"][...] = jnp.zeros_like(m_["QBG"])

        def body(m):
            r = at_micro(m)
            mask = masks(m)[0]
            hm, hot = head_rows()
            ag = dot(G[r, :], WO[...], NT)
            nd = m_["ND"][r, :]
            num, den = nd[:, :hf], nd[:, hf:]
            ng = (ag / den).astype(bf16)
            sums = dot(ag * num, ones16[0:hf, 0:hf].astype(f32), precision=HIGH) * 16.0
            dg = (-sums / (den * den)).astype(bf16)
            v = m_["VB"][r, :]
            pb = m_["PHB"][r, :]
            v1 = jnp.concatenate([v, jnp.ones(v.shape, bf16)], 1)
            dq = dk = dv = jnp.zeros((s.span, hf), f32)
            for h in range(2):
                e = dot(jnp.concatenate([ng * hm[h], dg * hot[h]], 1), v1, NT)
                em = jnp.where(mask, e, 0.0).astype(bf16)
                dq = dq + dot(em, pb[:, hf:] * hm[h])
                dk = dk + dot(em, pb[:, :hf] * hm[h], TN)
                dv = dv + dot(m_["SB"][m, h], ng * hm[h], TN)
            dph = jnp.concatenate([dq, dk], 1) * m_["PHF"][r, :]
            rot = m_["ROTV"][r, :]
            both = dot(dph, ones16[...].astype(f32), precision=HIGH) * 2.0
            drot = dot(dph, m_["A2"][...], NT, precision=HIGH) - rot * both
            cs = m_["CSB"][r, :]
            cc = jnp.concatenate([cs[:, :hf], cs[:, :hf]], 1)
            ss = jnp.concatenate([cs[:, hf:], cs[:, hf:]], 1)
            dw = drot * cc + dot(drot * ss, swap[...].astype(f32), NT, precision=HIGH)
            pg = jnp.concatenate([dw, dv], 1).astype(bf16)
            m_["PG"][r, :] = pg
            m_["QBG"][...] += jnp.sum(pg.astype(f32), 0, keepdims=True)

        loop(s.micro, body, side)

    def up_phase(side=None):
        bias = small[0:1, lanes(zl, s.hidden)]

        def body(m):
            r = at_micro(m)
            pre = dot(NB[r, :], WU[...]) + bias
            cdf = 0.5 * (1.0 + lax.erf(pre * math.sqrt(0.5)))
            m_["HB"][r, :] = (pre * cdf).astype(bf16)
            m_["GP"][r, :] = cdf + pre * jnp.exp(-0.5 * pre * pre) * (1.0 / math.sqrt(2.0 * math.pi))

        loop(s.micro, body, side)

    def pre_phase(side=None):
        m_["UBG"][...] = jnp.zeros_like(m_["UBG"])

        def body(m):
            r = at_micro(m)
            pre = (dot(G[r, :], WD[...], NT) * m_["GP"][r, :]).astype(bf16)
            m_["PRE"][r, :] = pre
            m_["UBG"][...] += jnp.sum(pre.astype(f32), 0, keepdims=True)

        loop(s.micro, body, side)

    def nrm_phase(side=None):
        def body(i):
            r = rows_of(i)
            wq = jnp.concatenate([WQ[0], WQ[1], WQ[2]], 1)
            act_put(NRM, i, dot(m_["PG"][r, :], wq, NT) + dot(m_["PRE"][r, :], WU[...], NT))

        loop(4, body, side)

    def blk_phase(side=None):
        def body(i):
            r = rows_of(i)
            act_put(BLK, i, dot(m_["AT"][r, :], WO[...]) + dot(m_["HB"][r, :], WD[...]))

        loop(4, body, side)

    two = 2 * s.block

    def grad_phase(w, side=None):
        def body(i):
            zp = partner(3 - i)
            cols = lanes(zp, two)
            if w == QKV:
                value = dot(NB[:, cols], m_["PG"][...], TN)
                mine, theirs = halves(value, 0)
                mine = jnp.stack([mine[:, k * hf : (k + 1) * hf] for k in range(3)], 0)
                theirs = jnp.stack([theirs[:, k * hf : (k + 1) * hf] for k in range(3)], 0)
            elif w == UP:
                mine, theirs = halves(dot(NB[:, cols], m_["PRE"][...], TN), 0)
            elif w == OUT:
                mine, theirs = halves(dot(m_["AT"][...], G[:, cols], TN), 1)
            else:
                mine, theirs = halves(dot(m_["HB"][...], G[:, cols], TN), 1)
            put_grad(w, zp, mine, theirs)

        loop(s.planes, body, side)

    def out_rows(i):
        return pl.ds(i * s.span, s.span)

    def blk_last():
        for i in range(MB):
            own = XG[zl, i * s.span : (i + 1) * s.span, lanes(ft, s.width)].astype(f32)
            bias = small[1:2, 3 * s.width : 4 * s.width]
            o_blk[out_rows(i), :] = (own + act_last(BLK, i) + bias).astype(bf16)

    sem_st = new(3)
    stat_where = [device(fc=True), device(fy=True), device(fy=True, fc=True)]

    def own_parts():
        extra = XG[0, s.rows : s.rows + EXTRA, lanes(ft, s.width)].astype(f32)
        r = lanes(zl, s.rows)
        own = XG[zl, 0 : s.rows, lanes(ft, s.width)].astype(f32)
        xhat = (own - MU[r, :]) * IV[r, :]
        return extra[0:1], xhat

    def nrm_last():
        for i in range(MB):
            m_["NGF"][out_rows(i), :] = act_last(NRM, i)
        gain, xhat = own_parts()
        ngrad = m_["NGF"][...]
        scaled = ngrad * gain
        ones = jnp.ones((8, s.width), f32)
        m_["ST"][0:8, :] = dot(ones, scaled, NT, precision=HIGHEST)
        m_["ST"][8:16, :] = dot(ones, scaled * xhat, NT, precision=HIGHEST)
        for k, where in enumerate(stat_where):
            go(m_["ST"], m_["STR"].at[k], sem_st + k, where)
        own_g = G[lanes(zl, s.rows), lanes(ft, s.width)].astype(f32)
        rows = [
            jnp.sum(ngrad * xhat, 0, keepdims=True),
            jnp.sum(ngrad, 0, keepdims=True),
            jnp.sum(own_g, 0, keepdims=True),
        ]
        sv = m_["SV"]
        sv[...] = jnp.zeros_like(sv)
        for k, row in enumerate(rows):
            for j in range(2):
                sv[2 * k + j : 2 * k + j + 1, :] = row[:, j * 128 : (j + 1) * 128]
        for k in range(3):
            sv[pl.ds(6 + 2 * k + zl, 1), :] = m_["QBG"][0:1, k * hf : (k + 1) * hf]
        for j in range(s.hidden // 128):
            sv[pl.ds(12 + zl * (s.hidden // 128) + j, 1), :] = m_["UBG"][0:1, j * 128 : (j + 1) * 128]

    sem_sv = new(7)
    sv_where = [device(d) for d in (1, 2, 3)] + [device(d, fx=True) for d in (0, 1, 2, 3)]

    def small_send():
        for k, where in enumerate(sv_where):
            go(m_["SV"], m_["SVR"].at[k], sem_sv + k, where)

    def small_last():
        total = m_["SV"][...]
        for k, where in enumerate(sv_where):
            arrived(m_["SVR"].at[k], sem_sv + k, where)
            total = total + m_["SVR"][k]
        o_small[...] = total

    def input_last():
        total = m_["ST"][...]
        for k, where in enumerate(stat_where):
            arrived(m_["STR"].at[k], sem_st + k, where)
            total = total + m_["STR"][k]
        spread = jnp.full((8, s.width), 1.0 / (8.0 * s.model), f32)
        mean1 = dot(total[0:8, :], spread, TN, precision=HIGHEST)
        mean2 = dot(total[8:16, :], spread, TN, precision=HIGHEST)
        gain, xhat = own_parts()
        own_g = G[lanes(zl, s.rows), lanes(ft, s.width)].astype(f32)
        scaled = m_["NGF"][...] * gain
        inv = IV[lanes(zl, s.rows), :]
        o_inp[...] = (own_g + inv * (scaled - mean1 - xhat * mean2)).astype(bf16)

    act_own(TOK, tok_at, "y")
    act_own(TOK, tok_at, "z")
    w_own(DOWN)
    act_own(GRD, grd_at, "c")
    w_z(QKV, 2)
    w_own(QKV)
    w_z(QKV, 1)
    act_own(GRD, grd_at, "z")
    act_own(GRD, grd_at, "y")
    w_forward(QKV, 2)
    w_forward(QKV, 1)
    act_own(TOK, tok_at, "c")
    act_arrive(TOK, tok_at, 0)
    w_z(OUT, 2)
    w_z(QKV, 3)
    table_phase()
    act_arrive(TOK, tok_at, 1)
    w_own(OUT)
    w_own(UP)
    act_arrive(GRD, grd_at, 0)
    act_arrive(TOK, tok_at, 2)
    w_z(UP, 1)
    w_forward(QKV, 3)
    w_z(UP, 3)
    w_z(OUT, 1)
    act_rest(TOK, tok_at)
    norm_phase(
        beside(
            (1, w_z, OUT, 3),
        ),
    )
    w_forward(OUT, 2)
    w_rest(QKV)
    fwd_phase(
        beside(
            (1, w_forward, UP, 1),
            (2, act_arrive, GRD, grd_at, 1),
            (2, w_forward, UP, 3),
            (2, w_z, UP, 2),
            (2, w_forward, OUT, 1),
            (2, act_arrive, GRD, grd_at, 2),
        ),
    )
    w_forward(OUT, 3)
    w_z(DOWN, 1)
    act_rest(GRD, grd_at)
    grad_phase(OUT)
    w_z(DOWN, 3)
    w_forward(UP, 2)
    w_rest(OUT)
    bwd_phase(
        beside(
            (2, w_z, DOWN, 2),
            (2, w_forward, DOWN, 1),
            (3, w_forward, DOWN, 3),
        ),
    )
    grad_phase(
        QKV,
        beside(
            (1, grad_z, OUT, 2),
            (2, grad_z, OUT, 3),
            (2, grad_z, OUT, 1),
            (2, w_forward, DOWN, 2),
        ),
    )
    w_rest(UP)
    up_phase(
        beside(
            (1, grad_z, QKV, 3),
        ),
    )
    grad_z(QKV, 2)
    grad_phase(DOWN)
    w_rest(DOWN)
    blk_phase(
        beside(
            (3, act_y, BLK, 0),
        ),
    )
    grad_z(QKV, 1)
    pre_phase()
    act_z(BLK, 0)
    grad_z(DOWN, 3)
    grad_z(OUT, 0)
    act_y(BLK, 1)
    nrm_phase(
        beside(
            (2, grad_last, OUT),
        ),
    )
    act_y(NRM, 0)
    grad_z(DOWN, 1)
    grad_z(DOWN, 2)
    grad_phase(
        UP,
        beside(
            (2, act_y, NRM, 1),
            (3, act_y, BLK, 3),
            (3, act_z, NRM, 0),
        ),
    )
    act_z(NRM, 1)
    grad_z(UP, 2)
    act_z(BLK, 1)
    grad_z(DOWN, 0)
    act_y(NRM, 3)
    act_y(NRM, 2)
    act_y(BLK, 2)
    nrm_last()
    grad_z(UP, 1)
    grad_z(UP, 0)
    grad_z(QKV, 0)
    grad_z(UP, 3)
    grad_last(QKV)
    small_send()
    input_last()
    blk_last()
    grad_last(DOWN)
    grad_last(UP)
    small_last()
    act_gathered(TOK, tok_at)
    act_gathered(GRD, grd_at)
    for w in ws:
        w_sent(w)
        grad_sent(w)
    for name in (BLK, NRM):
        act_sent(name)
    for k, where in enumerate(stat_where):
        send(m_["ST"], m_["STR"].at[k], sem_st + k, where).wait_send()
    for k, where in enumerate(sv_where):
        send(m_["SV"], m_["SVR"].at[k], sem_sv + k, where).wait_send()
    assert counter[0] <= N_REMOTE


def finish_kernel(*refs):
    whole, small = refs[:6], refs[6]
    outs, (gain, shift, out_bias, qkv_bias, up_bias) = refs[7:13], refs[13:18]
    sem = refs[18]
    copies = [pltpu.make_async_copy(whole[i], outs[i], sem.at[i]) for i in range(6)]
    for copy in copies:
        copy.start()
    for k, ref in enumerate((gain, shift, out_bias)):
        ref[...] = small[2 * k : 2 * k + 2, :]
    for k in range(3):
        for j in range(2):
            ref = qkv_bias.at[k : k + 1, j * 128 : (j + 1) * 128]
            ref[...] = small[6 + 2 * k + j : 7 + 2 * k + j, :]
    up_bias[...] = small[12 : 12 + up_bias.shape[0], :]
    for copy in copies:
        copy.wait()


def on_device_fused(
    dp_count,
    feat_count,
    tokens,
    doc_lengths,
    norm_gain,
    norm_shift,
    qkv_weight,
    qkv_bias,
    omega,
    qmc_weights,
    out_weight,
    out_bias,
    up_weight,
    up_bias,
    down_weight,
    out_grad,
):
    rows, width = tokens.shape
    s = Sizes(rows, width, up_weight.shape[1], dp_count, feat_count)
    ones16 = np.kron(np.eye(4), np.full((HD, HD), 1.0 / 16.0)).astype(ml_dtypes.bfloat16)
    rep = np.tile(np.eye(HD, dtype=np.float32), (1, 4))
    shapes = scratch_list(s)
    names = list(shapes) + ["lsem", "ssem", "rsem"]
    scratch = [pltpu.VMEM(shape, kind) for shape, kind in shapes.values()]
    scratch += [
        pltpu.SemaphoreType.DMA((N_LOCAL,)),
        pltpu.SemaphoreType.DMA((N_REMOTE,)),
        pltpu.SemaphoreType.DMA((N_REMOTE,)),
    ]
    results = [
        ((rows, width), bf16),
        ((rows, width), bf16),
        ((3, s.block, width), f32),
        (up_weight.shape, f32),
        (out_weight.shape, f32),
        (down_weight.shape, f32),
        ((24, 128), f32),
    ]
    raw = pl.BlockSpec(memory_space=pl.ANY)
    vm = pl.BlockSpec(memory_space=pltpu.VMEM)
    outs = pl.pallas_call(
        functools.partial(fused_kernel, s, names),
        out_shape=tuple(pltpu.VMEM(shape, kind) for shape, kind in results),
        in_specs=[raw] * (6 + len(SMALL)),
        out_specs=[vm] * 7,
        scratch_shapes=scratch,
        compiler_params=pltpu.CompilerParams(
            collective_id=0, has_side_effects=True, vmem_limit_bytes=56 * 2**20
        ),
    )(
        tokens,
        out_grad,
        jnp.transpose(qkv_weight, (1, 0, 2)),
        up_weight,
        out_weight,
        down_weight,
        doc_lengths,
        norm_gain,
        norm_shift,
        qkv_bias,
        out_bias,
        up_bias,
        qmc_weights,
        jnp.asarray(rotary_table(rows // MB // 2)),
        jnp.asarray(rotary_swap()),
        jnp.asarray(ones16),
        jnp.asarray(dct_rows()),
        jnp.asarray(rep),
        omega,
    )
    whole = [jax.ShapeDtypeStruct(shape, kind) for shape, kind in results[:6]]
    full = up_bias.shape[0]
    short = [(width // 128, 128)] * 3 + [(3, width), (full // 128, 128)]
    done = pl.pallas_call(
        finish_kernel,
        out_shape=tuple(whole) + tuple(jax.ShapeDtypeStruct(shape, f32) for shape in short),
        in_specs=[vm] * 7,
        out_specs=[raw] * 6 + [vm] * 5,
        scratch_shapes=[pltpu.SemaphoreType.DMA((6,))],
        compiler_params=pltpu.CompilerParams(vmem_limit_bytes=4 * 2**20),
    )(*(pltpu.with_memory_space_constraint(out, pltpu.VMEM) for out in outs))
    o_blk, o_inp, o_qkv, o_up, o_out, o_down, gain, shift, out_bias_grad, qkv_bias_grad, up_bias_grad = done
    return (
        o_blk,
        o_inp,
        gain.reshape(-1),
        shift.reshape(-1),
        jnp.transpose(o_qkv, (1, 0, 2)),
        qkv_bias_grad,
        o_out,
        out_bias_grad.reshape(-1),
        o_up,
        up_bias_grad.reshape(-1),
        o_down,
    )


def solution(mesh):
    in_specs = (
        P(DP, FEAT),
        P(DP, None),
        P(FEAT),
        P(FEAT),
        P(DP, None, FEAT),
        P(None, FEAT),
        P(),
        P(),
        P(FEAT, DP),
        P(FEAT),
        P(DP, FEAT),
        P(FEAT),
        P(FEAT, DP),
        P(DP, FEAT),
    )
    out_specs = (
        P(DP, FEAT),
        P(DP, FEAT),
        P(FEAT),
        P(FEAT),
        P(DP, None, FEAT),
        P(None, FEAT),
        P(FEAT, DP),
        P(FEAT),
        P(DP, FEAT),
        P(FEAT),
        P(FEAT, DP),
    )
    dp_count, feat_count = mesh.shape[DP], mesh.shape[FEAT]
    if (dp_count, feat_count) == (8, 4):
        per_device = functools.partial(on_device_fused, dp_count, feat_count)
    else:
        per_device = on_device
    return jax.shard_map(
        per_device, mesh=mesh, in_specs=in_specs, out_specs=out_specs, check_vma=False
    )
```

```python
import functools
import math

import jax
import jax.numpy as jnp
import ml_dtypes
import numpy as np
from jax import lax
from jax.experimental import pallas as pl
from jax.experimental.pallas import tpu as pltpu
from jax.sharding import PartitionSpec as P

D = 1024
HD = 64
ROT = 16
M = 64
SPAN = 64
MB = 2
SEQS = 3


FEAT = "feat"
DP = "dp"
QKV = "qkv"
OUT = "out"
UP = "up"
DOWN = "down"
TOK = "tok"
GRD = "grd"
NRM = "nrm"
BLK = "blk"


epsilon = 1e-05
highest = lax.Precision.HIGHEST


def row_layout(lengths, row_count):
    seq_ends = jnp.cumsum(lengths)
    starts = seq_ends - lengths
    row_ids = jnp.arange(row_count, dtype=jnp.int32)
    segment = jnp.sum((row_ids[:, None] >= seq_ends[None, :]).astype(jnp.int32), 1)
    belongs = segment[:, None] == jnp.arange(lengths.shape[0], dtype=jnp.int32)[None, :]
    row_begin = jnp.sum(jnp.where(belongs, starts[None, :], 0), 1)
    return (segment, (row_ids - row_begin).astype(jnp.float32))


def rotate(vectors, positions):
    half_rot = ROT // 2
    inv_freq = jnp.exp(-jnp.arange(half_rot, dtype=jnp.float32) * (2.0 / ROT) * math.log(10000.0))
    angles = positions[:, None] * inv_freq[None, :]
    cosine = jnp.cos(angles)[:, None, :]
    sine = jnp.sin(angles)[:, None, :]
    lower_part = vectors[..., :half_rot]
    upper_part = vectors[..., half_rot:ROT]
    return jnp.concatenate(
        [
            lower_part * cosine - upper_part * sine,
            upper_part * cosine + lower_part * sine,
            vectors[..., ROT:],
        ],
        -1,
    )


def dct_table():
    ramp_vals = jnp.arange(HD, dtype=jnp.float32)
    weights_row = jnp.where(ramp_vals == 0.0, jnp.sqrt(1.0 / HD), jnp.sqrt(2.0 / HD))
    return (
        jnp.cos(math.pi * (2.0 * ramp_vals[None, :] + 1.0) * ramp_vals[:, None] / (2.0 * HD))
        * weights_row[:, None]
    )


def feature_map(vectors, positions, omega):
    turned = rotate(vectors, positions) * HD ** (-0.25)
    spectrum = jnp.einsum("rhn,kn->rhk", turned, dct_table(), precision=highest)
    scores = jnp.einsum("rhk,kj->rhj", spectrum, omega, precision=highest)
    return jnp.exp(scores - 0.5 * jnp.sum(turned * turned, -1, keepdims=True))


def both_maps(queries, keys_raw, positions, omega_used, weights_used):
    return (
        weights_used * feature_map(queries, positions, omega_used),
        feature_map(keys_raw, positions, omega_used),
    )


def gelu_exact(pre_act):
    return jax.nn.gelu(pre_act, approximate=False)


def block_masks(segment):
    nblocks = segment.shape[0] // SPAN
    blocks = segment.reshape(nblocks, SPAN)
    head_seg = blocks[:, 0]
    following = jnp.concatenate([head_seg[1:], jnp.full((1,), -1, jnp.int32)])
    carry_keep = (head_seg == following).astype(jnp.float32)
    row_gate = (blocks == head_seg[:, None]).astype(jnp.float32)
    chosen = (blocks == following[:, None]).astype(jnp.float32)
    offsets_in = jnp.arange(SPAN, dtype=jnp.int32)
    causal = offsets_in[:, None] >= offsets_in[None, :]
    same_seq = blocks[:, :, None] == blocks[:, None, :]
    block_mask = (causal[None] & same_seq).astype(jnp.float32)
    return (carry_keep, row_gate, chosen, block_mask)


def carry_chain(carry_keep, increments):

    def combine(earlier, latter):
        return (earlier[0] * latter[0], latter[0] * earlier[1] + latter[1])

    factors = jnp.broadcast_to(carry_keep[:, None, None, None], increments.shape)
    return lax.associative_scan(combine, (factors, increments))[1]


def block_states(carry_keep, picked, block_v):
    increments = jnp.einsum("bshj,bshe->bhje", picked, block_v, precision=highest)
    totals = carry_chain(carry_keep, increments)
    return jnp.concatenate([jnp.zeros_like(totals[:1]), totals[:-1]], 0)


def attend(query_feat, key_feat, extended, masks):
    carry_keep, row_gate, chosen, block_mask = masks
    nblocks, span_len = row_gate.shape
    head_count = query_feat.shape[1]
    block_q = query_feat.reshape(nblocks, span_len, head_count, -1)
    block_k = key_feat.reshape(nblocks, span_len, head_count, -1)
    block_v = extended.reshape(nblocks, span_len, head_count, -1)
    scores = (
        jnp.einsum("bthj,bshj->bhts", block_q, block_k, precision=highest) * block_mask[:, None]
    )
    inside = jnp.einsum("bhts,bshe->bthe", scores, block_v, precision=highest)
    states = block_states(carry_keep, block_k * chosen[:, :, None, None], block_v)
    outside = jnp.einsum(
        "bthj,bhje->bthe", block_q * row_gate[:, :, None, None], states, precision=highest
    )
    return (inside + outside).reshape(nblocks * span_len, head_count, -1)


def attend_back(query_feat, key_feat, extended, masks, upstream):
    carry_keep, row_gate, chosen, block_mask = masks
    nblocks, span_len = row_gate.shape
    head_count = query_feat.shape[1]
    block_q = query_feat.reshape(nblocks, span_len, head_count, -1)
    block_k = key_feat.reshape(nblocks, span_len, head_count, -1)
    block_v = extended.reshape(nblocks, span_len, head_count, -1)
    block_g = upstream.reshape(nblocks, span_len, head_count, -1)
    picked = block_k * chosen[:, :, None, None]
    gated = block_q * row_gate[:, :, None, None]
    scores = (
        jnp.einsum("bthj,bshj->bhts", block_q, block_k, precision=highest) * block_mask[:, None]
    )
    states = block_states(carry_keep, picked, block_v)
    score_grad = (
        jnp.einsum("bthe,bshe->bhts", block_g, block_v, precision=highest) * block_mask[:, None]
    )
    query_grad = jnp.einsum("bhts,bshj->bthj", score_grad, block_k, precision=highest)
    query_grad = query_grad + row_gate[:, :, None, None] * jnp.einsum(
        "bthe,bhje->bthj", block_g, states, precision=highest
    )
    key_grad = jnp.einsum("bhts,bthj->bshj", score_grad, block_q, precision=highest)
    value_grad = jnp.einsum("bhts,bthe->bshe", scores, block_g, precision=highest)
    state_grad = jnp.einsum("bthj,bthe->bhje", gated, block_g, precision=highest)
    later_total = jnp.flip(carry_chain(jnp.flip(carry_keep, 0), jnp.flip(state_grad, 0)), 0)
    incr_grad = jnp.concatenate([later_total[1:], jnp.zeros_like(later_total[:1])], 0)
    key_grad = key_grad + chosen[:, :, None, None] * jnp.einsum(
        "bhje,bshe->bshj", incr_grad, block_v, precision=highest
    )
    value_grad = value_grad + jnp.einsum("bshj,bhje->bshe", picked, incr_grad, precision=highest)
    row_total = nblocks * span_len
    return (
        query_grad.reshape(row_total, head_count, -1),
        key_grad.reshape(row_total, head_count, -1),
        value_grad.reshape(row_total, head_count, -1),
    )


def on_device(
    tokens,
    doc_lengths,
    norm_gain,
    norm_shift,
    qkv_weight,
    qkv_bias,
    omega,
    qmc_weights,
    out_weight,
    out_bias,
    up_weight,
    up_bias,
    down_weight,
    out_grad,
):
    feat_parts = lax.axis_size(FEAT)
    feat_index = lax.axis_index(FEAT)
    qkv_full, up_full, out_rows, down_rows = (
        lax.all_gather(qkv_weight, DP, axis=0, tiled=True),
        lax.all_gather(up_weight, DP, axis=0, tiled=True),
        lax.all_gather(out_weight, DP, axis=1, tiled=True),
        lax.all_gather(down_weight, DP, axis=1, tiled=True),
    )
    gain_vec = norm_gain.astype(jnp.float32)
    shift_vec = norm_shift.astype(jnp.float32)
    inputs = tokens.astype(jnp.float32)
    row_sums = lax.psum((jnp.sum(inputs, 1), jnp.sum(inputs * inputs, 1)), FEAT)
    center = row_sums[0] / D
    spread = row_sums[1] / D - center * center
    inv_root = lax.rsqrt(spread + epsilon)
    standard = (inputs - center[:, None]) * inv_root[:, None]
    normed_all = lax.all_gather(
        (standard * gain_vec + shift_vec).astype(jnp.bfloat16), FEAT, axis=1, tiled=True
    )
    local_width = tokens.shape[1]
    local_heads = local_width // HD
    feat_count = M // feat_parts
    omega_used = lax.dynamic_slice_in_dim(omega, feat_index * feat_count, feat_count, 1)
    weights_used = lax.dynamic_slice_in_dim(qmc_weights, feat_index * feat_count, feat_count, 0)
    row_count = tokens.shape[0] // MB
    qkv_bias_f = qkv_bias.astype(jnp.float32)
    up_bias_f = up_bias.astype(jnp.float32)
    out_bias_f = out_bias.astype(jnp.float32)
    block_outs = []
    saved_state = []
    for micro_idx in range(MB):
        offset = micro_idx * row_count
        normed_rows = normed_all[offset : offset + row_count]
        segment, positions = row_layout(doc_lengths[micro_idx], row_count)
        masks = block_masks(segment)
        projected = (
            jnp.einsum("rd,dcf->rcf", normed_rows, qkv_full, preferred_element_type=jnp.float32)
            + qkv_bias_f
        ).astype(jnp.bfloat16)
        pre_act = jnp.dot(normed_rows, up_full, preferred_element_type=jnp.float32) + up_bias_f
        hidden = gelu_exact(pre_act).astype(jnp.bfloat16)
        projected_used = lax.all_gather(projected, FEAT, axis=2, tiled=True)
        heads_used = projected_used.shape[2] // HD
        heads_view = projected_used.astype(jnp.float32).reshape(row_count, 3, heads_used, HD)
        queries = heads_view[:, 0]
        keys_raw = heads_view[:, 1]
        query_map, key_map = both_maps(queries, keys_raw, positions, omega_used, weights_used)
        query_feat = query_map.astype(jnp.bfloat16).astype(jnp.float32)
        key_feat = key_map.astype(jnp.bfloat16).astype(jnp.float32)
        extended = jnp.concatenate(
            [heads_view[:, 2], jnp.ones((row_count, heads_used, 1), jnp.float32)], 2
        )
        mixed = attend(query_feat, key_feat, extended, masks)
        numerator = mixed[..., :HD]
        denominator = mixed[..., HD]
        numerator, denominator = (
            lax.psum_scatter(numerator, FEAT, scatter_dimension=1, tiled=True),
            lax.psum_scatter(denominator, FEAT, scatter_dimension=1, tiled=True),
        )
        attended = (
            (numerator / denominator[..., None])
            .reshape(row_count, local_width)
            .astype(jnp.bfloat16)
        )
        branch = jnp.dot(attended, out_rows, preferred_element_type=jnp.float32)
        branch = branch + jnp.dot(hidden, down_rows, preferred_element_type=jnp.float32)
        summed = lax.psum_scatter(
            branch.astype(jnp.bfloat16), FEAT, scatter_dimension=1, tiled=True
        ).astype(jnp.float32)
        block_outs.append(
            (inputs[offset : offset + row_count] + summed + out_bias_f).astype(jnp.bfloat16)
        )
        saved_state.append(
            (
                normed_rows,
                positions,
                masks,
                pre_act,
                hidden,
                queries,
                keys_raw,
                extended,
                query_feat,
                key_feat,
                numerator,
                denominator,
                attended,
            )
        )
    qkv_acc = jnp.zeros(qkv_full.shape, jnp.float32)
    up_acc = jnp.zeros(up_full.shape, jnp.float32)
    outw_acc = jnp.zeros(out_rows.shape, jnp.float32)
    down_acc = jnp.zeros(down_rows.shape, jnp.float32)
    qkv_bias_acc = jnp.zeros((3, local_width), jnp.float32)
    up_bias_acc = jnp.zeros((up_full.shape[1],), jnp.float32)
    normed_grads = []
    for micro_idx in range(MB):
        offset = micro_idx * row_count
        (
            normed_rows,
            positions,
            masks,
            pre_act,
            hidden,
            queries,
            keys_raw,
            extended,
            query_feat,
            key_feat,
            numerator,
            denominator,
            attended,
        ) = saved_state[micro_idx]
        cotangent = lax.all_gather(
            out_grad[offset : offset + row_count], FEAT, axis=1, tiled=True
        )
        outw_acc = outw_acc + jnp.einsum(
            "rk,rd->kd", attended, cotangent, preferred_element_type=jnp.float32
        )
        down_acc = down_acc + jnp.einsum(
            "rk,rd->kd", hidden, cotangent, preferred_element_type=jnp.float32
        )
        att_grad = jnp.einsum("rd,kd->rk", cotangent, out_rows, preferred_element_type=jnp.float32)
        hidden_grad = jnp.einsum(
            "rd,kd->rk", cotangent, down_rows, preferred_element_type=jnp.float32
        )
        _, gelu_pull = jax.vjp(gelu_exact, pre_act)
        pre_grad = gelu_pull(hidden_grad)[0].astype(jnp.bfloat16)
        up_acc = up_acc + jnp.einsum(
            "rd,rk->dk", normed_rows, pre_grad, preferred_element_type=jnp.float32
        )
        up_bias_acc = up_bias_acc + jnp.sum(pre_grad.astype(jnp.float32), 0)
        att_grad = att_grad.reshape(row_count, local_heads, HD)
        numer_grad = (att_grad / denominator[..., None]).astype(jnp.bfloat16)
        denom_grad = (-jnp.sum(att_grad * numerator, 2) / (denominator * denominator)).astype(
            jnp.bfloat16
        )
        numer_grad, denom_grad = (
            lax.all_gather(numer_grad, FEAT, axis=1, tiled=True),
            lax.all_gather(denom_grad, FEAT, axis=1, tiled=True),
        )
        upstream = jnp.concatenate(
            [numer_grad.astype(jnp.float32), denom_grad.astype(jnp.float32)[..., None]], 2
        )
        query_feat_grad, key_feat_grad, extended_grad = attend_back(
            query_feat, key_feat, extended, masks, upstream
        )

        def map_local(query_in, key_in):
            return both_maps(query_in, key_in, positions, omega_used, weights_used)

        _, map_pull = jax.vjp(map_local, queries, keys_raw)
        query_grad, key_grad = map_pull((query_feat_grad, key_feat_grad))
        proj_rows = jnp.stack([query_grad, key_grad, extended_grad[..., :HD]], 1).reshape(
            row_count, 3, -1
        )
        proj_rows = lax.psum_scatter(proj_rows, FEAT, scatter_dimension=2, tiled=True)
        proj_grad = proj_rows.astype(jnp.bfloat16)
        qkv_acc = qkv_acc + jnp.einsum(
            "rd,rcf->dcf", normed_rows, proj_grad, preferred_element_type=jnp.float32
        )
        qkv_bias_acc = qkv_bias_acc + jnp.sum(proj_grad.astype(jnp.float32), 0)
        normed_part = jnp.einsum(
            "rcf,dcf->rd", proj_grad, qkv_full, preferred_element_type=jnp.float32
        )
        normed_part = normed_part + jnp.einsum(
            "rk,dk->rd", pre_grad, up_full, preferred_element_type=jnp.float32
        )
        normed_grads.append(
            lax.psum_scatter(
                normed_part.astype(jnp.bfloat16), FEAT, scatter_dimension=1, tiled=True
            ).astype(jnp.float32)
        )
    normed_grad = jnp.concatenate(normed_grads, 0)
    scaled = normed_grad * gain_vec
    grad_sums = lax.psum((jnp.sum(scaled, 1), jnp.sum(scaled * standard, 1)), FEAT)
    out_grad_f = out_grad.astype(jnp.float32)
    input_grad = out_grad_f + inv_root[:, None] * (
        scaled - grad_sums[0][:, None] / D - standard * grad_sums[1][:, None] / D
    )
    gain_part = jnp.sum(normed_grad * standard, 0)
    shift_part = jnp.sum(normed_grad, 0)
    out_bias_part = jnp.sum(out_grad_f, 0)
    qkv_grad, up_grad, outw_grad, down_grad = (
        lax.psum_scatter(
            qkv_acc.astype(jnp.bfloat16), DP, scatter_dimension=0, tiled=True
        ).astype(jnp.float32),
        lax.psum_scatter(up_acc.astype(jnp.bfloat16), DP, scatter_dimension=0, tiled=True).astype(
            jnp.float32
        ),
        lax.psum_scatter(
            outw_acc.astype(jnp.bfloat16), DP, scatter_dimension=1, tiled=True
        ).astype(jnp.float32),
        lax.psum_scatter(
            down_acc.astype(jnp.bfloat16), DP, scatter_dimension=1, tiled=True
        ).astype(jnp.float32),
    )
    gain_grad, shift_grad, qkv_bias_grad, out_bias_grad, up_bias_grad = lax.psum(
        (gain_part, shift_part, qkv_bias_acc, out_bias_part, up_bias_acc), DP
    )
    return (
        jnp.concatenate(block_outs, 0),
        input_grad.astype(jnp.bfloat16),
        gain_grad,
        shift_grad,
        qkv_grad,
        qkv_bias_grad,
        outw_grad,
        out_bias_grad,
        up_grad,
        up_bias_grad,
        down_grad,
    )


MESH = pl.DeviceIdType.MESH
f32, bf16 = jnp.float32, jnp.bfloat16
NT = ((1,), (1,))
TN = ((0,), (0,))
EXTRA = 16


def dot(a, b, dims=((1,), (0,)), precision=None):
    return lax.dot_general(
        a, b, (dims, ((), ())), precision=precision, preferred_element_type=f32
    )


def rotary_table(longest):
    half_rot = ROT // 2
    inv_freq = np.exp(
        -np.arange(half_rot, dtype=np.float32)
        * np.float32(2.0 / ROT)
        * np.float32(math.log(10000.0))
    ).astype(np.float32)
    angles = np.arange(longest, dtype=np.float32)[:, None] * inv_freq[None, :]
    cosine = np.ones((longest, HD), np.float32)
    sine = np.zeros((longest, HD), np.float32)
    for part in range(2):
        cosine[:, part * half_rot : (part + 1) * half_rot] = np.cos(angles)
        sine[:, part * half_rot : (part + 1) * half_rot] = np.sin(angles)
    rest = np.concatenate([cosine, cosine, sine, sine], 1).astype(np.float32)
    terms = []
    for _ in range(3):
        term = rest.astype(ml_dtypes.bfloat16)
        terms.append(term)
        rest = rest - term.astype(np.float32)
    return np.concatenate(terms, 0)


def rotary_swap():
    half_rot = ROT // 2
    one = np.zeros((HD, HD), np.float32)
    for i in range(half_rot):
        one[i + half_rot, i] = -1.0
        one[i, i + half_rot] = 1.0
    return np.kron(np.eye(4, dtype=np.float32), one).astype(ml_dtypes.bfloat16)


def dct_rows():
    ramp = np.arange(HD, dtype=np.float32)
    scale = np.where(ramp == 0.0, np.sqrt(1.0 / HD), np.sqrt(2.0 / HD))
    table = np.cos(math.pi * (2.0 * ramp[None, :] + 1.0) * ramp[:, None] / (2.0 * HD)) * scale[:, None]
    return np.tile(table.T, (4, 1)).astype(np.float32)


class Sizes:
    def __init__(self, rows, width, hidden, dp_count, feat_count):
        self.rows = rows
        self.width = width
        self.model = width * feat_count
        self.span = rows // MB
        self.total = 2 * rows
        self.micro = 2 * MB
        self.half = width // 2
        self.hidden = hidden // 2
        self.block = self.model // dp_count
        self.planes = dp_count // 2


def scratch_list(s):
    pl_, bl, hf, hd, tt, md = s.planes, s.block, s.half, s.hidden, s.total, s.model
    grads = {
        QKV: (3, bl, hf),
        OUT: (hf, bl),
        UP: (bl, hd),
        DOWN: (hd, bl),
    }
    shapes = dict(
        XG=((2, s.rows + EXTRA, md), bf16),
        G=((tt, md), bf16),
        WQ=((3, md, hf), bf16),
        WU=((md, hd), bf16),
        WO=((hf, md), bf16),
        WD=((hd, md), bf16),
        NB=((tt, md), bf16),
        MU=((tt, 1), f32),
        IV=((tt, 1), f32),
        A2=((2 * s.width // 2, s.width), f32),
        WB=((tt, 2 * hf), bf16),
        VB=((tt, hf), bf16),
        PHF=((tt, 2 * hf), f32),
        PHB=((tt, 2 * hf), bf16),
        ROTV=((tt, 2 * hf), f32),
        CSB=((tt, 2 * hf), f32),
        SB=((s.micro, 2, s.span, s.span), bf16),
        ND=((tt, 2 * hf), f32),
        AT=((tt, hf), bf16),
        PG=((tt, 3 * hf), bf16),
        HB=((tt, hd), bf16),
        GP=((tt, hd), f32),
        PRE=((tt, hd), bf16),
        QBG=((1, 3 * hf), f32),
        UBG=((1, hd), f32),
        NGF=((s.rows, s.width), f32),
        ST=((16, s.rows), f32),
        STR=((3, 16, s.rows), f32),
        SV=((24, 128), f32),
        SMALL=((3, max(2 * hd, 4 * s.width)), f32),
        IN_lens=((MB, SEQS), jnp.int32),
        IN_gain=((s.width,), bf16),
        IN_shift=((s.width,), bf16),
        IN_qkv_bias=((3, s.width), bf16),
        IN_out_bias=((s.width,), bf16),
        IN_up_bias=((2 * hd,), bf16),
        IN_qmc=((M,), f32),
        IN_tab=((3 * (s.span // 2), 2 * hf), bf16),
        IN_swap=((2 * hf, 2 * hf), bf16),
        IN_ones16=((2 * hf, 2 * hf), bf16),
        IN_dct=((2 * hf, HD), f32),
        IN_rep=((HD, 2 * hf), f32),
        IN_omega=((HD, M), f32),
        SVR=((7, 24, 128), f32),
    )
    for name, shape in grads.items():
        shapes["SX" + name] = ((pl_,) + shape, bf16)
        shapes["RX" + name] = ((pl_,) + shape, bf16)
        shapes["KX" + name] = ((pl_,) + shape, f32)
        shapes["ZS" + name] = ((3,) + shape, bf16)
        shapes["ZR" + name] = ((3,) + shape, bf16)
        shapes["ZM" + name] = (shape, bf16)
    for name in (BLK, NRM):
        shapes["CS" + name] = ((tt, 2 * s.width), bf16)
        shapes["CR" + name] = ((tt, 2 * s.width), bf16)
        shapes["KC" + name] = ((tt, 2 * s.width), f32)
        shapes["KY" + name] = ((tt, s.width), f32)
        shapes["YS" + name] = ((tt, s.width), bf16)
        shapes["YR" + name] = ((tt, s.width), bf16)
        shapes["AS" + name] = ((s.rows, s.width), bf16)
        shapes["AR" + name] = ((s.rows, s.width), bf16)
    return shapes


SMALL = ("lens", "gain", "shift", "qkv_bias", "out_bias", "up_bias", "qmc", "tab", "swap", "ones16", "dct", "rep", "omega")
N_LOCAL = 6 + len(SMALL)
N_REMOTE = 120


def fused_kernel(s, names, *refs):
    (tok, grd, wq_in, wu_in, wo_in, wd_in) = refs[:6]
    small_in = refs[6 : 6 + len(SMALL)]
    o_blk, o_inp, o_qkv, o_up, o_out, o_down, o_small = refs[6 + len(SMALL) : 13 + len(SMALL)]
    m_ = dict(zip(names, refs[13 + len(SMALL) :]))
    small, tab, swap, ones16 = m_["SMALL"], m_["IN_tab"], m_["IN_swap"], m_["IN_ones16"]
    dct, rep, omega = m_["IN_dct"], m_["IN_rep"], m_["IN_omega"]
    lsem, ssem, rsem = m_["lsem"], m_["ssem"], m_["rsem"]
    XG, G, WQ, WU, WO, WD = (m_[k] for k in ("XG", "G", "WQ", "WU", "WO", "WD"))
    NB, MU, IV = m_["NB"], m_["MU"], m_["IV"]

    dp = lax.axis_index(DP)
    ft = lax.axis_index(FEAT)
    z, x = dp // 2, dp % 2
    zl = z % 2
    y, c = ft // 2, ft % 2
    zd = (z, z + 1 - 2 * zl, (z + 2) % 4, 3 - z)
    hl = (zl, 1 - zl, zl, 1 - zl)
    inner = zl != z // 2

    def partner(d):
        if isinstance(d, int):
            return zd[d]
        return (z // 2 + d // 2) % 2 * 2 + (z + d) % 2

    counter = [0]

    def new(n=1):
        counter[0] += n
        return counter[0] - n

    def device(d=0, fx=False, fy=False, fc=False):
        return {
            DP: partner(d) * 2 + (1 - x if fx else x),
            FEAT: (1 - y if fy else y) * 2 + (1 - c if fc else c),
        }

    def send(src, dst, sem, where, arrival=None):
        copy = pltpu.make_async_remote_copy(
            src_ref=src,
            dst_ref=dst,
            send_sem=ssem.at[sem],
            recv_sem=rsem.at[sem if arrival is None else arrival],
            device_id=where,
            device_id_type=MESH,
        )
        return copy

    def go(src, dst, sem, where):
        send(src, dst, sem, where).start()

    def arrived(ref, sem, where):
        send(ref, ref, sem, where).wait_recv()

    mo = pl.multiple_of

    def lanes(index, size):
        return pl.ds(mo(index * size, size), size)

    def tok_at(b, f):
        return XG.at[b, :, lanes(f, s.width)]

    def grd_at(b, f):
        return G.at[lanes(b, s.rows), lanes(f, s.width)]

    def own_half(w, h):
        if w == QKV:
            return wq_in.at[:, :, lanes(h, s.half)]
        if w == UP:
            return wu_in.at[:, lanes(h, s.hidden)]
        if w == OUT:
            return wo_in.at[lanes(h, s.half), :]
        return wd_in.at[lanes(h, s.hidden), :]

    def weight_at(w, block):
        if w == QKV:
            return WQ.at[:, lanes(block, s.block), :]
        if w == UP:
            return WU.at[lanes(block, s.block), :]
        if w == OUT:
            return WO.at[:, lanes(block, s.block)]
        return WD.at[:, lanes(block, s.block)]

    ws = (QKV, OUT, UP, DOWN)

    local = [
        pltpu.make_async_copy(tok, XG.at[zl, pl.ds(0, s.rows), lanes(ft, s.width)], lsem.at[0]),
        pltpu.make_async_copy(grd, grd_at(zl, ft), lsem.at[1]),
    ]
    for i, w in enumerate(ws):
        local.append(pltpu.make_async_copy(own_half(w, zl), weight_at(w, dp), lsem.at[2 + i]))
    for i, name in enumerate(SMALL):
        local.append(pltpu.make_async_copy(small_in[i], m_["IN_" + name], lsem.at[6 + i]))
    for copy in local:
        copy.start()

    barrier = pltpu.get_barrier_semaphore()
    partners = [device(d) for d in (1, 2, 3)] + [device(d, fx=True) for d in (0, 1, 2, 3)]
    partners += [device(fy=True), device(fc=True), device(fy=True, fc=True)]
    for where in partners:
        pl.semaphore_signal(barrier, inc=1, device_id=where, device_id_type=MESH)
    pl.semaphore_wait(barrier, len(partners))
    local_grd, local_weight, local_table = local[1], dict(zip(ws, local[2:6])), local[-6:]
    for copy in local[:1] + local[6:-6]:
        copy.wait()

    def row_of(name):
        value = m_["IN_" + name][...].astype(f32)
        return value.reshape(1, value.shape[0])

    lens = m_["IN_lens"][...].astype(f32)
    rows = [row_of("gain"), row_of("shift")]
    for i in range(MB):
        for j in range(SEQS):
            rows.append(jnp.broadcast_to(lens[i : i + 1, j : j + 1], (1, s.width)))
    rows.append(jnp.zeros((EXTRA - len(rows), s.width), f32))
    XG[zl, s.rows : s.rows + EXTRA, lanes(ft, s.width)] = jnp.concatenate(rows, 0).astype(bf16)
    small[0:1, 0 : 2 * s.hidden] = row_of("up_bias")
    for k in range(3):
        small[1:2, k * s.width : (k + 1) * s.width] = m_["IN_qkv_bias"][k : k + 1, :].astype(f32)
    small[1:2, 3 * s.width : 4 * s.width] = row_of("out_bias")
    qmc = row_of("qmc")
    small[2:3, 0 : 2 * s.half] = jnp.concatenate([qmc, qmc, jnp.ones((1, s.half), f32)], 1)

    sem_act = {TOK: new(7), GRD: new(7)}

    def act_own(name, at, axis):
        k, where = {"c": (0, device(fc=True)), "y": (1, device(fy=True)), "z": (2, device(1))}[axis]
        go(at(zl, ft) if name == TOK else grd, at(zl, ft), sem_act[name] + k, where)

    def act_arrive(name, at, k):
        base = sem_act[name]
        fy = (1 - y) * 2 + c
        zb = 1 - zl
        if k == 0:
            arrived(at(zb, ft), base + 2, device(1))
            go(at(zb, ft), at(zb, ft), base + 3, device(fy=True))
            go(at(zb, ft), at(zb, ft), base + 4, device(fc=True))
        elif k == 1:
            arrived(at(zl, fy), base + 1, device(fy=True))
            go(at(zl, fy), at(zl, fy), base + 5, device(fc=True))
        else:
            arrived(at(zb, fy), base + 3, device(fy=True))
            go(at(zb, fy), at(zb, fy), base + 6, device(fc=True))

    def act_rest(name, at):
        base = sem_act[name]
        if name == GRD:
            local_grd.wait()
        fc = y * 2 + 1 - c
        fyc = (1 - y) * 2 + 1 - c
        for k, b, f in ((0, zl, fc), (4, 1 - zl, fc), (5, zl, fyc), (6, 1 - zl, fyc)):
            arrived(at(b, f), base + k, device(fc=True))

    def act_gathered(name, at):
        base = sem_act[name]
        fy = (1 - y) * 2 + c
        zb = 1 - zl
        to_c, to_y = device(fc=True), device(fy=True)
        for k, b, f, where in (
            (0, zl, ft, to_c),
            (1, zl, ft, to_y),
            (2, zl, ft, device(1)),
            (3, zb, ft, to_y),
            (4, zb, ft, to_c),
            (5, zl, fy, to_c),
            (6, zb, fy, to_c),
        ):
            send(at(b, f), at(b, f), base + k, where).wait_send()

    sem_z = {w: new(3) for w in ws}
    sem_x = {w: new(4) for w in ws}
    sem_r = {w: new() for w in ws}
    sem_m = {w: new() for w in ws}

    waited = set()

    def w_z(w, d):
        def start():
            go(own_half(w, hl[d]), weight_at(w, dp), sem_z[w] + d - 1, device(d))

        if d == 3:
            pl.when(inner)(start)
        else:
            start()

    def w_near(w):
        at = weight_at(w, zd[1] * 2 + x)
        arrived(at, sem_z[w], device(1))

    def relay(w):
        at = weight_at(w, zd[1] * 2 + x)
        return send(at, at, sem_r[w], device(2), sem_z[w] + 2)

    def w_relay(w):
        first = w not in waited
        waited.add(w)

        @pl.when(inner)
        def _():
            if first:
                w_near(w)
            relay(w).start()

    def w_own(w):
        go(own_half(w, zl), weight_at(w, dp), sem_x[w], device(fx=True))

    def w_forward(w, d):
        at = weight_at(w, partner(d) * 2 + x)
        if d > 1:
            arrived(at, sem_z[w] + d - 1, device(d))
        elif w in waited:
            pl.when(jnp.logical_not(inner))(lambda: w_near(w))
        else:
            waited.add(w)
            w_near(w)
        go(at, at, sem_x[w] + d, device(fx=True))

    def w_sent(w):
        for d in range(4):
            at = weight_at(w, zd[d] * 2 + x)
            send(at, at, sem_x[w] + d, device(fx=True)).wait_send()
            if d in (1, 2):
                send(own_half(w, hl[d]), weight_at(w, dp), sem_z[w] + d - 1, device(d)).wait_send()

        @pl.when(inner)
        def _():
            send(own_half(w, hl[3]), weight_at(w, dp), sem_z[w] + 2, device(3)).wait_send()
            relay(w).wait_send()

    def w_rest(w):
        local_weight[w].wait()
        for d in range(4):
            arrived(weight_at(w, zd[d] * 2 + 1 - x), sem_x[w] + d, device(fx=True))

    sem_gx = {w: new(4) for w in ws}
    sem_gz = {w: new(3) for w in ws}

    def put_grad(w, zp, mine, theirs):
        m_["KX" + w][zp] = mine
        m_["SX" + w][zp] = theirs.astype(bf16)
        src, dst = m_["SX" + w].at[zp], m_["RX" + w].at[zp]
        send(src, dst, sem_gx[w] + zp, device(fx=True)).start()

    def grad_copy(w, d):
        return send(m_["ZS" + w].at[d - 1], m_["ZR" + w].at[d - 1], sem_gz[w] + d - 1, device(d))

    def grad_pass(w):
        return send(m_["ZS" + w].at[2], m_["ZM" + w], sem_m[w], device(2))

    def grad_z(w, d):
        zp = zd[d]
        arrived(m_["RX" + w].at[zp], sem_gx[w] + zp, device(fx=True))
        both = m_["KX" + w][zp] + m_["RX" + w][zp].astype(f32)
        if d == 0:
            m_["KX" + w][zp] = both
            return
        if d == 1:

            @pl.when(inner)
            def _():
                arrived(m_["ZM" + w], sem_m[w], device(2))
                m_["ZS" + w][0] = (both + m_["ZM" + w][...].astype(f32)).astype(bf16)

            @pl.when(jnp.logical_not(inner))
            def _():
                m_["ZS" + w][0] = both.astype(bf16)

        else:
            m_["ZS" + w][d - 1] = both.astype(bf16)
        if d < 3:
            grad_copy(w, d).start()
        else:
            pl.when(inner)(lambda: grad_copy(w, 3).start())
            pl.when(jnp.logical_not(inner))(lambda: grad_pass(w).start())

    def grad_last(w):
        for d in (1, 2):
            arrived(m_["ZR" + w].at[d - 1], sem_gz[w] + d - 1, device(d))
        got = m_["ZR" + w]
        same = m_["KX" + w][z] + got[1].astype(f32)
        other = got[0].astype(f32)
        def put(half, value):
            if w == QKV:
                o_qkv[:, :, lanes(half, s.half)] = value
            elif w == UP:
                o_up[:, lanes(half, s.hidden)] = value
            elif w == OUT:
                o_out[lanes(half, s.half), :] = value
            else:
                o_down[lanes(half, s.hidden), :] = value

        put(zl, same)

        @pl.when(inner)
        def _():
            arrived(m_["ZR" + w].at[2], sem_gz[w] + 2, device(3))
            put(1 - zl, other + got[2].astype(f32))

        pl.when(jnp.logical_not(inner))(lambda: put(1 - zl, other))

    def grad_sent(w):
        for zp in range(4):
            send(m_["SX" + w].at[zp], m_["RX" + w].at[zp], sem_gx[w] + zp, device(fx=True)).wait_send()
        for d in (1, 2):
            grad_copy(w, d).wait_send()
        pl.when(inner)(lambda: grad_copy(w, 3).wait_send())
        pl.when(jnp.logical_not(inner))(lambda: grad_pass(w).wait_send())

    def pick(flag, a, b):
        return jnp.where(flag == 0, a, b)

    def halves(value, axis):
        n = value.shape[axis] // 2
        lo, hi = lax.slice_in_dim(value, 0, n, axis=axis), lax.slice_in_dim(value, n, 2 * n, axis=axis)
        return pick(x, lo, hi), pick(x, hi, lo)

    sem_c = {k: new(4) for k in (BLK, NRM)}
    sem_y = {k: new(4) for k in (BLK, NRM)}
    sem_a = {k: new(2) for k in (BLK, NRM)}

    def rows_of(i):
        block = (1 - zl) + (i // MB) * (2 * zl - 1)
        return pl.ds(mo(block * s.rows + (i % MB) * s.span, s.span), s.span)

    def act_put(name, i, value):
        r = rows_of(i)
        w_ = s.width
        v = [value[:, k * w_ : (k + 1) * w_] for k in range(4)]
        m_["KC" + name][r, 0:w_] = pick(c, v[0], v[1])
        m_["KC" + name][r, w_ : 2 * w_] = pick(c, v[2], v[3])
        m_["CS" + name][r, 0:w_] = pick(c, v[1], v[0]).astype(bf16)
        m_["CS" + name][r, w_ : 2 * w_] = pick(c, v[3], v[2]).astype(bf16)
        send(m_["CS" + name].at[r], m_["CR" + name].at[r], sem_c[name] + i, device(fc=True)).start()

    def act_y(name, i):
        r = rows_of(i)
        w_ = s.width
        arrived(m_["CR" + name].at[r], sem_c[name] + i, device(fc=True))
        both = m_["KC" + name][r, :] + m_["CR" + name][r, :].astype(f32)
        lo, hi = both[:, :w_], both[:, w_:]
        m_["KY" + name][r, :] = pick(y, lo, hi)
        m_["YS" + name][r, :] = pick(y, hi, lo).astype(bf16)
        send(m_["YS" + name].at[r], m_["YR" + name].at[r], sem_y[name] + i, device(fy=True)).start()

    def act_z(name, i):
        r = rows_of(i)
        q = pl.ds(i * s.span, s.span)
        arrived(m_["YR" + name].at[r], sem_y[name] + i, device(fy=True))
        both = m_["KY" + name][r, :] + m_["YR" + name][r, :].astype(f32)
        m_["AS" + name][q, :] = both.astype(bf16)
        go(m_["AS" + name].at[q], m_["AR" + name].at[q], sem_a[name] + i, device(1))

    def act_last(name, i):
        r = rows_of(MB + i)
        q = pl.ds(i * s.span, s.span)
        arrived(m_["YR" + name].at[r], sem_y[name] + MB + i, device(fy=True))
        arrived(m_["AR" + name].at[q], sem_a[name] + i, device(1))
        return (
            m_["KY" + name][r, :]
            + m_["YR" + name][r, :].astype(f32)
            + m_["AR" + name][q, :].astype(f32)
        )

    def act_sent(name):
        for i in range(4):
            r = rows_of(i)
            send(m_["CS" + name].at[r], m_["CR" + name].at[r], sem_c[name] + i, device(fc=True)).wait_send()
            send(m_["YS" + name].at[r], m_["YR" + name].at[r], sem_y[name] + i, device(fy=True)).wait_send()
        for i in range(MB):
            q = pl.ds(i * s.span, s.span)
            send(m_["AS" + name].at[q], m_["AR" + name].at[q], sem_a[name] + i, device(1)).wait_send()

    def beside(*steps):
        def side(i):
            for at in sorted(set(step[0] for step in steps)):

                @pl.when(i == at)
                def _():
                    for when, do, *args in steps:
                        if when == at:
                            do(*args)

        return side

    def loop(n, body, side=None):
        def step(i, carry):
            if side is not None:
                side(i)
            body(i)
            return carry

        lax.fori_loop(0, n, step, 0)

    def at_micro(m):
        return pl.ds(mo(m * s.span, s.span), s.span)

    def norm_phase(side=None):
        extra = XG[0, s.rows : s.rows + EXTRA, :].astype(f32)
        gain, shift = extra[0:1], extra[1:2]

        def body(m):
            xv = XG[m // MB, pl.ds(mo((m % MB) * s.span, s.span), s.span), :].astype(f32)
            mu = jnp.sum(xv, 1, keepdims=True) * (1.0 / s.model)
            var = jnp.sum(xv * xv, 1, keepdims=True) * (1.0 / s.model) - mu * mu
            inv = lax.rsqrt(var + epsilon)
            r = at_micro(m)
            MU[r, :] = mu
            IV[r, :] = inv
            NB[r, :] = ((xv - mu) * inv * gain + shift).astype(bf16)

        loop(s.micro, body, side)

    def masks(m):
        extra = XG[m // MB, s.rows : s.rows + EXTRA, 0 : s.span].astype(f32)
        row_id = lax.broadcasted_iota(jnp.int32, extra.shape, 0)
        first = 2 + SEQS * (m % MB)

        def length(k):
            return jnp.sum(jnp.where(row_id == first + k, extra, 0.0), 0, keepdims=True)

        end0 = length(0)
        end1 = end0 + length(1)
        t = lax.broadcasted_iota(jnp.int32, (s.span, s.span), 0).astype(f32)
        u = lax.broadcasted_iota(jnp.int32, (s.span, s.span), 1).astype(f32)
        start = jnp.where(t >= end1, end1, jnp.where(t >= end0, end0, 0.0))
        return jnp.logical_and(u <= t, u >= start), t, u, start

    def head_rows():
        lane = lax.broadcasted_iota(jnp.int32, (1, s.half), 1)
        return [jnp.where(lane // HD == h, 1.0, 0.0).astype(bf16) for h in range(2)], [
            jnp.where(lane == h * HD, 1.0, 0.0).astype(bf16) for h in range(2)
        ]

    HIGH = lax.Precision.HIGH
    HIGHEST = lax.Precision.HIGHEST
    hf = s.half

    def table_phase():
        for copy in local_table:
            copy.wait()
        wide = dot(dot(dct[...], omega[...], precision=HIGHEST), rep[...], precision=HIGHEST)
        m_["A2"][...] = wide * (ones16[...].astype(f32) * (16.0 * HD ** (-0.25)))

    def fwd_phase(side=None):
        def body(m):
            r = at_micro(m)
            wq = jnp.concatenate([WQ[0], WQ[1], WQ[2]], 1)
            bias = jnp.concatenate(
                [small[1:2, pl.ds(mo(k * s.width + zl * hf, hf), hf)] for k in range(3)], 1
            )
            p = (dot(NB[r, :], wq) + bias).astype(bf16)
            w, v = p[:, : 2 * hf], p[:, 2 * hf :]
            m_["VB"][r, :] = v
            mask, t, u, start = masks(m)
            pos = t[:, :hf] - start[:, :hf]
            hot = jnp.where(pos == u[:, :hf], 1.0, 0.0).astype(bf16)
            cs = dot(jnp.concatenate([hot, hot, hot], 1), tab[...])
            m_["CSB"][r, :] = cs
            cc = jnp.concatenate([cs[:, :hf], cs[:, :hf]], 1)
            ss = jnp.concatenate([cs[:, hf:], cs[:, hf:]], 1)
            wf = w.astype(f32)
            rot = wf * cc + dot(w, swap[...]) * ss
            m_["ROTV"][r, :] = rot
            score = dot(rot, m_["A2"][...], precision=HIGH)
            norm2 = dot(wf * wf, ones16[...].astype(f32), precision=HIGH)
            ph = jnp.exp(score - norm2) * small[2:3, 0 : 2 * hf]
            m_["PHF"][r, :] = ph
            pb = ph.astype(bf16)
            m_["PHB"][r, :] = pb
            hm, _ = head_rows()
            acc = jnp.zeros((s.span, 2 * hf), f32)
            for h in range(2):
                sc = dot(pb[:, :hf] * hm[h], pb[:, hf:], NT)
                sm = jnp.where(mask, sc, 0.0).astype(bf16)
                m_["SB"][m, h] = sm
                rhs = jnp.concatenate([v * hm[h], jnp.broadcast_to(hm[h], v.shape)], 1)
                acc = acc + dot(sm, rhs)
            m_["ND"][r, :] = acc
            m_["AT"][r, :] = (acc[:, :hf] / acc[:, hf:]).astype(bf16)

        loop(s.micro, body, side)

    def bwd_phase(side=None):
        m_["QBG"][...] = jnp.zeros_like(m_["QBG"])

        def body(m):
            r = at_micro(m)
            mask = masks(m)[0]
            hm, hot = head_rows()
            ag = dot(G[r, :], WO[...], NT)
            nd = m_["ND"][r, :]
            num, den = nd[:, :hf], nd[:, hf:]
            ng = (ag / den).astype(bf16)
            sums = dot(ag * num, ones16[0:hf, 0:hf].astype(f32), precision=HIGH) * 16.0
            dg = (-sums / (den * den)).astype(bf16)
            v = m_["VB"][r, :]
            pb = m_["PHB"][r, :]
            v1 = jnp.concatenate([v, jnp.ones(v.shape, bf16)], 1)
            dq = dk = dv = jnp.zeros((s.span, hf), f32)
            for h in range(2):
                e = dot(jnp.concatenate([ng * hm[h], dg * hot[h]], 1), v1, NT)
                em = jnp.where(mask, e, 0.0).astype(bf16)
                dq = dq + dot(em, pb[:, hf:] * hm[h])
                dk = dk + dot(em, pb[:, :hf] * hm[h], TN)
                dv = dv + dot(m_["SB"][m, h], ng * hm[h], TN)
            dph = jnp.concatenate([dq, dk], 1) * m_["PHF"][r, :]
            rot = m_["ROTV"][r, :]
            both = dot(dph, ones16[...].astype(f32), precision=HIGH) * 2.0
            drot = dot(dph, m_["A2"][...], NT, precision=HIGH) - rot * both
            cs = m_["CSB"][r, :]
            cc = jnp.concatenate([cs[:, :hf], cs[:, :hf]], 1)
            ss = jnp.concatenate([cs[:, hf:], cs[:, hf:]], 1)
            dw = drot * cc + dot(drot * ss, swap[...].astype(f32), NT, precision=HIGH)
            pg = jnp.concatenate([dw, dv], 1).astype(bf16)
            m_["PG"][r, :] = pg
            m_["QBG"][...] += jnp.sum(pg.astype(f32), 0, keepdims=True)

        loop(s.micro, body, side)

    def up_phase(side=None):
        bias = small[0:1, lanes(zl, s.hidden)]

        def body(m):
            r = at_micro(m)
            pre = dot(NB[r, :], WU[...]) + bias
            cdf = 0.5 * (1.0 + lax.erf(pre * math.sqrt(0.5)))
            m_["HB"][r, :] = (pre * cdf).astype(bf16)
            m_["GP"][r, :] = cdf + pre * jnp.exp(-0.5 * pre * pre) * (1.0 / math.sqrt(2.0 * math.pi))

        loop(s.micro, body, side)

    def pre_phase(side=None):
        m_["UBG"][...] = jnp.zeros_like(m_["UBG"])

        def body(m):
            r = at_micro(m)
            pre = (dot(G[r, :], WD[...], NT) * m_["GP"][r, :]).astype(bf16)
            m_["PRE"][r, :] = pre
            m_["UBG"][...] += jnp.sum(pre.astype(f32), 0, keepdims=True)

        loop(s.micro, body, side)

    def nrm_phase(side=None):
        def body(i):
            r = rows_of(i)
            wq = jnp.concatenate([WQ[0], WQ[1], WQ[2]], 1)
            act_put(NRM, i, dot(m_["PG"][r, :], wq, NT) + dot(m_["PRE"][r, :], WU[...], NT))

        loop(4, body, side)

    def blk_phase(side=None):
        def body(i):
            r = rows_of(i)
            act_put(BLK, i, dot(m_["AT"][r, :], WO[...]) + dot(m_["HB"][r, :], WD[...]))

        loop(4, body, side)

    two = 2 * s.block

    def grad_phase(w, side=None):
        def body(i):
            zp = partner(3 - i)
            cols = lanes(zp, two)
            if w == QKV:
                value = dot(NB[:, cols], m_["PG"][...], TN)
                mine, theirs = halves(value, 0)
                mine = jnp.stack([mine[:, k * hf : (k + 1) * hf] for k in range(3)], 0)
                theirs = jnp.stack([theirs[:, k * hf : (k + 1) * hf] for k in range(3)], 0)
            elif w == UP:
                mine, theirs = halves(dot(NB[:, cols], m_["PRE"][...], TN), 0)
            elif w == OUT:
                mine, theirs = halves(dot(m_["AT"][...], G[:, cols], TN), 1)
            else:
                mine, theirs = halves(dot(m_["HB"][...], G[:, cols], TN), 1)
            put_grad(w, zp, mine, theirs)

        loop(s.planes, body, side)

    def out_rows(i):
        return pl.ds(i * s.span, s.span)

    def blk_last():
        for i in range(MB):
            own = XG[zl, i * s.span : (i + 1) * s.span, lanes(ft, s.width)].astype(f32)
            bias = small[1:2, 3 * s.width : 4 * s.width]
            o_blk[out_rows(i), :] = (own + act_last(BLK, i) + bias).astype(bf16)

    sem_st = new(3)
    stat_where = [device(fc=True), device(fy=True), device(fy=True, fc=True)]

    def own_parts():
        extra = XG[0, s.rows : s.rows + EXTRA, lanes(ft, s.width)].astype(f32)
        r = lanes(zl, s.rows)
        own = XG[zl, 0 : s.rows, lanes(ft, s.width)].astype(f32)
        xhat = (own - MU[r, :]) * IV[r, :]
        return extra[0:1], xhat

    def nrm_last():
        for i in range(MB):
            m_["NGF"][out_rows(i), :] = act_last(NRM, i)
        gain, xhat = own_parts()
        ngrad = m_["NGF"][...]
        scaled = ngrad * gain
        ones = jnp.ones((8, s.width), f32)
        m_["ST"][0:8, :] = dot(ones, scaled, NT, precision=HIGHEST)
        m_["ST"][8:16, :] = dot(ones, scaled * xhat, NT, precision=HIGHEST)
        for k, where in enumerate(stat_where):
            go(m_["ST"], m_["STR"].at[k], sem_st + k, where)
        own_g = G[lanes(zl, s.rows), lanes(ft, s.width)].astype(f32)
        rows = [
            jnp.sum(ngrad * xhat, 0, keepdims=True),
            jnp.sum(ngrad, 0, keepdims=True),
            jnp.sum(own_g, 0, keepdims=True),
        ]
        sv = m_["SV"]
        sv[...] = jnp.zeros_like(sv)
        for k, row in enumerate(rows):
            for j in range(2):
                sv[2 * k + j : 2 * k + j + 1, :] = row[:, j * 128 : (j + 1) * 128]
        for k in range(3):
            sv[pl.ds(6 + 2 * k + zl, 1), :] = m_["QBG"][0:1, k * hf : (k + 1) * hf]
        for j in range(s.hidden // 128):
            sv[pl.ds(12 + zl * (s.hidden // 128) + j, 1), :] = m_["UBG"][0:1, j * 128 : (j + 1) * 128]

    sem_sv = new(7)
    sv_where = [device(d) for d in (1, 2, 3)] + [device(d, fx=True) for d in (0, 1, 2, 3)]

    def small_send():
        for k, where in enumerate(sv_where):
            go(m_["SV"], m_["SVR"].at[k], sem_sv + k, where)

    def small_last():
        total = m_["SV"][...]
        for k, where in enumerate(sv_where):
            arrived(m_["SVR"].at[k], sem_sv + k, where)
            total = total + m_["SVR"][k]
        o_small[...] = total

    def input_last():
        total = m_["ST"][...]
        for k, where in enumerate(stat_where):
            arrived(m_["STR"].at[k], sem_st + k, where)
            total = total + m_["STR"][k]
        spread = jnp.full((8, s.width), 1.0 / (8.0 * s.model), f32)
        mean1 = dot(total[0:8, :], spread, TN, precision=HIGHEST)
        mean2 = dot(total[8:16, :], spread, TN, precision=HIGHEST)
        gain, xhat = own_parts()
        own_g = G[lanes(zl, s.rows), lanes(ft, s.width)].astype(f32)
        scaled = m_["NGF"][...] * gain
        inv = IV[lanes(zl, s.rows), :]
        o_inp[...] = (own_g + inv * (scaled - mean1 - xhat * mean2)).astype(bf16)

    w_z(QKV, 3)
    w_z(QKV, 1)
    act_own(GRD, grd_at, "y")
    table_phase()
    w_own(DOWN)
    act_own(TOK, tok_at, "c")
    w_own(QKV)
    act_own(TOK, tok_at, "y")
    w_z(OUT, 3)
    w_own(UP)
    w_z(OUT, 1)
    act_own(TOK, tok_at, "z")
    w_z(UP, 3)
    w_relay(QKV)
    act_own(GRD, grd_at, "z")
    w_forward(OUT, 1)
    w_z(QKV, 2)
    w_z(OUT, 2)
    act_arrive(TOK, tok_at, 0)
    w_z(DOWN, 1)
    act_arrive(TOK, tok_at, 1)
    w_own(OUT)
    w_forward(QKV, 1)
    w_forward(QKV, 3)
    w_forward(QKV, 2)
    act_own(GRD, grd_at, "c")
    act_arrive(TOK, tok_at, 2)
    act_arrive(GRD, grd_at, 0)
    w_z(UP, 1)
    act_rest(TOK, tok_at)
    w_relay(OUT)
    w_forward(OUT, 2)
    w_z(DOWN, 3)
    norm_phase(
        beside(
            (3, w_forward, OUT, 3),
        ),
    )
    w_z(UP, 2)
    w_rest(QKV)
    fwd_phase(
        beside(
            (1, w_forward, DOWN, 1),
            (1, act_arrive, GRD, grd_at, 1),
            (2, w_forward, UP, 1),
            (3, act_arrive, GRD, grd_at, 2),
        ),
    )
    act_rest(GRD, grd_at)
    grad_phase(
        OUT,
        beside(
            (2, w_rest, OUT),
            (2, w_relay, DOWN),
        ),
    )
    w_forward(UP, 2)
    bwd_phase(
        beside(
            (1, w_forward, DOWN, 3),
            (1, w_relay, UP),
            (1, w_z, DOWN, 2),
            (3, w_forward, UP, 3),
        ),
    )
    grad_phase(
        QKV,
        beside(
            (1, w_forward, DOWN, 2),
            (1, grad_z, OUT, 2),
            (2, w_rest, UP),
            (2, grad_z, OUT, 3),
        ),
    )
    up_phase(
        beside(
            (1, grad_z, QKV, 3),
        ),
    )
    grad_z(OUT, 1)
    w_rest(DOWN)
    blk_phase(
        beside(
            (1, grad_z, OUT, 0),
            (3, grad_z, QKV, 2),
        ),
    )
    act_y(BLK, 1)
    grad_phase(
        DOWN,
        beside(
            (1, act_y, BLK, 0),
            (1, grad_last, OUT),
            (2, grad_z, QKV, 1),
        ),
    )
    act_z(BLK, 1)
    pre_phase(
        beside(
            (1, grad_z, DOWN, 3),
            (3, act_z, BLK, 0),
        ),
    )
    nrm_phase(
        beside(
            (2, act_y, NRM, 0),
            (3, grad_z, DOWN, 2),
        ),
    )
    grad_z(QKV, 0)
    grad_z(DOWN, 0)
    act_y(NRM, 1)
    act_z(NRM, 0)
    act_y(NRM, 2)
    grad_phase(
        UP,
        beside(
            (1, act_y, BLK, 3),
            (1, grad_z, DOWN, 1),
            (3, grad_z, UP, 3),
        ),
    )
    act_z(NRM, 1)
    grad_last(DOWN)
    act_y(BLK, 2)
    grad_last(QKV)
    act_y(NRM, 3)
    grad_z(UP, 2)
    grad_z(UP, 0)
    grad_z(UP, 1)
    blk_last()
    nrm_last()
    small_send()
    input_last()
    grad_last(UP)
    small_last()
    act_gathered(TOK, tok_at)
    act_gathered(GRD, grd_at)
    for w in ws:
        w_sent(w)
        grad_sent(w)
    for name in (BLK, NRM):
        act_sent(name)
    for k, where in enumerate(stat_where):
        send(m_["ST"], m_["STR"].at[k], sem_st + k, where).wait_send()
    for k, where in enumerate(sv_where):
        send(m_["SV"], m_["SVR"].at[k], sem_sv + k, where).wait_send()
    assert counter[0] <= N_REMOTE


def finish_kernel(*refs):
    whole, small = refs[:6], refs[6]
    outs, (gain, shift, out_bias, qkv_bias, up_bias) = refs[7:13], refs[13:18]
    sem = refs[18]
    copies = [pltpu.make_async_copy(whole[i], outs[i], sem.at[i]) for i in range(6)]
    for copy in copies:
        copy.start()
    for k, ref in enumerate((gain, shift, out_bias)):
        ref[...] = small[2 * k : 2 * k + 2, :]
    for k in range(3):
        for j in range(2):
            ref = qkv_bias.at[k : k + 1, j * 128 : (j + 1) * 128]
            ref[...] = small[6 + 2 * k + j : 7 + 2 * k + j, :]
    up_bias[...] = small[12 : 12 + up_bias.shape[0], :]
    for copy in copies:
        copy.wait()


def on_device_fused(
    dp_count,
    feat_count,
    tokens,
    doc_lengths,
    norm_gain,
    norm_shift,
    qkv_weight,
    qkv_bias,
    omega,
    qmc_weights,
    out_weight,
    out_bias,
    up_weight,
    up_bias,
    down_weight,
    out_grad,
):
    rows, width = tokens.shape
    s = Sizes(rows, width, up_weight.shape[1], dp_count, feat_count)
    ones16 = np.kron(np.eye(4), np.full((HD, HD), 1.0 / 16.0)).astype(ml_dtypes.bfloat16)
    rep = np.tile(np.eye(HD, dtype=np.float32), (1, 4))
    shapes = scratch_list(s)
    names = list(shapes) + ["lsem", "ssem", "rsem"]
    scratch = [pltpu.VMEM(shape, kind) for shape, kind in shapes.values()]
    scratch += [
        pltpu.SemaphoreType.DMA((N_LOCAL,)),
        pltpu.SemaphoreType.DMA((N_REMOTE,)),
        pltpu.SemaphoreType.DMA((N_REMOTE,)),
    ]
    results = [
        ((rows, width), bf16),
        ((rows, width), bf16),
        ((3, s.block, width), f32),
        (up_weight.shape, f32),
        (out_weight.shape, f32),
        (down_weight.shape, f32),
        ((24, 128), f32),
    ]
    raw = pl.BlockSpec(memory_space=pl.ANY)
    vm = pl.BlockSpec(memory_space=pltpu.VMEM)
    outs = pl.pallas_call(
        functools.partial(fused_kernel, s, names),
        out_shape=tuple(pltpu.VMEM(shape, kind) for shape, kind in results),
        in_specs=[raw] * (6 + len(SMALL)),
        out_specs=[vm] * 7,
        scratch_shapes=scratch,
        compiler_params=pltpu.CompilerParams(
            collective_id=0, has_side_effects=True, vmem_limit_bytes=56 * 2**20
        ),
    )(
        tokens,
        out_grad,
        jnp.transpose(qkv_weight, (1, 0, 2)),
        up_weight,
        out_weight,
        down_weight,
        doc_lengths,
        norm_gain,
        norm_shift,
        qkv_bias,
        out_bias,
        up_bias,
        qmc_weights,
        jnp.asarray(rotary_table(rows // MB // 2)),
        jnp.asarray(rotary_swap()),
        jnp.asarray(ones16),
        jnp.asarray(dct_rows()),
        jnp.asarray(rep),
        omega,
    )
    whole = [jax.ShapeDtypeStruct(shape, kind) for shape, kind in results[:6]]
    full = up_bias.shape[0]
    short = [(width // 128, 128)] * 3 + [(3, width), (full // 128, 128)]
    done = pl.pallas_call(
        finish_kernel,
        out_shape=tuple(whole) + tuple(jax.ShapeDtypeStruct(shape, f32) for shape in short),
        in_specs=[vm] * 7,
        out_specs=[raw] * 6 + [vm] * 5,
        scratch_shapes=[pltpu.SemaphoreType.DMA((6,))],
        compiler_params=pltpu.CompilerParams(vmem_limit_bytes=4 * 2**20),
    )(*(pltpu.with_memory_space_constraint(out, pltpu.VMEM) for out in outs))
    o_blk, o_inp, o_qkv, o_up, o_out, o_down, gain, shift, out_bias_grad, qkv_bias_grad, up_bias_grad = done
    return (
        o_blk,
        o_inp,
        gain.reshape(-1),
        shift.reshape(-1),
        jnp.transpose(o_qkv, (1, 0, 2)),
        qkv_bias_grad,
        o_out,
        out_bias_grad.reshape(-1),
        o_up,
        up_bias_grad.reshape(-1),
        o_down,
    )


def solution(mesh):
    in_specs = (
        P(DP, FEAT),
        P(DP, None),
        P(FEAT),
        P(FEAT),
        P(DP, None, FEAT),
        P(None, FEAT),
        P(),
        P(),
        P(FEAT, DP),
        P(FEAT),
        P(DP, FEAT),
        P(FEAT),
        P(FEAT, DP),
        P(DP, FEAT),
    )
    out_specs = (
        P(DP, FEAT),
        P(DP, FEAT),
        P(FEAT),
        P(FEAT),
        P(DP, None, FEAT),
        P(None, FEAT),
        P(FEAT, DP),
        P(FEAT),
        P(DP, FEAT),
        P(FEAT),
        P(FEAT, DP),
    )
    dp_count, feat_count = mesh.shape[DP], mesh.shape[FEAT]
    if (dp_count, feat_count) == (8, 4):
        per_device = functools.partial(on_device_fused, dp_count, feat_count)
    else:
        per_device = on_device
    return jax.shard_map(
        per_device, mesh=mesh, in_specs=in_specs, out_specs=out_specs, check_vma=False
    )
```

```python
import functools
import math

import jax
import jax.numpy as jnp
import ml_dtypes
import numpy as np
from jax import lax
from jax.experimental import pallas as pl
from jax.experimental.pallas import tpu as pltpu
from jax.sharding import PartitionSpec as P

D = 1024
HD = 64
ROT = 16
M = 64
SPAN = 64
MB = 2
SEQS = 3


FEAT = "feat"
DP = "dp"
QKV = "qkv"
OUT = "out"
UP = "up"
DOWN = "down"
TOK = "tok"
GRD = "grd"
NRM = "nrm"
BLK = "blk"


epsilon = 1e-05
highest = lax.Precision.HIGHEST


def row_layout(lengths, row_count):
    seq_ends = jnp.cumsum(lengths)
    starts = seq_ends - lengths
    row_ids = jnp.arange(row_count, dtype=jnp.int32)
    segment = jnp.sum((row_ids[:, None] >= seq_ends[None, :]).astype(jnp.int32), 1)
    belongs = segment[:, None] == jnp.arange(lengths.shape[0], dtype=jnp.int32)[None, :]
    row_begin = jnp.sum(jnp.where(belongs, starts[None, :], 0), 1)
    return (segment, (row_ids - row_begin).astype(jnp.float32))


def rotate(vectors, positions):
    half_rot = ROT // 2
    inv_freq = jnp.exp(-jnp.arange(half_rot, dtype=jnp.float32) * (2.0 / ROT) * math.log(10000.0))
    angles = positions[:, None] * inv_freq[None, :]
    cosine = jnp.cos(angles)[:, None, :]
    sine = jnp.sin(angles)[:, None, :]
    lower_part = vectors[..., :half_rot]
    upper_part = vectors[..., half_rot:ROT]
    return jnp.concatenate(
        [
            lower_part * cosine - upper_part * sine,
            upper_part * cosine + lower_part * sine,
            vectors[..., ROT:],
        ],
        -1,
    )


def dct_table():
    ramp_vals = jnp.arange(HD, dtype=jnp.float32)
    weights_row = jnp.where(ramp_vals == 0.0, jnp.sqrt(1.0 / HD), jnp.sqrt(2.0 / HD))
    return (
        jnp.cos(math.pi * (2.0 * ramp_vals[None, :] + 1.0) * ramp_vals[:, None] / (2.0 * HD))
        * weights_row[:, None]
    )


def feature_map(vectors, positions, omega):
    turned = rotate(vectors, positions) * HD ** (-0.25)
    spectrum = jnp.einsum("rhn,kn->rhk", turned, dct_table(), precision=highest)
    scores = jnp.einsum("rhk,kj->rhj", spectrum, omega, precision=highest)
    return jnp.exp(scores - 0.5 * jnp.sum(turned * turned, -1, keepdims=True))


def both_maps(queries, keys_raw, positions, omega_used, weights_used):
    return (
        weights_used * feature_map(queries, positions, omega_used),
        feature_map(keys_raw, positions, omega_used),
    )


def gelu_exact(pre_act):
    return jax.nn.gelu(pre_act, approximate=False)


def block_masks(segment):
    nblocks = segment.shape[0] // SPAN
    blocks = segment.reshape(nblocks, SPAN)
    head_seg = blocks[:, 0]
    following = jnp.concatenate([head_seg[1:], jnp.full((1,), -1, jnp.int32)])
    carry_keep = (head_seg == following).astype(jnp.float32)
    row_gate = (blocks == head_seg[:, None]).astype(jnp.float32)
    chosen = (blocks == following[:, None]).astype(jnp.float32)
    offsets_in = jnp.arange(SPAN, dtype=jnp.int32)
    causal = offsets_in[:, None] >= offsets_in[None, :]
    same_seq = blocks[:, :, None] == blocks[:, None, :]
    block_mask = (causal[None] & same_seq).astype(jnp.float32)
    return (carry_keep, row_gate, chosen, block_mask)


def carry_chain(carry_keep, increments):

    def combine(earlier, latter):
        return (earlier[0] * latter[0], latter[0] * earlier[1] + latter[1])

    factors = jnp.broadcast_to(carry_keep[:, None, None, None], increments.shape)
    return lax.associative_scan(combine, (factors, increments))[1]


def block_states(carry_keep, picked, block_v):
    increments = jnp.einsum("bshj,bshe->bhje", picked, block_v, precision=highest)
    totals = carry_chain(carry_keep, increments)
    return jnp.concatenate([jnp.zeros_like(totals[:1]), totals[:-1]], 0)


def attend(query_feat, key_feat, extended, masks):
    carry_keep, row_gate, chosen, block_mask = masks
    nblocks, span_len = row_gate.shape
    head_count = query_feat.shape[1]
    block_q = query_feat.reshape(nblocks, span_len, head_count, -1)
    block_k = key_feat.reshape(nblocks, span_len, head_count, -1)
    block_v = extended.reshape(nblocks, span_len, head_count, -1)
    scores = (
        jnp.einsum("bthj,bshj->bhts", block_q, block_k, precision=highest) * block_mask[:, None]
    )
    inside = jnp.einsum("bhts,bshe->bthe", scores, block_v, precision=highest)
    states = block_states(carry_keep, block_k * chosen[:, :, None, None], block_v)
    outside = jnp.einsum(
        "bthj,bhje->bthe", block_q * row_gate[:, :, None, None], states, precision=highest
    )
    return (inside + outside).reshape(nblocks * span_len, head_count, -1)


def attend_back(query_feat, key_feat, extended, masks, upstream):
    carry_keep, row_gate, chosen, block_mask = masks
    nblocks, span_len = row_gate.shape
    head_count = query_feat.shape[1]
    block_q = query_feat.reshape(nblocks, span_len, head_count, -1)
    block_k = key_feat.reshape(nblocks, span_len, head_count, -1)
    block_v = extended.reshape(nblocks, span_len, head_count, -1)
    block_g = upstream.reshape(nblocks, span_len, head_count, -1)
    picked = block_k * chosen[:, :, None, None]
    gated = block_q * row_gate[:, :, None, None]
    scores = (
        jnp.einsum("bthj,bshj->bhts", block_q, block_k, precision=highest) * block_mask[:, None]
    )
    states = block_states(carry_keep, picked, block_v)
    score_grad = (
        jnp.einsum("bthe,bshe->bhts", block_g, block_v, precision=highest) * block_mask[:, None]
    )
    query_grad = jnp.einsum("bhts,bshj->bthj", score_grad, block_k, precision=highest)
    query_grad = query_grad + row_gate[:, :, None, None] * jnp.einsum(
        "bthe,bhje->bthj", block_g, states, precision=highest
    )
    key_grad = jnp.einsum("bhts,bthj->bshj", score_grad, block_q, precision=highest)
    value_grad = jnp.einsum("bhts,bthe->bshe", scores, block_g, precision=highest)
    state_grad = jnp.einsum("bthj,bthe->bhje", gated, block_g, precision=highest)
    later_total = jnp.flip(carry_chain(jnp.flip(carry_keep, 0), jnp.flip(state_grad, 0)), 0)
    incr_grad = jnp.concatenate([later_total[1:], jnp.zeros_like(later_total[:1])], 0)
    key_grad = key_grad + chosen[:, :, None, None] * jnp.einsum(
        "bhje,bshe->bshj", incr_grad, block_v, precision=highest
    )
    value_grad = value_grad + jnp.einsum("bshj,bhje->bshe", picked, incr_grad, precision=highest)
    row_total = nblocks * span_len
    return (
        query_grad.reshape(row_total, head_count, -1),
        key_grad.reshape(row_total, head_count, -1),
        value_grad.reshape(row_total, head_count, -1),
    )


def on_device(
    tokens,
    doc_lengths,
    norm_gain,
    norm_shift,
    qkv_weight,
    qkv_bias,
    omega,
    qmc_weights,
    out_weight,
    out_bias,
    up_weight,
    up_bias,
    down_weight,
    out_grad,
):
    feat_parts = lax.axis_size(FEAT)
    feat_index = lax.axis_index(FEAT)
    qkv_full, up_full, out_rows, down_rows = (
        lax.all_gather(qkv_weight, DP, axis=0, tiled=True),
        lax.all_gather(up_weight, DP, axis=0, tiled=True),
        lax.all_gather(out_weight, DP, axis=1, tiled=True),
        lax.all_gather(down_weight, DP, axis=1, tiled=True),
    )
    gain_vec = norm_gain.astype(jnp.float32)
    shift_vec = norm_shift.astype(jnp.float32)
    inputs = tokens.astype(jnp.float32)
    row_sums = lax.psum((jnp.sum(inputs, 1), jnp.sum(inputs * inputs, 1)), FEAT)
    center = row_sums[0] / D
    spread = row_sums[1] / D - center * center
    inv_root = lax.rsqrt(spread + epsilon)
    standard = (inputs - center[:, None]) * inv_root[:, None]
    normed_all = lax.all_gather(
        (standard * gain_vec + shift_vec).astype(jnp.bfloat16), FEAT, axis=1, tiled=True
    )
    local_width = tokens.shape[1]
    local_heads = local_width // HD
    feat_count = M // feat_parts
    omega_used = lax.dynamic_slice_in_dim(omega, feat_index * feat_count, feat_count, 1)
    weights_used = lax.dynamic_slice_in_dim(qmc_weights, feat_index * feat_count, feat_count, 0)
    row_count = tokens.shape[0] // MB
    qkv_bias_f = qkv_bias.astype(jnp.float32)
    up_bias_f = up_bias.astype(jnp.float32)
    out_bias_f = out_bias.astype(jnp.float32)
    block_outs = []
    saved_state = []
    for micro_idx in range(MB):
        offset = micro_idx * row_count
        normed_rows = normed_all[offset : offset + row_count]
        segment, positions = row_layout(doc_lengths[micro_idx], row_count)
        masks = block_masks(segment)
        projected = (
            jnp.einsum("rd,dcf->rcf", normed_rows, qkv_full, preferred_element_type=jnp.float32)
            + qkv_bias_f
        ).astype(jnp.bfloat16)
        pre_act = jnp.dot(normed_rows, up_full, preferred_element_type=jnp.float32) + up_bias_f
        hidden = gelu_exact(pre_act).astype(jnp.bfloat16)
        projected_used = lax.all_gather(projected, FEAT, axis=2, tiled=True)
        heads_used = projected_used.shape[2] // HD
        heads_view = projected_used.astype(jnp.float32).reshape(row_count, 3, heads_used, HD)
        queries = heads_view[:, 0]
        keys_raw = heads_view[:, 1]
        query_map, key_map = both_maps(queries, keys_raw, positions, omega_used, weights_used)
        query_feat = query_map.astype(jnp.bfloat16).astype(jnp.float32)
        key_feat = key_map.astype(jnp.bfloat16).astype(jnp.float32)
        extended = jnp.concatenate(
            [heads_view[:, 2], jnp.ones((row_count, heads_used, 1), jnp.float32)], 2
        )
        mixed = attend(query_feat, key_feat, extended, masks)
        numerator = mixed[..., :HD]
        denominator = mixed[..., HD]
        numerator, denominator = (
            lax.psum_scatter(numerator, FEAT, scatter_dimension=1, tiled=True),
            lax.psum_scatter(denominator, FEAT, scatter_dimension=1, tiled=True),
        )
        attended = (
            (numerator / denominator[..., None])
            .reshape(row_count, local_width)
            .astype(jnp.bfloat16)
        )
        branch = jnp.dot(attended, out_rows, preferred_element_type=jnp.float32)
        branch = branch + jnp.dot(hidden, down_rows, preferred_element_type=jnp.float32)
        summed = lax.psum_scatter(
            branch.astype(jnp.bfloat16), FEAT, scatter_dimension=1, tiled=True
        ).astype(jnp.float32)
        block_outs.append(
            (inputs[offset : offset + row_count] + summed + out_bias_f).astype(jnp.bfloat16)
        )
        saved_state.append(
            (
                normed_rows,
                positions,
                masks,
                pre_act,
                hidden,
                queries,
                keys_raw,
                extended,
                query_feat,
                key_feat,
                numerator,
                denominator,
                attended,
            )
        )
    qkv_acc = jnp.zeros(qkv_full.shape, jnp.float32)
    up_acc = jnp.zeros(up_full.shape, jnp.float32)
    outw_acc = jnp.zeros(out_rows.shape, jnp.float32)
    down_acc = jnp.zeros(down_rows.shape, jnp.float32)
    qkv_bias_acc = jnp.zeros((3, local_width), jnp.float32)
    up_bias_acc = jnp.zeros((up_full.shape[1],), jnp.float32)
    normed_grads = []
    for micro_idx in range(MB):
        offset = micro_idx * row_count
        (
            normed_rows,
            positions,
            masks,
            pre_act,
            hidden,
            queries,
            keys_raw,
            extended,
            query_feat,
            key_feat,
            numerator,
            denominator,
            attended,
        ) = saved_state[micro_idx]
        cotangent = lax.all_gather(
            out_grad[offset : offset + row_count], FEAT, axis=1, tiled=True
        )
        outw_acc = outw_acc + jnp.einsum(
            "rk,rd->kd", attended, cotangent, preferred_element_type=jnp.float32
        )
        down_acc = down_acc + jnp.einsum(
            "rk,rd->kd", hidden, cotangent, preferred_element_type=jnp.float32
        )
        att_grad = jnp.einsum("rd,kd->rk", cotangent, out_rows, preferred_element_type=jnp.float32)
        hidden_grad = jnp.einsum(
            "rd,kd->rk", cotangent, down_rows, preferred_element_type=jnp.float32
        )
        _, gelu_pull = jax.vjp(gelu_exact, pre_act)
        pre_grad = gelu_pull(hidden_grad)[0].astype(jnp.bfloat16)
        up_acc = up_acc + jnp.einsum(
            "rd,rk->dk", normed_rows, pre_grad, preferred_element_type=jnp.float32
        )
        up_bias_acc = up_bias_acc + jnp.sum(pre_grad.astype(jnp.float32), 0)
        att_grad = att_grad.reshape(row_count, local_heads, HD)
        numer_grad = (att_grad / denominator[..., None]).astype(jnp.bfloat16)
        denom_grad = (-jnp.sum(att_grad * numerator, 2) / (denominator * denominator)).astype(
            jnp.bfloat16
        )
        numer_grad, denom_grad = (
            lax.all_gather(numer_grad, FEAT, axis=1, tiled=True),
            lax.all_gather(denom_grad, FEAT, axis=1, tiled=True),
        )
        upstream = jnp.concatenate(
            [numer_grad.astype(jnp.float32), denom_grad.astype(jnp.float32)[..., None]], 2
        )
        query_feat_grad, key_feat_grad, extended_grad = attend_back(
            query_feat, key_feat, extended, masks, upstream
        )

        def map_local(query_in, key_in):
            return both_maps(query_in, key_in, positions, omega_used, weights_used)

        _, map_pull = jax.vjp(map_local, queries, keys_raw)
        query_grad, key_grad = map_pull((query_feat_grad, key_feat_grad))
        proj_rows = jnp.stack([query_grad, key_grad, extended_grad[..., :HD]], 1).reshape(
            row_count, 3, -1
        )
        proj_rows = lax.psum_scatter(proj_rows, FEAT, scatter_dimension=2, tiled=True)
        proj_grad = proj_rows.astype(jnp.bfloat16)
        qkv_acc = qkv_acc + jnp.einsum(
            "rd,rcf->dcf", normed_rows, proj_grad, preferred_element_type=jnp.float32
        )
        qkv_bias_acc = qkv_bias_acc + jnp.sum(proj_grad.astype(jnp.float32), 0)
        normed_part = jnp.einsum(
            "rcf,dcf->rd", proj_grad, qkv_full, preferred_element_type=jnp.float32
        )
        normed_part = normed_part + jnp.einsum(
            "rk,dk->rd", pre_grad, up_full, preferred_element_type=jnp.float32
        )
        normed_grads.append(
            lax.psum_scatter(
                normed_part.astype(jnp.bfloat16), FEAT, scatter_dimension=1, tiled=True
            ).astype(jnp.float32)
        )
    normed_grad = jnp.concatenate(normed_grads, 0)
    scaled = normed_grad * gain_vec
    grad_sums = lax.psum((jnp.sum(scaled, 1), jnp.sum(scaled * standard, 1)), FEAT)
    out_grad_f = out_grad.astype(jnp.float32)
    input_grad = out_grad_f + inv_root[:, None] * (
        scaled - grad_sums[0][:, None] / D - standard * grad_sums[1][:, None] / D
    )
    gain_part = jnp.sum(normed_grad * standard, 0)
    shift_part = jnp.sum(normed_grad, 0)
    out_bias_part = jnp.sum(out_grad_f, 0)
    qkv_grad, up_grad, outw_grad, down_grad = (
        lax.psum_scatter(
            qkv_acc.astype(jnp.bfloat16), DP, scatter_dimension=0, tiled=True
        ).astype(jnp.float32),
        lax.psum_scatter(up_acc.astype(jnp.bfloat16), DP, scatter_dimension=0, tiled=True).astype(
            jnp.float32
        ),
        lax.psum_scatter(
            outw_acc.astype(jnp.bfloat16), DP, scatter_dimension=1, tiled=True
        ).astype(jnp.float32),
        lax.psum_scatter(
            down_acc.astype(jnp.bfloat16), DP, scatter_dimension=1, tiled=True
        ).astype(jnp.float32),
    )
    gain_grad, shift_grad, qkv_bias_grad, out_bias_grad, up_bias_grad = lax.psum(
        (gain_part, shift_part, qkv_bias_acc, out_bias_part, up_bias_acc), DP
    )
    return (
        jnp.concatenate(block_outs, 0),
        input_grad.astype(jnp.bfloat16),
        gain_grad,
        shift_grad,
        qkv_grad,
        qkv_bias_grad,
        outw_grad,
        out_bias_grad,
        up_grad,
        up_bias_grad,
        down_grad,
    )


MESH = pl.DeviceIdType.MESH
f32, bf16 = jnp.float32, jnp.bfloat16
NT = ((1,), (1,))
TN = ((0,), (0,))
EXTRA = 16


def dot(a, b, dims=((1,), (0,)), precision=None):
    return lax.dot_general(
        a, b, (dims, ((), ())), precision=precision, preferred_element_type=f32
    )


def rotary_table(longest):
    half_rot = ROT // 2
    inv_freq = np.exp(
        -np.arange(half_rot, dtype=np.float32)
        * np.float32(2.0 / ROT)
        * np.float32(math.log(10000.0))
    ).astype(np.float32)
    angles = np.arange(longest, dtype=np.float32)[:, None] * inv_freq[None, :]
    cosine = np.ones((longest, HD), np.float32)
    sine = np.zeros((longest, HD), np.float32)
    for part in range(2):
        cosine[:, part * half_rot : (part + 1) * half_rot] = np.cos(angles)
        sine[:, part * half_rot : (part + 1) * half_rot] = np.sin(angles)
    rest = np.concatenate([cosine, cosine, sine, sine], 1).astype(np.float32)
    terms = []
    for _ in range(3):
        term = rest.astype(ml_dtypes.bfloat16)
        terms.append(term)
        rest = rest - term.astype(np.float32)
    return np.concatenate(terms, 0)


def rotary_swap():
    half_rot = ROT // 2
    one = np.zeros((HD, HD), np.float32)
    for i in range(half_rot):
        one[i + half_rot, i] = -1.0
        one[i, i + half_rot] = 1.0
    return np.kron(np.eye(4, dtype=np.float32), one).astype(ml_dtypes.bfloat16)


def dct_rows():
    ramp = np.arange(HD, dtype=np.float32)
    scale = np.where(ramp == 0.0, np.sqrt(1.0 / HD), np.sqrt(2.0 / HD))
    table = np.cos(math.pi * (2.0 * ramp[None, :] + 1.0) * ramp[:, None] / (2.0 * HD)) * scale[:, None]
    return np.tile(table.T, (4, 1)).astype(np.float32)


class Sizes:
    def __init__(self, rows, width, hidden, dp_count, feat_count):
        self.rows = rows
        self.width = width
        self.model = width * feat_count
        self.span = rows // MB
        self.total = 2 * rows
        self.micro = 2 * MB
        self.half = width // 2
        self.hidden = hidden // 2
        self.block = self.model // dp_count
        self.planes = dp_count // 2


def scratch_list(s):
    pl_, bl, hf, hd, tt, md = s.planes, s.block, s.half, s.hidden, s.total, s.model
    grads = {
        QKV: (3, bl, hf),
        OUT: (hf, bl),
        UP: (bl, hd),
        DOWN: (hd, bl),
    }
    shapes = dict(
        XG=((2, s.rows + EXTRA, md), bf16),
        G=((tt, md), bf16),
        WQ=((3, md, hf), bf16),
        WU=((md, hd), bf16),
        WO=((hf, md), bf16),
        WD=((hd, md), bf16),
        NB=((tt, md), bf16),
        MU=((tt, 1), f32),
        IV=((tt, 1), f32),
        A2=((2 * s.width // 2, s.width), f32),
        WB=((tt, 2 * hf), bf16),
        VB=((tt, hf), bf16),
        PHF=((tt, 2 * hf), f32),
        PHB=((tt, 2 * hf), bf16),
        ROTV=((tt, 2 * hf), f32),
        CSB=((tt, 2 * hf), f32),
        SB=((s.micro, 2, s.span, s.span), bf16),
        ND=((tt, 2 * hf), f32),
        AT=((tt, hf), bf16),
        PG=((tt, 3 * hf), bf16),
        HB=((tt, hd), bf16),
        GP=((tt, hd), f32),
        PRE=((tt, hd), bf16),
        QBG=((1, 3 * hf), f32),
        UBG=((1, hd), f32),
        NGF=((s.rows, s.width), f32),
        ST=((16, s.rows), f32),
        STR=((3, 16, s.rows), f32),
        SV=((24, 128), f32),
        SMALL=((3, max(2 * hd, 4 * s.width)), f32),
        IN_lens=((MB, SEQS), jnp.int32),
        IN_gain=((s.width,), bf16),
        IN_shift=((s.width,), bf16),
        IN_qkv_bias=((3, s.width), bf16),
        IN_out_bias=((s.width,), bf16),
        IN_up_bias=((2 * hd,), bf16),
        IN_qmc=((M,), f32),
        IN_tab=((3 * (s.span // 2), 2 * hf), bf16),
        IN_swap=((2 * hf, 2 * hf), bf16),
        IN_ones16=((2 * hf, 2 * hf), bf16),
        IN_dct=((2 * hf, HD), f32),
        IN_rep=((HD, 2 * hf), f32),
        IN_omega=((HD, M), f32),
        SVR=((7, 24, 128), f32),
    )
    for name, shape in grads.items():
        shapes["SX" + name] = ((pl_,) + shape, bf16)
        shapes["RX" + name] = ((pl_,) + shape, bf16)
        shapes["KX" + name] = ((pl_,) + shape, f32)
        shapes["ZS" + name] = ((3,) + shape, bf16)
        shapes["ZR" + name] = ((3,) + shape, bf16)
        shapes["ZM" + name] = (shape, bf16)
    for name in (BLK, NRM):
        shapes["CS" + name] = ((tt, 2 * s.width), bf16)
        shapes["CR" + name] = ((tt, 2 * s.width), bf16)
        shapes["KC" + name] = ((tt, 2 * s.width), f32)
        shapes["KY" + name] = ((tt, s.width), f32)
        shapes["YS" + name] = ((tt, s.width), bf16)
        shapes["YR" + name] = ((tt, s.width), bf16)
        shapes["AS" + name] = ((s.rows, s.width), bf16)
        shapes["AR" + name] = ((s.rows, s.width), bf16)
    return shapes


SMALL = ("lens", "gain", "shift", "qkv_bias", "out_bias", "up_bias", "qmc", "tab", "swap", "ones16", "dct", "rep", "omega")
N_LOCAL = 6 + len(SMALL)
N_REMOTE = 120


def fused_kernel(s, names, *refs):
    (tok, grd, wq_in, wu_in, wo_in, wd_in) = refs[:6]
    small_in = refs[6 : 6 + len(SMALL)]
    o_blk, o_inp, o_qkv, o_up, o_out, o_down, o_small = refs[6 + len(SMALL) : 13 + len(SMALL)]
    m_ = dict(zip(names, refs[13 + len(SMALL) :]))
    small, tab, swap, ones16 = m_["SMALL"], m_["IN_tab"], m_["IN_swap"], m_["IN_ones16"]
    dct, rep, omega = m_["IN_dct"], m_["IN_rep"], m_["IN_omega"]
    lsem, ssem, rsem = m_["lsem"], m_["ssem"], m_["rsem"]
    XG, G, WQ, WU, WO, WD = (m_[k] for k in ("XG", "G", "WQ", "WU", "WO", "WD"))
    NB, MU, IV = m_["NB"], m_["MU"], m_["IV"]

    dp = lax.axis_index(DP)
    ft = lax.axis_index(FEAT)
    z, x = dp // 2, dp % 2
    zl = z % 2
    y, c = ft // 2, ft % 2
    zd = (z, z + 1 - 2 * zl, (z + 2) % 4, 3 - z)
    hl = (zl, 1 - zl, zl, 1 - zl)
    inner = zl != z // 2

    def partner(d):
        if isinstance(d, int):
            return zd[d]
        return (z // 2 + d // 2) % 2 * 2 + (z + d) % 2

    counter = [0]

    def new(n=1):
        counter[0] += n
        return counter[0] - n

    def device(d=0, fx=False, fy=False, fc=False):
        return {
            DP: partner(d) * 2 + (1 - x if fx else x),
            FEAT: (1 - y if fy else y) * 2 + (1 - c if fc else c),
        }

    def send(src, dst, sem, where, arrival=None):
        copy = pltpu.make_async_remote_copy(
            src_ref=src,
            dst_ref=dst,
            send_sem=ssem.at[sem],
            recv_sem=rsem.at[sem if arrival is None else arrival],
            device_id=where,
            device_id_type=MESH,
        )
        return copy

    def go(src, dst, sem, where):
        send(src, dst, sem, where).start()

    def arrived(ref, sem, where):
        send(ref, ref, sem, where).wait_recv()

    mo = pl.multiple_of

    def lanes(index, size):
        return pl.ds(mo(index * size, size), size)

    def tok_at(b, f):
        return XG.at[b, :, lanes(f, s.width)]

    def grd_at(b, f):
        return G.at[lanes(b, s.rows), lanes(f, s.width)]

    def own_half(w, h):
        if w == QKV:
            return wq_in.at[:, :, lanes(h, s.half)]
        if w == UP:
            return wu_in.at[:, lanes(h, s.hidden)]
        if w == OUT:
            return wo_in.at[lanes(h, s.half), :]
        return wd_in.at[lanes(h, s.hidden), :]

    def weight_at(w, block):
        if w == QKV:
            return WQ.at[:, lanes(block, s.block), :]
        if w == UP:
            return WU.at[lanes(block, s.block), :]
        if w == OUT:
            return WO.at[:, lanes(block, s.block)]
        return WD.at[:, lanes(block, s.block)]

    ws = (QKV, OUT, UP, DOWN)

    local = [
        pltpu.make_async_copy(tok, XG.at[zl, pl.ds(0, s.rows), lanes(ft, s.width)], lsem.at[0]),
        pltpu.make_async_copy(grd, grd_at(zl, ft), lsem.at[1]),
    ]
    for i, w in enumerate(ws):
        local.append(pltpu.make_async_copy(own_half(w, zl), weight_at(w, dp), lsem.at[2 + i]))
    for i, name in enumerate(SMALL):
        local.append(pltpu.make_async_copy(small_in[i], m_["IN_" + name], lsem.at[6 + i]))
    for copy in local:
        copy.start()

    barrier = pltpu.get_barrier_semaphore()
    partners = [device(d) for d in (1, 2, 3)] + [device(d, fx=True) for d in (0, 1, 2, 3)]
    partners += [device(fy=True), device(fc=True), device(fy=True, fc=True)]
    for where in partners:
        pl.semaphore_signal(barrier, inc=1, device_id=where, device_id_type=MESH)
    pl.semaphore_wait(barrier, len(partners))
    local_grd, local_weight, local_table = local[1], dict(zip(ws, local[2:6])), local[-6:]
    for copy in local[:1] + local[6:-6]:
        copy.wait()

    def row_of(name):
        value = m_["IN_" + name][...].astype(f32)
        return value.reshape(1, value.shape[0])

    lens = m_["IN_lens"][...].astype(f32)
    rows = [row_of("gain"), row_of("shift")]
    for i in range(MB):
        for j in range(SEQS):
            rows.append(jnp.broadcast_to(lens[i : i + 1, j : j + 1], (1, s.width)))
    rows.append(jnp.zeros((EXTRA - len(rows), s.width), f32))
    XG[zl, s.rows : s.rows + EXTRA, lanes(ft, s.width)] = jnp.concatenate(rows, 0).astype(bf16)
    small[0:1, 0 : 2 * s.hidden] = row_of("up_bias")
    for k in range(3):
        small[1:2, k * s.width : (k + 1) * s.width] = m_["IN_qkv_bias"][k : k + 1, :].astype(f32)
    small[1:2, 3 * s.width : 4 * s.width] = row_of("out_bias")
    qmc = row_of("qmc")
    small[2:3, 0 : 2 * s.half] = jnp.concatenate([qmc, qmc, jnp.ones((1, s.half), f32)], 1)

    sem_act = {TOK: new(7), GRD: new(7)}

    def act_own(name, at, axis):
        k, where = {"c": (0, device(fc=True)), "y": (1, device(fy=True)), "z": (2, device(1))}[axis]
        go(at(zl, ft) if name == TOK else grd, at(zl, ft), sem_act[name] + k, where)

    def act_arrive(name, at, k):
        base = sem_act[name]
        fy = (1 - y) * 2 + c
        zb = 1 - zl
        if k == 0:
            arrived(at(zb, ft), base + 2, device(1))
            go(at(zb, ft), at(zb, ft), base + 3, device(fy=True))
            go(at(zb, ft), at(zb, ft), base + 4, device(fc=True))
        elif k == 1:
            arrived(at(zl, fy), base + 1, device(fy=True))
            go(at(zl, fy), at(zl, fy), base + 5, device(fc=True))
        else:
            arrived(at(zb, fy), base + 3, device(fy=True))
            go(at(zb, fy), at(zb, fy), base + 6, device(fc=True))

    def act_rest(name, at):
        base = sem_act[name]
        if name == GRD:
            local_grd.wait()
        fc = y * 2 + 1 - c
        fyc = (1 - y) * 2 + 1 - c
        for k, b, f in ((0, zl, fc), (4, 1 - zl, fc), (5, zl, fyc), (6, 1 - zl, fyc)):
            arrived(at(b, f), base + k, device(fc=True))

    def act_gathered(name, at):
        base = sem_act[name]
        fy = (1 - y) * 2 + c
        zb = 1 - zl
        to_c, to_y = device(fc=True), device(fy=True)
        for k, b, f, where in (
            (0, zl, ft, to_c),
            (1, zl, ft, to_y),
            (2, zl, ft, device(1)),
            (3, zb, ft, to_y),
            (4, zb, ft, to_c),
            (5, zl, fy, to_c),
            (6, zb, fy, to_c),
        ):
            send(at(b, f), at(b, f), base + k, where).wait_send()

    sem_z = {w: new(3) for w in ws}
    sem_x = {w: new(4) for w in ws}
    sem_r = {w: new() for w in ws}
    sem_m = {w: new() for w in ws}

    waited = set()

    def w_z(w, d):
        def start():
            go(own_half(w, hl[d]), weight_at(w, dp), sem_z[w] + d - 1, device(d))

        if d == 3:
            pl.when(inner)(start)
        else:
            start()

    def w_near(w):
        at = weight_at(w, zd[1] * 2 + x)
        arrived(at, sem_z[w], device(1))

    def relay(w):
        at = weight_at(w, zd[1] * 2 + x)
        return send(at, at, sem_r[w], device(2), sem_z[w] + 2)

    def w_relay(w):
        first = w not in waited
        waited.add(w)

        @pl.when(inner)
        def _():
            if first:
                w_near(w)
            relay(w).start()

    def w_own(w):
        go(own_half(w, zl), weight_at(w, dp), sem_x[w], device(fx=True))

    def w_forward(w, d):
        at = weight_at(w, partner(d) * 2 + x)
        if d > 1:
            arrived(at, sem_z[w] + d - 1, device(d))
        elif w in waited:
            pl.when(jnp.logical_not(inner))(lambda: w_near(w))
        else:
            waited.add(w)
            w_near(w)
        go(at, at, sem_x[w] + d, device(fx=True))

    def w_sent(w):
        for d in range(4):
            at = weight_at(w, zd[d] * 2 + x)
            send(at, at, sem_x[w] + d, device(fx=True)).wait_send()
            if d in (1, 2):
                send(own_half(w, hl[d]), weight_at(w, dp), sem_z[w] + d - 1, device(d)).wait_send()

        @pl.when(inner)
        def _():
            send(own_half(w, hl[3]), weight_at(w, dp), sem_z[w] + 2, device(3)).wait_send()
            relay(w).wait_send()

    def w_rest(w):
        local_weight[w].wait()
        for d in range(4):
            arrived(weight_at(w, zd[d] * 2 + 1 - x), sem_x[w] + d, device(fx=True))

    sem_gx = {w: new(4) for w in ws}
    sem_gz = {w: new(3) for w in ws}

    def put_grad(w, zp, mine, theirs):
        m_["KX" + w][zp] = mine
        m_["SX" + w][zp] = theirs.astype(bf16)
        src, dst = m_["SX" + w].at[zp], m_["RX" + w].at[zp]
        send(src, dst, sem_gx[w] + zp, device(fx=True)).start()

    def grad_copy(w, d):
        return send(m_["ZS" + w].at[d - 1], m_["ZR" + w].at[d - 1], sem_gz[w] + d - 1, device(d))

    def grad_pass(w):
        return send(m_["ZS" + w].at[2], m_["ZM" + w], sem_m[w], device(2))

    def grad_z(w, d):
        zp = zd[d]
        arrived(m_["RX" + w].at[zp], sem_gx[w] + zp, device(fx=True))
        both = m_["KX" + w][zp] + m_["RX" + w][zp].astype(f32)
        if d == 0:
            m_["KX" + w][zp] = both
            return
        if d == 1:

            @pl.when(inner)
            def _():
                arrived(m_["ZM" + w], sem_m[w], device(2))
                m_["ZS" + w][0] = (both + m_["ZM" + w][...].astype(f32)).astype(bf16)

            @pl.when(jnp.logical_not(inner))
            def _():
                m_["ZS" + w][0] = both.astype(bf16)

        else:
            m_["ZS" + w][d - 1] = both.astype(bf16)
        if d < 3:
            grad_copy(w, d).start()
        else:
            pl.when(inner)(lambda: grad_copy(w, 3).start())
            pl.when(jnp.logical_not(inner))(lambda: grad_pass(w).start())

    def grad_last(w):
        for d in (1, 2):
            arrived(m_["ZR" + w].at[d - 1], sem_gz[w] + d - 1, device(d))
        got = m_["ZR" + w]
        same = m_["KX" + w][z] + got[1].astype(f32)
        other = got[0].astype(f32)
        def put(half, value):
            if w == QKV:
                o_qkv[:, :, lanes(half, s.half)] = value
            elif w == UP:
                o_up[:, lanes(half, s.hidden)] = value
            elif w == OUT:
                o_out[lanes(half, s.half), :] = value
            else:
                o_down[lanes(half, s.hidden), :] = value

        put(zl, same)

        @pl.when(inner)
        def _():
            arrived(m_["ZR" + w].at[2], sem_gz[w] + 2, device(3))
            put(1 - zl, other + got[2].astype(f32))

        pl.when(jnp.logical_not(inner))(lambda: put(1 - zl, other))

    def grad_sent(w):
        for zp in range(4):
            send(m_["SX" + w].at[zp], m_["RX" + w].at[zp], sem_gx[w] + zp, device(fx=True)).wait_send()
        for d in (1, 2):
            grad_copy(w, d).wait_send()
        pl.when(inner)(lambda: grad_copy(w, 3).wait_send())
        pl.when(jnp.logical_not(inner))(lambda: grad_pass(w).wait_send())

    def pick(flag, a, b):
        return jnp.where(flag == 0, a, b)

    def halves(value, axis):
        n = value.shape[axis] // 2
        lo, hi = lax.slice_in_dim(value, 0, n, axis=axis), lax.slice_in_dim(value, n, 2 * n, axis=axis)
        return pick(x, lo, hi), pick(x, hi, lo)

    sem_c = {k: new(4) for k in (BLK, NRM)}
    sem_y = {k: new(4) for k in (BLK, NRM)}
    sem_a = {k: new(2) for k in (BLK, NRM)}

    def rows_of(i):
        block = (1 - zl) + (i // MB) * (2 * zl - 1)
        return pl.ds(mo(block * s.rows + (i % MB) * s.span, s.span), s.span)

    def act_put(name, i, value):
        r = rows_of(i)
        w_ = s.width
        v = [value[:, k * w_ : (k + 1) * w_] for k in range(4)]
        m_["KC" + name][r, 0:w_] = pick(c, v[0], v[1])
        m_["KC" + name][r, w_ : 2 * w_] = pick(c, v[2], v[3])
        m_["CS" + name][r, 0:w_] = pick(c, v[1], v[0]).astype(bf16)
        m_["CS" + name][r, w_ : 2 * w_] = pick(c, v[3], v[2]).astype(bf16)
        send(m_["CS" + name].at[r], m_["CR" + name].at[r], sem_c[name] + i, device(fc=True)).start()

    def act_y(name, i):
        r = rows_of(i)
        w_ = s.width
        arrived(m_["CR" + name].at[r], sem_c[name] + i, device(fc=True))
        both = m_["KC" + name][r, :] + m_["CR" + name][r, :].astype(f32)
        lo, hi = both[:, :w_], both[:, w_:]
        m_["KY" + name][r, :] = pick(y, lo, hi)
        m_["YS" + name][r, :] = pick(y, hi, lo).astype(bf16)
        send(m_["YS" + name].at[r], m_["YR" + name].at[r], sem_y[name] + i, device(fy=True)).start()

    def act_z(name, i):
        r = rows_of(i)
        q = pl.ds(i * s.span, s.span)
        arrived(m_["YR" + name].at[r], sem_y[name] + i, device(fy=True))
        both = m_["KY" + name][r, :] + m_["YR" + name][r, :].astype(f32)
        m_["AS" + name][q, :] = both.astype(bf16)
        go(m_["AS" + name].at[q], m_["AR" + name].at[q], sem_a[name] + i, device(1))

    def act_last(name, i):
        r = rows_of(MB + i)
        q = pl.ds(i * s.span, s.span)
        arrived(m_["YR" + name].at[r], sem_y[name] + MB + i, device(fy=True))
        arrived(m_["AR" + name].at[q], sem_a[name] + i, device(1))
        return (
            m_["KY" + name][r, :]
            + m_["YR" + name][r, :].astype(f32)
            + m_["AR" + name][q, :].astype(f32)
        )

    def act_sent(name):
        for i in range(4):
            r = rows_of(i)
            send(m_["CS" + name].at[r], m_["CR" + name].at[r], sem_c[name] + i, device(fc=True)).wait_send()
            send(m_["YS" + name].at[r], m_["YR" + name].at[r], sem_y[name] + i, device(fy=True)).wait_send()
        for i in range(MB):
            q = pl.ds(i * s.span, s.span)
            send(m_["AS" + name].at[q], m_["AR" + name].at[q], sem_a[name] + i, device(1)).wait_send()

    def beside(*steps):
        def side(i):
            for at in sorted(set(step[0] for step in steps)):

                @pl.when(i == at)
                def _():
                    for when, do, *args in steps:
                        if when == at:
                            do(*args)

        return side

    def loop(n, body, side=None):
        def step(i, carry):
            if side is not None:
                side(i)
            body(i)
            return carry

        lax.fori_loop(0, n, step, 0)

    def at_micro(m):
        return pl.ds(mo(m * s.span, s.span), s.span)

    def norm_phase(side=None):
        extra = XG[0, s.rows : s.rows + EXTRA, :].astype(f32)
        gain, shift = extra[0:1], extra[1:2]

        def body(m):
            xv = XG[m // MB, pl.ds(mo((m % MB) * s.span, s.span), s.span), :].astype(f32)
            mu = jnp.sum(xv, 1, keepdims=True) * (1.0 / s.model)
            var = jnp.sum(xv * xv, 1, keepdims=True) * (1.0 / s.model) - mu * mu
            inv = lax.rsqrt(var + epsilon)
            r = at_micro(m)
            MU[r, :] = mu
            IV[r, :] = inv
            NB[r, :] = ((xv - mu) * inv * gain + shift).astype(bf16)

        loop(s.micro, body, side)

    def masks(m):
        extra = XG[m // MB, s.rows : s.rows + EXTRA, 0 : s.span].astype(f32)
        row_id = lax.broadcasted_iota(jnp.int32, extra.shape, 0)
        first = 2 + SEQS * (m % MB)

        def length(k):
            return jnp.sum(jnp.where(row_id == first + k, extra, 0.0), 0, keepdims=True)

        end0 = length(0)
        end1 = end0 + length(1)
        t = lax.broadcasted_iota(jnp.int32, (s.span, s.span), 0).astype(f32)
        u = lax.broadcasted_iota(jnp.int32, (s.span, s.span), 1).astype(f32)
        start = jnp.where(t >= end1, end1, jnp.where(t >= end0, end0, 0.0))
        return jnp.logical_and(u <= t, u >= start), t, u, start

    def head_rows():
        lane = lax.broadcasted_iota(jnp.int32, (1, s.half), 1)
        return [jnp.where(lane // HD == h, 1.0, 0.0).astype(bf16) for h in range(2)], [
            jnp.where(lane == h * HD, 1.0, 0.0).astype(bf16) for h in range(2)
        ]

    HIGH = lax.Precision.HIGH
    HIGHEST = lax.Precision.HIGHEST
    hf = s.half

    def table_phase():
        for copy in local_table:
            copy.wait()
        wide = dot(dot(dct[...], omega[...], precision=HIGHEST), rep[...], precision=HIGHEST)
        m_["A2"][...] = wide * (ones16[...].astype(f32) * (16.0 * HD ** (-0.25)))

    def fwd_phase(side=None):
        def body(m):
            r = at_micro(m)
            wq = jnp.concatenate([WQ[0], WQ[1], WQ[2]], 1)
            bias = jnp.concatenate(
                [small[1:2, pl.ds(mo(k * s.width + zl * hf, hf), hf)] for k in range(3)], 1
            )
            p = (dot(NB[r, :], wq) + bias).astype(bf16)
            w, v = p[:, : 2 * hf], p[:, 2 * hf :]
            m_["VB"][r, :] = v
            mask, t, u, start = masks(m)
            pos = t[:, :hf] - start[:, :hf]
            hot = jnp.where(pos == u[:, :hf], 1.0, 0.0).astype(bf16)
            cs = dot(jnp.concatenate([hot, hot, hot], 1), tab[...])
            m_["CSB"][r, :] = cs
            cc = jnp.concatenate([cs[:, :hf], cs[:, :hf]], 1)
            ss = jnp.concatenate([cs[:, hf:], cs[:, hf:]], 1)
            wf = w.astype(f32)
            rot = wf * cc + dot(w, swap[...]) * ss
            m_["ROTV"][r, :] = rot
            score = dot(rot, m_["A2"][...], precision=HIGH)
            norm2 = dot(wf * wf, ones16[...].astype(f32), precision=HIGH)
            ph = jnp.exp(score - norm2) * small[2:3, 0 : 2 * hf]
            m_["PHF"][r, :] = ph
            pb = ph.astype(bf16)
            m_["PHB"][r, :] = pb
            hm, _ = head_rows()
            acc = jnp.zeros((s.span, 2 * hf), f32)
            for h in range(2):
                sc = dot(pb[:, :hf] * hm[h], pb[:, hf:], NT)
                sm = jnp.where(mask, sc, 0.0).astype(bf16)
                m_["SB"][m, h] = sm
                rhs = jnp.concatenate([v * hm[h], jnp.broadcast_to(hm[h], v.shape)], 1)
                acc = acc + dot(sm, rhs)
            m_["ND"][r, :] = acc
            m_["AT"][r, :] = (acc[:, :hf] / acc[:, hf:]).astype(bf16)

        loop(s.micro, body, side)

    def bwd_phase(side=None):
        m_["QBG"][...] = jnp.zeros_like(m_["QBG"])

        def body(m):
            r = at_micro(m)
            mask = masks(m)[0]
            hm, hot = head_rows()
            ag = dot(G[r, :], WO[...], NT)
            nd = m_["ND"][r, :]
            num, den = nd[:, :hf], nd[:, hf:]
            ng = (ag / den).astype(bf16)
            sums = dot(ag * num, ones16[0:hf, 0:hf].astype(f32), precision=HIGH) * 16.0
            dg = (-sums / (den * den)).astype(bf16)
            v = m_["VB"][r, :]
            pb = m_["PHB"][r, :]
            v1 = jnp.concatenate([v, jnp.ones(v.shape, bf16)], 1)
            dq = dk = dv = jnp.zeros((s.span, hf), f32)
            for h in range(2):
                e = dot(jnp.concatenate([ng * hm[h], dg * hot[h]], 1), v1, NT)
                em = jnp.where(mask, e, 0.0).astype(bf16)
                dq = dq + dot(em, pb[:, hf:] * hm[h])
                dk = dk + dot(em, pb[:, :hf] * hm[h], TN)
                dv = dv + dot(m_["SB"][m, h], ng * hm[h], TN)
            dph = jnp.concatenate([dq, dk], 1) * m_["PHF"][r, :]
            rot = m_["ROTV"][r, :]
            both = dot(dph, ones16[...].astype(f32), precision=HIGH) * 2.0
            drot = dot(dph, m_["A2"][...], NT, precision=HIGH) - rot * both
            cs = m_["CSB"][r, :]
            cc = jnp.concatenate([cs[:, :hf], cs[:, :hf]], 1)
            ss = jnp.concatenate([cs[:, hf:], cs[:, hf:]], 1)
            dw = drot * cc + dot(drot * ss, swap[...].astype(f32), NT, precision=HIGH)
            pg = jnp.concatenate([dw, dv], 1).astype(bf16)
            m_["PG"][r, :] = pg
            m_["QBG"][...] += jnp.sum(pg.astype(f32), 0, keepdims=True)

        loop(s.micro, body, side)

    def up_phase(side=None):
        bias = small[0:1, lanes(zl, s.hidden)]

        def body(m):
            r = at_micro(m)
            pre = dot(NB[r, :], WU[...]) + bias
            cdf = 0.5 * (1.0 + lax.erf(pre * math.sqrt(0.5)))
            m_["HB"][r, :] = (pre * cdf).astype(bf16)
            m_["GP"][r, :] = cdf + pre * jnp.exp(-0.5 * pre * pre) * (1.0 / math.sqrt(2.0 * math.pi))

        loop(s.micro, body, side)

    def pre_phase(side=None):
        m_["UBG"][...] = jnp.zeros_like(m_["UBG"])

        def body(m):
            r = at_micro(m)
            pre = (dot(G[r, :], WD[...], NT) * m_["GP"][r, :]).astype(bf16)
            m_["PRE"][r, :] = pre
            m_["UBG"][...] += jnp.sum(pre.astype(f32), 0, keepdims=True)

        loop(s.micro, body, side)

    def nrm_phase(side=None):
        def body(i):
            r = rows_of(i)
            wq = jnp.concatenate([WQ[0], WQ[1], WQ[2]], 1)
            act_put(NRM, i, dot(m_["PG"][r, :], wq, NT) + dot(m_["PRE"][r, :], WU[...], NT))

        loop(4, body, side)

    def blk_phase(side=None):
        def body(i):
            r = rows_of(i)
            act_put(BLK, i, dot(m_["AT"][r, :], WO[...]) + dot(m_["HB"][r, :], WD[...]))

        loop(4, body, side)

    two = 2 * s.block

    def grad_phase(w, side=None):
        def body(i):
            zp = partner(3 - i)
            cols = lanes(zp, two)
            if w == QKV:
                value = dot(NB[:, cols], m_["PG"][...], TN)
                mine, theirs = halves(value, 0)
                mine = jnp.stack([mine[:, k * hf : (k + 1) * hf] for k in range(3)], 0)
                theirs = jnp.stack([theirs[:, k * hf : (k + 1) * hf] for k in range(3)], 0)
            elif w == UP:
                mine, theirs = halves(dot(NB[:, cols], m_["PRE"][...], TN), 0)
            elif w == OUT:
                mine, theirs = halves(dot(m_["AT"][...], G[:, cols], TN), 1)
            else:
                mine, theirs = halves(dot(m_["HB"][...], G[:, cols], TN), 1)
            put_grad(w, zp, mine, theirs)

        loop(s.planes, body, side)

    def out_rows(i):
        return pl.ds(i * s.span, s.span)

    def blk_last():
        for i in range(MB):
            own = XG[zl, i * s.span : (i + 1) * s.span, lanes(ft, s.width)].astype(f32)
            bias = small[1:2, 3 * s.width : 4 * s.width]
            o_blk[out_rows(i), :] = (own + act_last(BLK, i) + bias).astype(bf16)

    sem_st = new(3)
    stat_where = [device(fc=True), device(fy=True), device(fy=True, fc=True)]

    def own_parts():
        extra = XG[0, s.rows : s.rows + EXTRA, lanes(ft, s.width)].astype(f32)
        r = lanes(zl, s.rows)
        own = XG[zl, 0 : s.rows, lanes(ft, s.width)].astype(f32)
        xhat = (own - MU[r, :]) * IV[r, :]
        return extra[0:1], xhat

    def nrm_last():
        for i in range(MB):
            m_["NGF"][out_rows(i), :] = act_last(NRM, i)
        gain, xhat = own_parts()
        ngrad = m_["NGF"][...]
        scaled = ngrad * gain
        ones = jnp.ones((8, s.width), f32)
        m_["ST"][0:8, :] = dot(ones, scaled, NT, precision=HIGHEST)
        m_["ST"][8:16, :] = dot(ones, scaled * xhat, NT, precision=HIGHEST)
        for k, where in enumerate(stat_where):
            go(m_["ST"], m_["STR"].at[k], sem_st + k, where)
        own_g = G[lanes(zl, s.rows), lanes(ft, s.width)].astype(f32)
        rows = [
            jnp.sum(ngrad * xhat, 0, keepdims=True),
            jnp.sum(ngrad, 0, keepdims=True),
            jnp.sum(own_g, 0, keepdims=True),
        ]
        sv = m_["SV"]
        sv[...] = jnp.zeros_like(sv)
        for k, row in enumerate(rows):
            for j in range(2):
                sv[2 * k + j : 2 * k + j + 1, :] = row[:, j * 128 : (j + 1) * 128]
        for k in range(3):
            sv[pl.ds(6 + 2 * k + zl, 1), :] = m_["QBG"][0:1, k * hf : (k + 1) * hf]
        for j in range(s.hidden // 128):
            sv[pl.ds(12 + zl * (s.hidden // 128) + j, 1), :] = m_["UBG"][0:1, j * 128 : (j + 1) * 128]

    sem_sv = new(7)
    sv_where = [device(d) for d in (1, 2, 3)] + [device(d, fx=True) for d in (0, 1, 2, 3)]

    def small_send():
        for k, where in enumerate(sv_where):
            go(m_["SV"], m_["SVR"].at[k], sem_sv + k, where)

    def small_last():
        total = m_["SV"][...]
        for k, where in enumerate(sv_where):
            arrived(m_["SVR"].at[k], sem_sv + k, where)
            total = total + m_["SVR"][k]
        o_small[...] = total

    def input_last():
        total = m_["ST"][...]
        for k, where in enumerate(stat_where):
            arrived(m_["STR"].at[k], sem_st + k, where)
            total = total + m_["STR"][k]
        spread = jnp.full((8, s.width), 1.0 / (8.0 * s.model), f32)
        mean1 = dot(total[0:8, :], spread, TN, precision=HIGHEST)
        mean2 = dot(total[8:16, :], spread, TN, precision=HIGHEST)
        gain, xhat = own_parts()
        own_g = G[lanes(zl, s.rows), lanes(ft, s.width)].astype(f32)
        scaled = m_["NGF"][...] * gain
        inv = IV[lanes(zl, s.rows), :]
        o_inp[...] = (own_g + inv * (scaled - mean1 - xhat * mean2)).astype(bf16)

    act_own(TOK, tok_at, "z")
    act_own(GRD, grd_at, "y")
    w_z(QKV, 1)
    w_own(DOWN)
    w_z(OUT, 2)
    w_z(QKV, 3)
    w_z(OUT, 3)
    w_z(QKV, 2)
    w_own(OUT)
    act_own(TOK, tok_at, "y")
    w_own(UP)
    act_own(GRD, grd_at, "z")
    act_own(TOK, tok_at, "c")
    act_own(GRD, grd_at, "c")
    w_forward(OUT, 2)
    w_relay(QKV)
    w_z(UP, 3)
    w_forward(QKV, 1)
    act_arrive(TOK, tok_at, 0)
    act_arrive(TOK, tok_at, 1)
    w_own(QKV)
    w_forward(QKV, 3)
    w_z(OUT, 1)
    w_z(UP, 2)
    w_relay(OUT)
    w_z(DOWN, 1)
    act_arrive(TOK, tok_at, 2)
    w_forward(QKV, 2)
    w_z(DOWN, 3)
    act_arrive(GRD, grd_at, 1)
    act_arrive(GRD, grd_at, 0)
    w_z(UP, 1)
    table_phase()
    act_rest(TOK, tok_at)
    norm_phase(
        beside(
            (1, w_forward, OUT, 1),
        ),
    )
    w_forward(UP, 2)
    w_rest(QKV)
    fwd_phase(
        beside(
            (2, w_forward, OUT, 3),
            (2, w_forward, DOWN, 1),
            (3, act_arrive, GRD, grd_at, 2),
            (3, w_relay, DOWN),
            (3, w_relay, UP),
            (3, w_forward, UP, 1),
            (3, w_rest, OUT),
            (3, w_z, DOWN, 2),
        ),
    )
    act_rest(GRD, grd_at)
    bwd_phase(
        beside(
            (1, w_forward, DOWN, 3),
            (3, w_forward, UP, 3),
        ),
    )
    w_forward(DOWN, 2)
    grad_phase(
        QKV,
        beside(
            (3, w_rest, UP),
        ),
    )
    up_phase()
    w_rest(DOWN)
    blk_phase(
        beside(
            (2, grad_z, QKV, 3),
        ),
    )
    act_y(BLK, 0)
    grad_z(QKV, 2)
    grad_phase(DOWN)
    act_y(BLK, 1)
    grad_z(QKV, 1)
    pre_phase(
        beside(
            (2, act_z, BLK, 0),
            (3, grad_z, DOWN, 3),
        ),
    )
    nrm_phase(
        beside(
            (2, act_z, BLK, 1),
            (3, act_y, NRM, 0),
        ),
    )
    act_y(NRM, 1)
    grad_z(DOWN, 2)
    grad_phase(OUT)
    grad_z(DOWN, 1)
    grad_phase(
        UP,
        beside(
            (1, act_y, NRM, 2),
            (1, act_z, NRM, 0),
            (1, act_y, NRM, 3),
            (3, grad_z, QKV, 0),
        ),
    )
    act_z(NRM, 1)
    grad_z(OUT, 3)
    grad_z(UP, 3)
    grad_z(UP, 2)
    grad_last(QKV)
    act_y(BLK, 3)
    grad_z(OUT, 1)
    act_y(BLK, 2)
    grad_z(UP, 1)
    act_gathered(TOK, tok_at)
    act_gathered(GRD, grd_at)
    for w in ws:
        w_sent(w)
    nrm_last()
    small_send()
    grad_z(UP, 0)
    blk_last()
    grad_z(OUT, 0)
    grad_z(DOWN, 0)
    grad_z(OUT, 2)
    grad_last(DOWN)
    input_last()
    grad_last(UP)
    for w in (QKV, OUT, DOWN):
        grad_sent(w)
    for name in (BLK, NRM):
        act_sent(name)
    small_last()
    grad_last(OUT)
    grad_sent(UP)
    for k, where in enumerate(stat_where):
        send(m_["ST"], m_["STR"].at[k], sem_st + k, where).wait_send()
    for k, where in enumerate(sv_where):
        send(m_["SV"], m_["SVR"].at[k], sem_sv + k, where).wait_send()
    assert counter[0] <= N_REMOTE


def finish_kernel(*refs):
    whole, small = refs[:6], refs[6]
    outs, (gain, shift, out_bias, qkv_bias, up_bias) = refs[7:13], refs[13:18]
    sem = refs[18]
    copies = [pltpu.make_async_copy(whole[i], outs[i], sem.at[i]) for i in range(6)]
    for copy in copies:
        copy.start()
    for k, ref in enumerate((gain, shift, out_bias)):
        ref[...] = small[2 * k : 2 * k + 2, :]
    for k in range(3):
        for j in range(2):
            ref = qkv_bias.at[k : k + 1, j * 128 : (j + 1) * 128]
            ref[...] = small[6 + 2 * k + j : 7 + 2 * k + j, :]
    up_bias[...] = small[12 : 12 + up_bias.shape[0], :]
    for copy in copies:
        copy.wait()


def on_device_fused(
    dp_count,
    feat_count,
    tokens,
    doc_lengths,
    norm_gain,
    norm_shift,
    qkv_weight,
    qkv_bias,
    omega,
    qmc_weights,
    out_weight,
    out_bias,
    up_weight,
    up_bias,
    down_weight,
    out_grad,
):
    rows, width = tokens.shape
    s = Sizes(rows, width, up_weight.shape[1], dp_count, feat_count)
    ones16 = np.kron(np.eye(4), np.full((HD, HD), 1.0 / 16.0)).astype(ml_dtypes.bfloat16)
    rep = np.tile(np.eye(HD, dtype=np.float32), (1, 4))
    shapes = scratch_list(s)
    names = list(shapes) + ["lsem", "ssem", "rsem"]
    scratch = [pltpu.VMEM(shape, kind) for shape, kind in shapes.values()]
    scratch += [
        pltpu.SemaphoreType.DMA((N_LOCAL,)),
        pltpu.SemaphoreType.DMA((N_REMOTE,)),
        pltpu.SemaphoreType.DMA((N_REMOTE,)),
    ]
    results = [
        ((rows, width), bf16),
        ((rows, width), bf16),
        ((3, s.block, width), f32),
        (up_weight.shape, f32),
        (out_weight.shape, f32),
        (down_weight.shape, f32),
        ((24, 128), f32),
    ]
    raw = pl.BlockSpec(memory_space=pl.ANY)
    vm = pl.BlockSpec(memory_space=pltpu.VMEM)
    outs = pl.pallas_call(
        functools.partial(fused_kernel, s, names),
        out_shape=tuple(pltpu.VMEM(shape, kind) for shape, kind in results),
        in_specs=[raw] * (6 + len(SMALL)),
        out_specs=[vm] * 7,
        scratch_shapes=scratch,
        compiler_params=pltpu.CompilerParams(
            collective_id=0, has_side_effects=True, vmem_limit_bytes=56 * 2**20
        ),
    )(
        tokens,
        out_grad,
        jnp.transpose(qkv_weight, (1, 0, 2)),
        up_weight,
        out_weight,
        down_weight,
        doc_lengths,
        norm_gain,
        norm_shift,
        qkv_bias,
        out_bias,
        up_bias,
        qmc_weights,
        jnp.asarray(rotary_table(rows // MB // 2)),
        jnp.asarray(rotary_swap()),
        jnp.asarray(ones16),
        jnp.asarray(dct_rows()),
        jnp.asarray(rep),
        omega,
    )
    whole = [jax.ShapeDtypeStruct(shape, kind) for shape, kind in results[:6]]
    full = up_bias.shape[0]
    short = [(width // 128, 128)] * 3 + [(3, width), (full // 128, 128)]
    done = pl.pallas_call(
        finish_kernel,
        out_shape=tuple(whole) + tuple(jax.ShapeDtypeStruct(shape, f32) for shape in short),
        in_specs=[vm] * 7,
        out_specs=[raw] * 6 + [vm] * 5,
        scratch_shapes=[pltpu.SemaphoreType.DMA((6,))],
        compiler_params=pltpu.CompilerParams(vmem_limit_bytes=4 * 2**20),
    )(*(pltpu.with_memory_space_constraint(out, pltpu.VMEM) for out in outs))
    o_blk, o_inp, o_qkv, o_up, o_out, o_down, gain, shift, out_bias_grad, qkv_bias_grad, up_bias_grad = done
    return (
        o_blk,
        o_inp,
        gain.reshape(-1),
        shift.reshape(-1),
        jnp.transpose(o_qkv, (1, 0, 2)),
        qkv_bias_grad,
        o_out,
        out_bias_grad.reshape(-1),
        o_up,
        up_bias_grad.reshape(-1),
        o_down,
    )


def solution(mesh):
    in_specs = (
        P(DP, FEAT),
        P(DP, None),
        P(FEAT),
        P(FEAT),
        P(DP, None, FEAT),
        P(None, FEAT),
        P(),
        P(),
        P(FEAT, DP),
        P(FEAT),
        P(DP, FEAT),
        P(FEAT),
        P(FEAT, DP),
        P(DP, FEAT),
    )
    out_specs = (
        P(DP, FEAT),
        P(DP, FEAT),
        P(FEAT),
        P(FEAT),
        P(DP, None, FEAT),
        P(None, FEAT),
        P(FEAT, DP),
        P(FEAT),
        P(DP, FEAT),
        P(FEAT),
        P(FEAT, DP),
    )
    dp_count, feat_count = mesh.shape[DP], mesh.shape[FEAT]
    if (dp_count, feat_count) == (8, 4):
        per_device = functools.partial(on_device_fused, dp_count, feat_count)
    else:
        per_device = on_device
    return jax.shard_map(
        per_device, mesh=mesh, in_specs=in_specs, out_specs=out_specs, check_vma=False
    )
```

```python
import functools
import math

import jax
import jax.numpy as jnp
import ml_dtypes
import numpy as np
from jax import lax
from jax.experimental import pallas as pl
from jax.experimental.pallas import tpu as pltpu
from jax.sharding import PartitionSpec as P

D = 1024
HD = 64
ROT = 16
M = 64
SPAN = 64
MB = 2
SEQS = 3


FEAT = "feat"
DP = "dp"
QKV = "qkv"
OUT = "out"
UP = "up"
DOWN = "down"
TOK = "tok"
GRD = "grd"
NRM = "nrm"
BLK = "blk"


epsilon = 1e-05
highest = lax.Precision.HIGHEST


def row_layout(lengths, row_count):
    seq_ends = jnp.cumsum(lengths)
    starts = seq_ends - lengths
    row_ids = jnp.arange(row_count, dtype=jnp.int32)
    segment = jnp.sum((row_ids[:, None] >= seq_ends[None, :]).astype(jnp.int32), 1)
    belongs = segment[:, None] == jnp.arange(lengths.shape[0], dtype=jnp.int32)[None, :]
    row_begin = jnp.sum(jnp.where(belongs, starts[None, :], 0), 1)
    return (segment, (row_ids - row_begin).astype(jnp.float32))


def rotate(vectors, positions):
    half_rot = ROT // 2
    inv_freq = jnp.exp(-jnp.arange(half_rot, dtype=jnp.float32) * (2.0 / ROT) * math.log(10000.0))
    angles = positions[:, None] * inv_freq[None, :]
    cosine = jnp.cos(angles)[:, None, :]
    sine = jnp.sin(angles)[:, None, :]
    lower_part = vectors[..., :half_rot]
    upper_part = vectors[..., half_rot:ROT]
    return jnp.concatenate(
        [
            lower_part * cosine - upper_part * sine,
            upper_part * cosine + lower_part * sine,
            vectors[..., ROT:],
        ],
        -1,
    )


def dct_table():
    ramp_vals = jnp.arange(HD, dtype=jnp.float32)
    weights_row = jnp.where(ramp_vals == 0.0, jnp.sqrt(1.0 / HD), jnp.sqrt(2.0 / HD))
    return (
        jnp.cos(math.pi * (2.0 * ramp_vals[None, :] + 1.0) * ramp_vals[:, None] / (2.0 * HD))
        * weights_row[:, None]
    )


def feature_map(vectors, positions, omega):
    turned = rotate(vectors, positions) * HD ** (-0.25)
    spectrum = jnp.einsum("rhn,kn->rhk", turned, dct_table(), precision=highest)
    scores = jnp.einsum("rhk,kj->rhj", spectrum, omega, precision=highest)
    return jnp.exp(scores - 0.5 * jnp.sum(turned * turned, -1, keepdims=True))


def both_maps(queries, keys_raw, positions, omega_used, weights_used):
    return (
        weights_used * feature_map(queries, positions, omega_used),
        feature_map(keys_raw, positions, omega_used),
    )


def gelu_exact(pre_act):
    return jax.nn.gelu(pre_act, approximate=False)


def block_masks(segment):
    nblocks = segment.shape[0] // SPAN
    blocks = segment.reshape(nblocks, SPAN)
    head_seg = blocks[:, 0]
    following = jnp.concatenate([head_seg[1:], jnp.full((1,), -1, jnp.int32)])
    carry_keep = (head_seg == following).astype(jnp.float32)
    row_gate = (blocks == head_seg[:, None]).astype(jnp.float32)
    chosen = (blocks == following[:, None]).astype(jnp.float32)
    offsets_in = jnp.arange(SPAN, dtype=jnp.int32)
    causal = offsets_in[:, None] >= offsets_in[None, :]
    same_seq = blocks[:, :, None] == blocks[:, None, :]
    block_mask = (causal[None] & same_seq).astype(jnp.float32)
    return (carry_keep, row_gate, chosen, block_mask)


def carry_chain(carry_keep, increments):

    def combine(earlier, latter):
        return (earlier[0] * latter[0], latter[0] * earlier[1] + latter[1])

    factors = jnp.broadcast_to(carry_keep[:, None, None, None], increments.shape)
    return lax.associative_scan(combine, (factors, increments))[1]


def block_states(carry_keep, picked, block_v):
    increments = jnp.einsum("bshj,bshe->bhje", picked, block_v, precision=highest)
    totals = carry_chain(carry_keep, increments)
    return jnp.concatenate([jnp.zeros_like(totals[:1]), totals[:-1]], 0)


def attend(query_feat, key_feat, extended, masks):
    carry_keep, row_gate, chosen, block_mask = masks
    nblocks, span_len = row_gate.shape
    head_count = query_feat.shape[1]
    block_q = query_feat.reshape(nblocks, span_len, head_count, -1)
    block_k = key_feat.reshape(nblocks, span_len, head_count, -1)
    block_v = extended.reshape(nblocks, span_len, head_count, -1)
    scores = (
        jnp.einsum("bthj,bshj->bhts", block_q, block_k, precision=highest) * block_mask[:, None]
    )
    inside = jnp.einsum("bhts,bshe->bthe", scores, block_v, precision=highest)
    states = block_states(carry_keep, block_k * chosen[:, :, None, None], block_v)
    outside = jnp.einsum(
        "bthj,bhje->bthe", block_q * row_gate[:, :, None, None], states, precision=highest
    )
    return (inside + outside).reshape(nblocks * span_len, head_count, -1)


def attend_back(query_feat, key_feat, extended, masks, upstream):
    carry_keep, row_gate, chosen, block_mask = masks
    nblocks, span_len = row_gate.shape
    head_count = query_feat.shape[1]
    block_q = query_feat.reshape(nblocks, span_len, head_count, -1)
    block_k = key_feat.reshape(nblocks, span_len, head_count, -1)
    block_v = extended.reshape(nblocks, span_len, head_count, -1)
    block_g = upstream.reshape(nblocks, span_len, head_count, -1)
    picked = block_k * chosen[:, :, None, None]
    gated = block_q * row_gate[:, :, None, None]
    scores = (
        jnp.einsum("bthj,bshj->bhts", block_q, block_k, precision=highest) * block_mask[:, None]
    )
    states = block_states(carry_keep, picked, block_v)
    score_grad = (
        jnp.einsum("bthe,bshe->bhts", block_g, block_v, precision=highest) * block_mask[:, None]
    )
    query_grad = jnp.einsum("bhts,bshj->bthj", score_grad, block_k, precision=highest)
    query_grad = query_grad + row_gate[:, :, None, None] * jnp.einsum(
        "bthe,bhje->bthj", block_g, states, precision=highest
    )
    key_grad = jnp.einsum("bhts,bthj->bshj", score_grad, block_q, precision=highest)
    value_grad = jnp.einsum("bhts,bthe->bshe", scores, block_g, precision=highest)
    state_grad = jnp.einsum("bthj,bthe->bhje", gated, block_g, precision=highest)
    later_total = jnp.flip(carry_chain(jnp.flip(carry_keep, 0), jnp.flip(state_grad, 0)), 0)
    incr_grad = jnp.concatenate([later_total[1:], jnp.zeros_like(later_total[:1])], 0)
    key_grad = key_grad + chosen[:, :, None, None] * jnp.einsum(
        "bhje,bshe->bshj", incr_grad, block_v, precision=highest
    )
    value_grad = value_grad + jnp.einsum("bshj,bhje->bshe", picked, incr_grad, precision=highest)
    row_total = nblocks * span_len
    return (
        query_grad.reshape(row_total, head_count, -1),
        key_grad.reshape(row_total, head_count, -1),
        value_grad.reshape(row_total, head_count, -1),
    )


def on_device(
    tokens,
    doc_lengths,
    norm_gain,
    norm_shift,
    qkv_weight,
    qkv_bias,
    omega,
    qmc_weights,
    out_weight,
    out_bias,
    up_weight,
    up_bias,
    down_weight,
    out_grad,
):
    feat_parts = lax.axis_size(FEAT)
    feat_index = lax.axis_index(FEAT)
    qkv_full, up_full, out_rows, down_rows = (
        lax.all_gather(qkv_weight, DP, axis=0, tiled=True),
        lax.all_gather(up_weight, DP, axis=0, tiled=True),
        lax.all_gather(out_weight, DP, axis=1, tiled=True),
        lax.all_gather(down_weight, DP, axis=1, tiled=True),
    )
    gain_vec = norm_gain.astype(jnp.float32)
    shift_vec = norm_shift.astype(jnp.float32)
    inputs = tokens.astype(jnp.float32)
    row_sums = lax.psum((jnp.sum(inputs, 1), jnp.sum(inputs * inputs, 1)), FEAT)
    center = row_sums[0] / D
    spread = row_sums[1] / D - center * center
    inv_root = lax.rsqrt(spread + epsilon)
    standard = (inputs - center[:, None]) * inv_root[:, None]
    normed_all = lax.all_gather(
        (standard * gain_vec + shift_vec).astype(jnp.bfloat16), FEAT, axis=1, tiled=True
    )
    local_width = tokens.shape[1]
    local_heads = local_width // HD
    feat_count = M // feat_parts
    omega_used = lax.dynamic_slice_in_dim(omega, feat_index * feat_count, feat_count, 1)
    weights_used = lax.dynamic_slice_in_dim(qmc_weights, feat_index * feat_count, feat_count, 0)
    row_count = tokens.shape[0] // MB
    qkv_bias_f = qkv_bias.astype(jnp.float32)
    up_bias_f = up_bias.astype(jnp.float32)
    out_bias_f = out_bias.astype(jnp.float32)
    block_outs = []
    saved_state = []
    for micro_idx in range(MB):
        offset = micro_idx * row_count
        normed_rows = normed_all[offset : offset + row_count]
        segment, positions = row_layout(doc_lengths[micro_idx], row_count)
        masks = block_masks(segment)
        projected = (
            jnp.einsum("rd,dcf->rcf", normed_rows, qkv_full, preferred_element_type=jnp.float32)
            + qkv_bias_f
        ).astype(jnp.bfloat16)
        pre_act = jnp.dot(normed_rows, up_full, preferred_element_type=jnp.float32) + up_bias_f
        hidden = gelu_exact(pre_act).astype(jnp.bfloat16)
        projected_used = lax.all_gather(projected, FEAT, axis=2, tiled=True)
        heads_used = projected_used.shape[2] // HD
        heads_view = projected_used.astype(jnp.float32).reshape(row_count, 3, heads_used, HD)
        queries = heads_view[:, 0]
        keys_raw = heads_view[:, 1]
        query_map, key_map = both_maps(queries, keys_raw, positions, omega_used, weights_used)
        query_feat = query_map.astype(jnp.bfloat16).astype(jnp.float32)
        key_feat = key_map.astype(jnp.bfloat16).astype(jnp.float32)
        extended = jnp.concatenate(
            [heads_view[:, 2], jnp.ones((row_count, heads_used, 1), jnp.float32)], 2
        )
        mixed = attend(query_feat, key_feat, extended, masks)
        numerator = mixed[..., :HD]
        denominator = mixed[..., HD]
        numerator, denominator = (
            lax.psum_scatter(numerator, FEAT, scatter_dimension=1, tiled=True),
            lax.psum_scatter(denominator, FEAT, scatter_dimension=1, tiled=True),
        )
        attended = (
            (numerator / denominator[..., None])
            .reshape(row_count, local_width)
            .astype(jnp.bfloat16)
        )
        branch = jnp.dot(attended, out_rows, preferred_element_type=jnp.float32)
        branch = branch + jnp.dot(hidden, down_rows, preferred_element_type=jnp.float32)
        summed = lax.psum_scatter(
            branch.astype(jnp.bfloat16), FEAT, scatter_dimension=1, tiled=True
        ).astype(jnp.float32)
        block_outs.append(
            (inputs[offset : offset + row_count] + summed + out_bias_f).astype(jnp.bfloat16)
        )
        saved_state.append(
            (
                normed_rows,
                positions,
                masks,
                pre_act,
                hidden,
                queries,
                keys_raw,
                extended,
                query_feat,
                key_feat,
                numerator,
                denominator,
                attended,
            )
        )
    qkv_acc = jnp.zeros(qkv_full.shape, jnp.float32)
    up_acc = jnp.zeros(up_full.shape, jnp.float32)
    outw_acc = jnp.zeros(out_rows.shape, jnp.float32)
    down_acc = jnp.zeros(down_rows.shape, jnp.float32)
    qkv_bias_acc = jnp.zeros((3, local_width), jnp.float32)
    up_bias_acc = jnp.zeros((up_full.shape[1],), jnp.float32)
    normed_grads = []
    for micro_idx in range(MB):
        offset = micro_idx * row_count
        (
            normed_rows,
            positions,
            masks,
            pre_act,
            hidden,
            queries,
            keys_raw,
            extended,
            query_feat,
            key_feat,
            numerator,
            denominator,
            attended,
        ) = saved_state[micro_idx]
        cotangent = lax.all_gather(
            out_grad[offset : offset + row_count], FEAT, axis=1, tiled=True
        )
        outw_acc = outw_acc + jnp.einsum(
            "rk,rd->kd", attended, cotangent, preferred_element_type=jnp.float32
        )
        down_acc = down_acc + jnp.einsum(
            "rk,rd->kd", hidden, cotangent, preferred_element_type=jnp.float32
        )
        att_grad = jnp.einsum("rd,kd->rk", cotangent, out_rows, preferred_element_type=jnp.float32)
        hidden_grad = jnp.einsum(
            "rd,kd->rk", cotangent, down_rows, preferred_element_type=jnp.float32
        )
        _, gelu_pull = jax.vjp(gelu_exact, pre_act)
        pre_grad = gelu_pull(hidden_grad)[0].astype(jnp.bfloat16)
        up_acc = up_acc + jnp.einsum(
            "rd,rk->dk", normed_rows, pre_grad, preferred_element_type=jnp.float32
        )
        up_bias_acc = up_bias_acc + jnp.sum(pre_grad.astype(jnp.float32), 0)
        att_grad = att_grad.reshape(row_count, local_heads, HD)
        numer_grad = (att_grad / denominator[..., None]).astype(jnp.bfloat16)
        denom_grad = (-jnp.sum(att_grad * numerator, 2) / (denominator * denominator)).astype(
            jnp.bfloat16
        )
        numer_grad, denom_grad = (
            lax.all_gather(numer_grad, FEAT, axis=1, tiled=True),
            lax.all_gather(denom_grad, FEAT, axis=1, tiled=True),
        )
        upstream = jnp.concatenate(
            [numer_grad.astype(jnp.float32), denom_grad.astype(jnp.float32)[..., None]], 2
        )
        query_feat_grad, key_feat_grad, extended_grad = attend_back(
            query_feat, key_feat, extended, masks, upstream
        )

        def map_local(query_in, key_in):
            return both_maps(query_in, key_in, positions, omega_used, weights_used)

        _, map_pull = jax.vjp(map_local, queries, keys_raw)
        query_grad, key_grad = map_pull((query_feat_grad, key_feat_grad))
        proj_rows = jnp.stack([query_grad, key_grad, extended_grad[..., :HD]], 1).reshape(
            row_count, 3, -1
        )
        proj_rows = lax.psum_scatter(proj_rows, FEAT, scatter_dimension=2, tiled=True)
        proj_grad = proj_rows.astype(jnp.bfloat16)
        qkv_acc = qkv_acc + jnp.einsum(
            "rd,rcf->dcf", normed_rows, proj_grad, preferred_element_type=jnp.float32
        )
        qkv_bias_acc = qkv_bias_acc + jnp.sum(proj_grad.astype(jnp.float32), 0)
        normed_part = jnp.einsum(
            "rcf,dcf->rd", proj_grad, qkv_full, preferred_element_type=jnp.float32
        )
        normed_part = normed_part + jnp.einsum(
            "rk,dk->rd", pre_grad, up_full, preferred_element_type=jnp.float32
        )
        normed_grads.append(
            lax.psum_scatter(
                normed_part.astype(jnp.bfloat16), FEAT, scatter_dimension=1, tiled=True
            ).astype(jnp.float32)
        )
    normed_grad = jnp.concatenate(normed_grads, 0)
    scaled = normed_grad * gain_vec
    grad_sums = lax.psum((jnp.sum(scaled, 1), jnp.sum(scaled * standard, 1)), FEAT)
    out_grad_f = out_grad.astype(jnp.float32)
    input_grad = out_grad_f + inv_root[:, None] * (
        scaled - grad_sums[0][:, None] / D - standard * grad_sums[1][:, None] / D
    )
    gain_part = jnp.sum(normed_grad * standard, 0)
    shift_part = jnp.sum(normed_grad, 0)
    out_bias_part = jnp.sum(out_grad_f, 0)
    qkv_grad, up_grad, outw_grad, down_grad = (
        lax.psum_scatter(
            qkv_acc.astype(jnp.bfloat16), DP, scatter_dimension=0, tiled=True
        ).astype(jnp.float32),
        lax.psum_scatter(up_acc.astype(jnp.bfloat16), DP, scatter_dimension=0, tiled=True).astype(
            jnp.float32
        ),
        lax.psum_scatter(
            outw_acc.astype(jnp.bfloat16), DP, scatter_dimension=1, tiled=True
        ).astype(jnp.float32),
        lax.psum_scatter(
            down_acc.astype(jnp.bfloat16), DP, scatter_dimension=1, tiled=True
        ).astype(jnp.float32),
    )
    gain_grad, shift_grad, qkv_bias_grad, out_bias_grad, up_bias_grad = lax.psum(
        (gain_part, shift_part, qkv_bias_acc, out_bias_part, up_bias_acc), DP
    )
    return (
        jnp.concatenate(block_outs, 0),
        input_grad.astype(jnp.bfloat16),
        gain_grad,
        shift_grad,
        qkv_grad,
        qkv_bias_grad,
        outw_grad,
        out_bias_grad,
        up_grad,
        up_bias_grad,
        down_grad,
    )


MESH = pl.DeviceIdType.MESH
f32, bf16 = jnp.float32, jnp.bfloat16
NT = ((1,), (1,))
TN = ((0,), (0,))
EXTRA = 16


def dot(a, b, dims=((1,), (0,)), precision=None):
    return lax.dot_general(
        a, b, (dims, ((), ())), precision=precision, preferred_element_type=f32
    )


def rotary_table(longest):
    half_rot = ROT // 2
    inv_freq = np.exp(
        -np.arange(half_rot, dtype=np.float32)
        * np.float32(2.0 / ROT)
        * np.float32(math.log(10000.0))
    ).astype(np.float32)
    angles = np.arange(longest, dtype=np.float32)[:, None] * inv_freq[None, :]
    cosine = np.ones((longest, HD), np.float32)
    sine = np.zeros((longest, HD), np.float32)
    for part in range(2):
        cosine[:, part * half_rot : (part + 1) * half_rot] = np.cos(angles)
        sine[:, part * half_rot : (part + 1) * half_rot] = np.sin(angles)
    rest = np.concatenate([cosine, cosine, sine, sine], 1).astype(np.float32)
    terms = []
    for _ in range(3):
        term = rest.astype(ml_dtypes.bfloat16)
        terms.append(term)
        rest = rest - term.astype(np.float32)
    return np.concatenate(terms, 0)


def rotary_swap():
    half_rot = ROT // 2
    one = np.zeros((HD, HD), np.float32)
    for i in range(half_rot):
        one[i + half_rot, i] = -1.0
        one[i, i + half_rot] = 1.0
    return np.kron(np.eye(4, dtype=np.float32), one).astype(ml_dtypes.bfloat16)


def dct_rows():
    ramp = np.arange(HD, dtype=np.float32)
    scale = np.where(ramp == 0.0, np.sqrt(1.0 / HD), np.sqrt(2.0 / HD))
    table = np.cos(math.pi * (2.0 * ramp[None, :] + 1.0) * ramp[:, None] / (2.0 * HD)) * scale[:, None]
    return np.tile(table.T, (4, 1)).astype(np.float32)


class Sizes:
    def __init__(self, rows, width, hidden, dp_count, feat_count):
        self.rows = rows
        self.width = width
        self.model = width * feat_count
        self.span = rows // MB
        self.total = 2 * rows
        self.micro = 2 * MB
        self.half = width // 2
        self.hidden = hidden // 2
        self.block = self.model // dp_count
        self.planes = dp_count // 2


def scratch_list(s):
    pl_, bl, hf, hd, tt, md = s.planes, s.block, s.half, s.hidden, s.total, s.model
    grads = {
        QKV: (3, bl, hf),
        OUT: (hf, bl),
        UP: (bl, hd),
        DOWN: (hd, bl),
    }
    shapes = dict(
        XG=((2, s.rows + EXTRA, md), bf16),
        G=((tt, md), bf16),
        WQ=((3, md, hf), bf16),
        WU=((md, hd), bf16),
        WO=((hf, md), bf16),
        WD=((hd, md), bf16),
        NB=((tt, md), bf16),
        MU=((tt, 1), f32),
        IV=((tt, 1), f32),
        A2=((2 * s.width // 2, s.width), f32),
        WB=((tt, 2 * hf), bf16),
        VB=((tt, hf), bf16),
        PHF=((tt, 2 * hf), f32),
        PHB=((tt, 2 * hf), bf16),
        ROTV=((tt, 2 * hf), f32),
        CSB=((tt, 2 * hf), f32),
        SB=((s.micro, 2, s.span, s.span), bf16),
        ND=((tt, 2 * hf), f32),
        AT=((tt, hf), bf16),
        PG=((tt, 3 * hf), bf16),
        HB=((tt, hd), bf16),
        GP=((tt, hd), f32),
        PRE=((tt, hd), bf16),
        QBG=((1, 3 * hf), f32),
        UBG=((1, hd), f32),
        NGF=((s.rows, s.width), f32),
        ST=((16, s.rows), f32),
        STR=((3, 16, s.rows), f32),
        SV=((24, 128), f32),
        SMALL=((3, max(2 * hd, 4 * s.width)), f32),
        IN_lens=((MB, SEQS), jnp.int32),
        IN_gain=((s.width,), bf16),
        IN_shift=((s.width,), bf16),
        IN_qkv_bias=((3, s.width), bf16),
        IN_out_bias=((s.width,), bf16),
        IN_up_bias=((2 * hd,), bf16),
        IN_qmc=((M,), f32),
        IN_tab=((3 * (s.span // 2), 2 * hf), bf16),
        IN_swap=((2 * hf, 2 * hf), bf16),
        IN_ones16=((2 * hf, 2 * hf), bf16),
        IN_dct=((2 * hf, HD), f32),
        IN_rep=((HD, 2 * hf), f32),
        IN_omega=((HD, M), f32),
        SVR=((7, 24, 128), f32),
    )
    for name, shape in grads.items():
        shapes["SX" + name] = ((pl_,) + shape, bf16)
        shapes["RX" + name] = ((pl_,) + shape, bf16)
        shapes["KX" + name] = ((pl_,) + shape, f32)
        shapes["ZS" + name] = ((3,) + shape, bf16)
        shapes["ZR" + name] = ((3,) + shape, bf16)
        shapes["ZM" + name] = (shape, bf16)
    for name in (BLK, NRM):
        shapes["CS" + name] = ((tt, 2 * s.width), bf16)
        shapes["CR" + name] = ((tt, 2 * s.width), bf16)
        shapes["KC" + name] = ((tt, 2 * s.width), f32)
        shapes["KY" + name] = ((tt, s.width), f32)
        shapes["YS" + name] = ((tt, s.width), bf16)
        shapes["YR" + name] = ((tt, s.width), bf16)
        shapes["AS" + name] = ((s.rows, s.width), bf16)
        shapes["AR" + name] = ((s.rows, s.width), bf16)
    return shapes


SMALL = ("lens", "gain", "shift", "qkv_bias", "out_bias", "up_bias", "qmc", "tab", "swap", "ones16", "dct", "rep", "omega")
N_LOCAL = 6 + len(SMALL)
N_REMOTE = 120


def fused_kernel(s, names, *refs):
    (tok, grd, wq_in, wu_in, wo_in, wd_in) = refs[:6]
    small_in = refs[6 : 6 + len(SMALL)]
    o_blk, o_inp, o_qkv, o_up, o_out, o_down, o_small = refs[6 + len(SMALL) : 13 + len(SMALL)]
    m_ = dict(zip(names, refs[13 + len(SMALL) :]))
    small, tab, swap, ones16 = m_["SMALL"], m_["IN_tab"], m_["IN_swap"], m_["IN_ones16"]
    dct, rep, omega = m_["IN_dct"], m_["IN_rep"], m_["IN_omega"]
    lsem, ssem, rsem = m_["lsem"], m_["ssem"], m_["rsem"]
    XG, G, WQ, WU, WO, WD = (m_[k] for k in ("XG", "G", "WQ", "WU", "WO", "WD"))
    NB, MU, IV = m_["NB"], m_["MU"], m_["IV"]

    dp = lax.axis_index(DP)
    ft = lax.axis_index(FEAT)
    z, x = dp // 2, dp % 2
    zl = z % 2
    y, c = ft // 2, ft % 2
    zd = (z, z + 1 - 2 * zl, (z + 2) % 4, 3 - z)
    hl = (zl, 1 - zl, zl, 1 - zl)
    inner = zl != z // 2

    def partner(d):
        if isinstance(d, int):
            return zd[d]
        return (z // 2 + d // 2) % 2 * 2 + (z + d) % 2

    counter = [0]

    def new(n=1):
        counter[0] += n
        return counter[0] - n

    def device(d=0, fx=False, fy=False, fc=False):
        return {
            DP: partner(d) * 2 + (1 - x if fx else x),
            FEAT: (1 - y if fy else y) * 2 + (1 - c if fc else c),
        }

    def send(src, dst, sem, where, arrival=None):
        copy = pltpu.make_async_remote_copy(
            src_ref=src,
            dst_ref=dst,
            send_sem=ssem.at[sem],
            recv_sem=rsem.at[sem if arrival is None else arrival],
            device_id=where,
            device_id_type=MESH,
        )
        return copy

    def go(src, dst, sem, where):
        send(src, dst, sem, where).start()

    def arrived(ref, sem, where):
        send(ref, ref, sem, where).wait_recv()

    mo = pl.multiple_of

    def lanes(index, size):
        return pl.ds(mo(index * size, size), size)

    def tok_at(b, f):
        return XG.at[b, :, lanes(f, s.width)]

    def grd_at(b, f):
        return G.at[lanes(b, s.rows), lanes(f, s.width)]

    def own_half(w, h):
        if w == QKV:
            return wq_in.at[:, :, lanes(h, s.half)]
        if w == UP:
            return wu_in.at[:, lanes(h, s.hidden)]
        if w == OUT:
            return wo_in.at[lanes(h, s.half), :]
        return wd_in.at[lanes(h, s.hidden), :]

    def weight_at(w, block):
        if w == QKV:
            return WQ.at[:, lanes(block, s.block), :]
        if w == UP:
            return WU.at[lanes(block, s.block), :]
        if w == OUT:
            return WO.at[:, lanes(block, s.block)]
        return WD.at[:, lanes(block, s.block)]

    ws = (QKV, OUT, UP, DOWN)

    local = [
        pltpu.make_async_copy(tok, XG.at[zl, pl.ds(0, s.rows), lanes(ft, s.width)], lsem.at[0]),
        pltpu.make_async_copy(grd, grd_at(zl, ft), lsem.at[1]),
    ]
    for i, w in enumerate(ws):
        local.append(pltpu.make_async_copy(own_half(w, zl), weight_at(w, dp), lsem.at[2 + i]))
    for i, name in enumerate(SMALL):
        local.append(pltpu.make_async_copy(small_in[i], m_["IN_" + name], lsem.at[6 + i]))
    for copy in local:
        copy.start()

    barrier = pltpu.get_barrier_semaphore()
    partners = [device(d) for d in (1, 2, 3)] + [device(d, fx=True) for d in (0, 1, 2, 3)]
    partners += [device(fy=True), device(fc=True), device(fy=True, fc=True)]
    for where in partners:
        pl.semaphore_signal(barrier, inc=1, device_id=where, device_id_type=MESH)
    pl.semaphore_wait(barrier, len(partners))
    local_grd, local_weight, local_table = local[1], dict(zip(ws, local[2:6])), local[-6:]
    for copy in local[:1] + local[6:-6]:
        copy.wait()

    def row_of(name):
        value = m_["IN_" + name][...].astype(f32)
        return value.reshape(1, value.shape[0])

    lens = m_["IN_lens"][...].astype(f32)
    rows = [row_of("gain"), row_of("shift")]
    for i in range(MB):
        for j in range(SEQS):
            rows.append(jnp.broadcast_to(lens[i : i + 1, j : j + 1], (1, s.width)))
    rows.append(jnp.zeros((EXTRA - len(rows), s.width), f32))
    XG[zl, s.rows : s.rows + EXTRA, lanes(ft, s.width)] = jnp.concatenate(rows, 0).astype(bf16)
    small[0:1, 0 : 2 * s.hidden] = row_of("up_bias")
    for k in range(3):
        small[1:2, k * s.width : (k + 1) * s.width] = m_["IN_qkv_bias"][k : k + 1, :].astype(f32)
    small[1:2, 3 * s.width : 4 * s.width] = row_of("out_bias")
    qmc = row_of("qmc")
    small[2:3, 0 : 2 * s.half] = jnp.concatenate([qmc, qmc, jnp.ones((1, s.half), f32)], 1)

    sem_act = {TOK: new(7), GRD: new(7)}

    def act_own(name, at, axis):
        k, where = {"c": (0, device(fc=True)), "y": (1, device(fy=True)), "z": (2, device(1))}[axis]
        go(at(zl, ft) if name == TOK else grd, at(zl, ft), sem_act[name] + k, where)

    def act_arrive(name, at, k):
        base = sem_act[name]
        fy = (1 - y) * 2 + c
        zb = 1 - zl
        if k == 0:
            arrived(at(zb, ft), base + 2, device(1))
            go(at(zb, ft), at(zb, ft), base + 3, device(fy=True))
            go(at(zb, ft), at(zb, ft), base + 4, device(fc=True))
        elif k == 1:
            arrived(at(zl, fy), base + 1, device(fy=True))
            go(at(zl, fy), at(zl, fy), base + 5, device(fc=True))
        else:
            arrived(at(zb, fy), base + 3, device(fy=True))
            go(at(zb, fy), at(zb, fy), base + 6, device(fc=True))

    def act_rest(name, at):
        base = sem_act[name]
        if name == GRD:
            local_grd.wait()
        fc = y * 2 + 1 - c
        fyc = (1 - y) * 2 + 1 - c
        for k, b, f in ((0, zl, fc), (4, 1 - zl, fc), (5, zl, fyc), (6, 1 - zl, fyc)):
            arrived(at(b, f), base + k, device(fc=True))

    def act_gathered(name, at):
        base = sem_act[name]
        fy = (1 - y) * 2 + c
        zb = 1 - zl
        to_c, to_y = device(fc=True), device(fy=True)
        for k, b, f, where in (
            (0, zl, ft, to_c),
            (1, zl, ft, to_y),
            (2, zl, ft, device(1)),
            (3, zb, ft, to_y),
            (4, zb, ft, to_c),
            (5, zl, fy, to_c),
            (6, zb, fy, to_c),
        ):
            send(at(b, f), at(b, f), base + k, where).wait_send()

    sem_z = {w: new(3) for w in ws}
    sem_x = {w: new(4) for w in ws}
    sem_r = {w: new() for w in ws}
    sem_m = {w: new() for w in ws}

    waited = set()

    def w_z(w, d):
        def start():
            go(own_half(w, hl[d]), weight_at(w, dp), sem_z[w] + d - 1, device(d))

        if d == 3:
            pl.when(inner)(start)
        else:
            start()

    def w_near(w):
        at = weight_at(w, zd[1] * 2 + x)
        arrived(at, sem_z[w], device(1))

    def relay(w):
        at = weight_at(w, zd[1] * 2 + x)
        return send(at, at, sem_r[w], device(2), sem_z[w] + 2)

    def w_relay(w):
        first = w not in waited
        waited.add(w)

        @pl.when(inner)
        def _():
            if first:
                w_near(w)
            relay(w).start()

    def w_own(w):
        go(own_half(w, zl), weight_at(w, dp), sem_x[w], device(fx=True))

    def w_forward(w, d):
        at = weight_at(w, partner(d) * 2 + x)
        if d > 1:
            arrived(at, sem_z[w] + d - 1, device(d))
        elif w in waited:
            pl.when(jnp.logical_not(inner))(lambda: w_near(w))
        else:
            waited.add(w)
            w_near(w)
        go(at, at, sem_x[w] + d, device(fx=True))

    def w_sent(w):
        for d in range(4):
            at = weight_at(w, zd[d] * 2 + x)
            send(at, at, sem_x[w] + d, device(fx=True)).wait_send()
            if d in (1, 2):
                send(own_half(w, hl[d]), weight_at(w, dp), sem_z[w] + d - 1, device(d)).wait_send()

        @pl.when(inner)
        def _():
            send(own_half(w, hl[3]), weight_at(w, dp), sem_z[w] + 2, device(3)).wait_send()
            relay(w).wait_send()

    def w_rest(w):
        local_weight[w].wait()
        for d in range(4):
            arrived(weight_at(w, zd[d] * 2 + 1 - x), sem_x[w] + d, device(fx=True))

    sem_gx = {w: new(4) for w in ws}
    sem_gz = {w: new(3) for w in ws}

    def put_grad(w, zp, mine, theirs):
        m_["KX" + w][zp] = mine
        m_["SX" + w][zp] = theirs.astype(bf16)
        src, dst = m_["SX" + w].at[zp], m_["RX" + w].at[zp]
        send(src, dst, sem_gx[w] + zp, device(fx=True)).start()

    def grad_copy(w, d):
        return send(m_["ZS" + w].at[d - 1], m_["ZR" + w].at[d - 1], sem_gz[w] + d - 1, device(d))

    def grad_pass(w):
        return send(m_["ZS" + w].at[2], m_["ZM" + w], sem_m[w], device(2))

    def grad_z(w, d):
        zp = zd[d]
        arrived(m_["RX" + w].at[zp], sem_gx[w] + zp, device(fx=True))
        both = m_["KX" + w][zp] + m_["RX" + w][zp].astype(f32)
        if d == 0:
            m_["KX" + w][zp] = both
            return
        if d == 1:

            @pl.when(inner)
            def _():
                arrived(m_["ZM" + w], sem_m[w], device(2))
                m_["ZS" + w][0] = (both + m_["ZM" + w][...].astype(f32)).astype(bf16)

            @pl.when(jnp.logical_not(inner))
            def _():
                m_["ZS" + w][0] = both.astype(bf16)

        else:
            m_["ZS" + w][d - 1] = both.astype(bf16)
        if d < 3:
            grad_copy(w, d).start()
        else:
            pl.when(inner)(lambda: grad_copy(w, 3).start())
            pl.when(jnp.logical_not(inner))(lambda: grad_pass(w).start())

    def grad_last(w):
        for d in (1, 2):
            arrived(m_["ZR" + w].at[d - 1], sem_gz[w] + d - 1, device(d))
        got = m_["ZR" + w]
        same = m_["KX" + w][z] + got[1].astype(f32)
        other = got[0].astype(f32)
        def put(half, value):
            if w == QKV:
                o_qkv[:, :, lanes(half, s.half)] = value
            elif w == UP:
                o_up[:, lanes(half, s.hidden)] = value
            elif w == OUT:
                o_out[lanes(half, s.half), :] = value
            else:
                o_down[lanes(half, s.hidden), :] = value

        put(zl, same)

        @pl.when(inner)
        def _():
            arrived(m_["ZR" + w].at[2], sem_gz[w] + 2, device(3))
            put(1 - zl, other + got[2].astype(f32))

        pl.when(jnp.logical_not(inner))(lambda: put(1 - zl, other))

    def grad_sent(w):
        for zp in range(4):
            send(m_["SX" + w].at[zp], m_["RX" + w].at[zp], sem_gx[w] + zp, device(fx=True)).wait_send()
        for d in (1, 2):
            grad_copy(w, d).wait_send()
        pl.when(inner)(lambda: grad_copy(w, 3).wait_send())
        pl.when(jnp.logical_not(inner))(lambda: grad_pass(w).wait_send())

    def pick(flag, a, b):
        return jnp.where(flag == 0, a, b)

    def halves(value, axis):
        n = value.shape[axis] // 2
        lo, hi = lax.slice_in_dim(value, 0, n, axis=axis), lax.slice_in_dim(value, n, 2 * n, axis=axis)
        return pick(x, lo, hi), pick(x, hi, lo)

    sem_c = {k: new(4) for k in (BLK, NRM)}
    sem_y = {k: new(4) for k in (BLK, NRM)}
    sem_a = {k: new(2) for k in (BLK, NRM)}

    def rows_of(i):
        block = (1 - zl) + (i // MB) * (2 * zl - 1)
        return pl.ds(mo(block * s.rows + (i % MB) * s.span, s.span), s.span)

    def act_put(name, i, value):
        r = rows_of(i)
        w_ = s.width
        v = [value[:, k * w_ : (k + 1) * w_] for k in range(4)]
        m_["KC" + name][r, 0:w_] = pick(c, v[0], v[1])
        m_["KC" + name][r, w_ : 2 * w_] = pick(c, v[2], v[3])
        m_["CS" + name][r, 0:w_] = pick(c, v[1], v[0]).astype(bf16)
        m_["CS" + name][r, w_ : 2 * w_] = pick(c, v[3], v[2]).astype(bf16)
        send(m_["CS" + name].at[r], m_["CR" + name].at[r], sem_c[name] + i, device(fc=True)).start()

    def act_y(name, i):
        r = rows_of(i)
        w_ = s.width
        arrived(m_["CR" + name].at[r], sem_c[name] + i, device(fc=True))
        both = m_["KC" + name][r, :] + m_["CR" + name][r, :].astype(f32)
        lo, hi = both[:, :w_], both[:, w_:]
        m_["KY" + name][r, :] = pick(y, lo, hi)
        m_["YS" + name][r, :] = pick(y, hi, lo).astype(bf16)
        send(m_["YS" + name].at[r], m_["YR" + name].at[r], sem_y[name] + i, device(fy=True)).start()

    def act_z(name, i):
        r = rows_of(i)
        q = pl.ds(i * s.span, s.span)
        arrived(m_["YR" + name].at[r], sem_y[name] + i, device(fy=True))
        both = m_["KY" + name][r, :] + m_["YR" + name][r, :].astype(f32)
        m_["AS" + name][q, :] = both.astype(bf16)
        go(m_["AS" + name].at[q], m_["AR" + name].at[q], sem_a[name] + i, device(1))

    def act_last(name, i):
        r = rows_of(MB + i)
        q = pl.ds(i * s.span, s.span)
        arrived(m_["YR" + name].at[r], sem_y[name] + MB + i, device(fy=True))
        arrived(m_["AR" + name].at[q], sem_a[name] + i, device(1))
        return (
            m_["KY" + name][r, :]
            + m_["YR" + name][r, :].astype(f32)
            + m_["AR" + name][q, :].astype(f32)
        )

    def act_sent(name):
        for i in range(4):
            r = rows_of(i)
            send(m_["CS" + name].at[r], m_["CR" + name].at[r], sem_c[name] + i, device(fc=True)).wait_send()
            send(m_["YS" + name].at[r], m_["YR" + name].at[r], sem_y[name] + i, device(fy=True)).wait_send()
        for i in range(MB):
            q = pl.ds(i * s.span, s.span)
            send(m_["AS" + name].at[q], m_["AR" + name].at[q], sem_a[name] + i, device(1)).wait_send()

    def beside(*steps):
        def side(i):
            for at in sorted(set(step[0] for step in steps)):

                @pl.when(i == at)
                def _():
                    for when, do, *args in steps:
                        if when == at:
                            do(*args)

        return side

    def loop(n, body, side=None):
        def step(i, carry):
            if side is not None:
                side(i)
            body(i)
            return carry

        lax.fori_loop(0, n, step, 0)

    def at_micro(m):
        return pl.ds(mo(m * s.span, s.span), s.span)

    def norm_phase(side=None):
        extra = XG[0, s.rows : s.rows + EXTRA, :].astype(f32)
        gain, shift = extra[0:1], extra[1:2]

        def body(m):
            xv = XG[m // MB, pl.ds(mo((m % MB) * s.span, s.span), s.span), :].astype(f32)
            mu = jnp.sum(xv, 1, keepdims=True) * (1.0 / s.model)
            var = jnp.sum(xv * xv, 1, keepdims=True) * (1.0 / s.model) - mu * mu
            inv = lax.rsqrt(var + epsilon)
            r = at_micro(m)
            MU[r, :] = mu
            IV[r, :] = inv
            NB[r, :] = ((xv - mu) * inv * gain + shift).astype(bf16)

        loop(s.micro, body, side)

    def masks(m):
        extra = XG[m // MB, s.rows : s.rows + EXTRA, 0 : s.span].astype(f32)
        row_id = lax.broadcasted_iota(jnp.int32, extra.shape, 0)
        first = 2 + SEQS * (m % MB)

        def length(k):
            return jnp.sum(jnp.where(row_id == first + k, extra, 0.0), 0, keepdims=True)

        end0 = length(0)
        end1 = end0 + length(1)
        t = lax.broadcasted_iota(jnp.int32, (s.span, s.span), 0).astype(f32)
        u = lax.broadcasted_iota(jnp.int32, (s.span, s.span), 1).astype(f32)
        start = jnp.where(t >= end1, end1, jnp.where(t >= end0, end0, 0.0))
        return jnp.logical_and(u <= t, u >= start), t, u, start

    def head_rows():
        lane = lax.broadcasted_iota(jnp.int32, (1, s.half), 1)
        return [jnp.where(lane // HD == h, 1.0, 0.0).astype(bf16) for h in range(2)], [
            jnp.where(lane == h * HD, 1.0, 0.0).astype(bf16) for h in range(2)
        ]

    HIGH = lax.Precision.HIGH
    HIGHEST = lax.Precision.HIGHEST
    hf = s.half

    def table_phase():
        for copy in local_table:
            copy.wait()
        wide = dot(dot(dct[...], omega[...], precision=HIGHEST), rep[...], precision=HIGHEST)
        m_["A2"][...] = wide * (ones16[...].astype(f32) * (16.0 * HD ** (-0.25)))

    def fwd_phase(side=None):
        def body(m):
            r = at_micro(m)
            wq = jnp.concatenate([WQ[0], WQ[1], WQ[2]], 1)
            bias = jnp.concatenate(
                [small[1:2, pl.ds(mo(k * s.width + zl * hf, hf), hf)] for k in range(3)], 1
            )
            p = (dot(NB[r, :], wq) + bias).astype(bf16)
            w, v = p[:, : 2 * hf], p[:, 2 * hf :]
            m_["VB"][r, :] = v
            mask, t, u, start = masks(m)
            pos = t[:, :hf] - start[:, :hf]
            hot = jnp.where(pos == u[:, :hf], 1.0, 0.0).astype(bf16)
            cs = dot(jnp.concatenate([hot, hot, hot], 1), tab[...])
            m_["CSB"][r, :] = cs
            cc = jnp.concatenate([cs[:, :hf], cs[:, :hf]], 1)
            ss = jnp.concatenate([cs[:, hf:], cs[:, hf:]], 1)
            wf = w.astype(f32)
            rot = wf * cc + dot(w, swap[...]) * ss
            m_["ROTV"][r, :] = rot
            score = dot(rot, m_["A2"][...], precision=HIGH)
            norm2 = dot(wf * wf, ones16[...].astype(f32), precision=HIGH)
            ph = jnp.exp(score - norm2) * small[2:3, 0 : 2 * hf]
            m_["PHF"][r, :] = ph
            pb = ph.astype(bf16)
            m_["PHB"][r, :] = pb
            hm, _ = head_rows()
            acc = jnp.zeros((s.span, 2 * hf), f32)
            for h in range(2):
                sc = dot(pb[:, :hf] * hm[h], pb[:, hf:], NT)
                sm = jnp.where(mask, sc, 0.0).astype(bf16)
                m_["SB"][m, h] = sm
                rhs = jnp.concatenate([v * hm[h], jnp.broadcast_to(hm[h], v.shape)], 1)
                acc = acc + dot(sm, rhs)
            m_["ND"][r, :] = acc
            m_["AT"][r, :] = (acc[:, :hf] / acc[:, hf:]).astype(bf16)

        loop(s.micro, body, side)

    def bwd_phase(side=None):
        m_["QBG"][...] = jnp.zeros_like(m_["QBG"])

        def body(m):
            r = at_micro(m)
            mask = masks(m)[0]
            hm, hot = head_rows()
            ag = dot(G[r, :], WO[...], NT)
            nd = m_["ND"][r, :]
            num, den = nd[:, :hf], nd[:, hf:]
            ng = (ag / den).astype(bf16)
            sums = dot(ag * num, ones16[0:hf, 0:hf].astype(f32), precision=HIGH) * 16.0
            dg = (-sums / (den * den)).astype(bf16)
            v = m_["VB"][r, :]
            pb = m_["PHB"][r, :]
            v1 = jnp.concatenate([v, jnp.ones(v.shape, bf16)], 1)
            dq = dk = dv = jnp.zeros((s.span, hf), f32)
            for h in range(2):
                e = dot(jnp.concatenate([ng * hm[h], dg * hot[h]], 1), v1, NT)
                em = jnp.where(mask, e, 0.0).astype(bf16)
                dq = dq + dot(em, pb[:, hf:] * hm[h])
                dk = dk + dot(em, pb[:, :hf] * hm[h], TN)
                dv = dv + dot(m_["SB"][m, h], ng * hm[h], TN)
            dph = jnp.concatenate([dq, dk], 1) * m_["PHF"][r, :]
            rot = m_["ROTV"][r, :]
            both = dot(dph, ones16[...].astype(f32), precision=HIGH) * 2.0
            drot = dot(dph, m_["A2"][...], NT, precision=HIGH) - rot * both
            cs = m_["CSB"][r, :]
            cc = jnp.concatenate([cs[:, :hf], cs[:, :hf]], 1)
            ss = jnp.concatenate([cs[:, hf:], cs[:, hf:]], 1)
            dw = drot * cc + dot(drot * ss, swap[...].astype(f32), NT, precision=HIGH)
            pg = jnp.concatenate([dw, dv], 1).astype(bf16)
            m_["PG"][r, :] = pg
            m_["QBG"][...] += jnp.sum(pg.astype(f32), 0, keepdims=True)

        loop(s.micro, body, side)

    def up_phase(side=None):
        bias = small[0:1, lanes(zl, s.hidden)]

        def body(m):
            r = at_micro(m)
            pre = dot(NB[r, :], WU[...]) + bias
            cdf = 0.5 * (1.0 + lax.erf(pre * math.sqrt(0.5)))
            m_["HB"][r, :] = (pre * cdf).astype(bf16)
            m_["GP"][r, :] = cdf + pre * jnp.exp(-0.5 * pre * pre) * (1.0 / math.sqrt(2.0 * math.pi))

        loop(s.micro, body, side)

    def pre_phase(side=None):
        m_["UBG"][...] = jnp.zeros_like(m_["UBG"])

        def body(m):
            r = at_micro(m)
            pre = (dot(G[r, :], WD[...], NT) * m_["GP"][r, :]).astype(bf16)
            m_["PRE"][r, :] = pre
            m_["UBG"][...] += jnp.sum(pre.astype(f32), 0, keepdims=True)

        loop(s.micro, body, side)

    def nrm_phase(side=None):
        def body(i):
            r = rows_of(i)
            wq = jnp.concatenate([WQ[0], WQ[1], WQ[2]], 1)
            act_put(NRM, i, dot(m_["PG"][r, :], wq, NT) + dot(m_["PRE"][r, :], WU[...], NT))

        loop(4, body, side)

    def blk_phase(side=None):
        def body(i):
            r = rows_of(i)
            act_put(BLK, i, dot(m_["AT"][r, :], WO[...]) + dot(m_["HB"][r, :], WD[...]))

        loop(4, body, side)

    two = 2 * s.block

    def grad_phase(w, side=None):
        def body(i):
            zp = partner(3 - i)
            cols = lanes(zp, two)
            if w == QKV:
                value = dot(NB[:, cols], m_["PG"][...], TN)
                mine, theirs = halves(value, 0)
                mine = jnp.stack([mine[:, k * hf : (k + 1) * hf] for k in range(3)], 0)
                theirs = jnp.stack([theirs[:, k * hf : (k + 1) * hf] for k in range(3)], 0)
            elif w == UP:
                mine, theirs = halves(dot(NB[:, cols], m_["PRE"][...], TN), 0)
            elif w == OUT:
                mine, theirs = halves(dot(m_["AT"][...], G[:, cols], TN), 1)
            else:
                mine, theirs = halves(dot(m_["HB"][...], G[:, cols], TN), 1)
            put_grad(w, zp, mine, theirs)

        loop(s.planes, body, side)

    def out_rows(i):
        return pl.ds(i * s.span, s.span)

    def blk_last():
        for i in range(MB):
            own = XG[zl, i * s.span : (i + 1) * s.span, lanes(ft, s.width)].astype(f32)
            bias = small[1:2, 3 * s.width : 4 * s.width]
            o_blk[out_rows(i), :] = (own + act_last(BLK, i) + bias).astype(bf16)

    sem_st = new(3)
    stat_where = [device(fc=True), device(fy=True), device(fy=True, fc=True)]

    def own_parts():
        extra = XG[0, s.rows : s.rows + EXTRA, lanes(ft, s.width)].astype(f32)
        r = lanes(zl, s.rows)
        own = XG[zl, 0 : s.rows, lanes(ft, s.width)].astype(f32)
        xhat = (own - MU[r, :]) * IV[r, :]
        return extra[0:1], xhat

    def nrm_last():
        for i in range(MB):
            m_["NGF"][out_rows(i), :] = act_last(NRM, i)
        gain, xhat = own_parts()
        ngrad = m_["NGF"][...]
        scaled = ngrad * gain
        ones = jnp.ones((8, s.width), f32)
        m_["ST"][0:8, :] = dot(ones, scaled, NT, precision=HIGHEST)
        m_["ST"][8:16, :] = dot(ones, scaled * xhat, NT, precision=HIGHEST)
        for k, where in enumerate(stat_where):
            go(m_["ST"], m_["STR"].at[k], sem_st + k, where)
        own_g = G[lanes(zl, s.rows), lanes(ft, s.width)].astype(f32)
        rows = [
            jnp.sum(ngrad * xhat, 0, keepdims=True),
            jnp.sum(ngrad, 0, keepdims=True),
            jnp.sum(own_g, 0, keepdims=True),
        ]
        sv = m_["SV"]
        sv[...] = jnp.zeros_like(sv)
        for k, row in enumerate(rows):
            for j in range(2):
                sv[2 * k + j : 2 * k + j + 1, :] = row[:, j * 128 : (j + 1) * 128]
        for k in range(3):
            sv[pl.ds(6 + 2 * k + zl, 1), :] = m_["QBG"][0:1, k * hf : (k + 1) * hf]
        for j in range(s.hidden // 128):
            sv[pl.ds(12 + zl * (s.hidden // 128) + j, 1), :] = m_["UBG"][0:1, j * 128 : (j + 1) * 128]

    sem_sv = new(7)
    sv_where = [device(d) for d in (1, 2, 3)] + [device(d, fx=True) for d in (0, 1, 2, 3)]

    def small_send():
        for k, where in enumerate(sv_where):
            go(m_["SV"], m_["SVR"].at[k], sem_sv + k, where)

    def small_last():
        total = m_["SV"][...]
        for k, where in enumerate(sv_where):
            arrived(m_["SVR"].at[k], sem_sv + k, where)
            total = total + m_["SVR"][k]
        o_small[...] = total

    def input_last():
        total = m_["ST"][...]
        for k, where in enumerate(stat_where):
            arrived(m_["STR"].at[k], sem_st + k, where)
            total = total + m_["STR"][k]
        spread = jnp.full((8, s.width), 1.0 / (8.0 * s.model), f32)
        mean1 = dot(total[0:8, :], spread, TN, precision=HIGHEST)
        mean2 = dot(total[8:16, :], spread, TN, precision=HIGHEST)
        gain, xhat = own_parts()
        own_g = G[lanes(zl, s.rows), lanes(ft, s.width)].astype(f32)
        scaled = m_["NGF"][...] * gain
        inv = IV[lanes(zl, s.rows), :]
        o_inp[...] = (own_g + inv * (scaled - mean1 - xhat * mean2)).astype(bf16)

    w_z(OUT, 3)
    act_own(TOK, tok_at, "z")
    w_own(QKV)
    w_own(OUT)
    act_own(TOK, tok_at, "y")
    w_z(DOWN, 3)
    w_z(OUT, 1)
    act_own(TOK, tok_at, "c")
    w_z(QKV, 2)
    w_own(UP)
    w_relay(OUT)
    act_arrive(TOK, tok_at, 1)
    w_z(DOWN, 1)
    act_arrive(TOK, tok_at, 0)
    w_z(QKV, 3)
    act_own(GRD, grd_at, "y")
    w_own(DOWN)
    w_forward(QKV, 2)
    w_z(QKV, 1)
    w_z(UP, 1)
    w_forward(OUT, 3)
    w_z(UP, 3)
    w_forward(DOWN, 1)
    w_forward(OUT, 1)
    act_own(GRD, grd_at, "z")
    w_z(UP, 2)
    w_relay(QKV)
    w_forward(QKV, 1)
    act_arrive(TOK, tok_at, 2)
    w_forward(UP, 1)
    w_forward(QKV, 3)
    act_rest(TOK, tok_at)
    w_z(OUT, 2)
    table_phase()
    w_forward(UP, 2)
    act_own(GRD, grd_at, "c")
    act_arrive(GRD, grd_at, 1)
    w_relay(UP)
    w_z(DOWN, 2)
    act_arrive(GRD, grd_at, 0)
    norm_phase(
        beside(
            (1, w_forward, OUT, 2),
            (1, w_rest, QKV),
            (2, w_relay, DOWN),
        ),
    )
    fwd_phase(
        beside(
            (1, w_forward, UP, 3),
            (3, w_forward, DOWN, 2),
        ),
    )
    act_arrive(GRD, grd_at, 2)
    w_rest(UP)
    up_phase(
        beside(
            (1, w_forward, DOWN, 3),
            (3, act_rest, GRD, grd_at),
        ),
    )
    grad_phase(DOWN)
    w_rest(DOWN)
    pre_phase(
        beside(
            (1, w_rest, OUT),
        ),
    )
    blk_phase(
        beside(
            (1, grad_z, DOWN, 3),
        ),
    )
    act_y(BLK, 0)
    grad_phase(
        UP,
        beside(
            (1, grad_z, DOWN, 2),
            (2, act_y, BLK, 1),
        ),
    )
    act_y(BLK, 2)
    grad_z(DOWN, 1)
    act_z(BLK, 0)
    bwd_phase(
        beside(
            (2, grad_z, UP, 3),
            (3, act_z, BLK, 1),
        ),
    )
    nrm_phase(
        beside(
            (2, grad_z, UP, 2),
            (3, act_y, NRM, 0),
        ),
    )
    grad_z(UP, 1)
    grad_phase(
        OUT,
        beside(
            (1, act_y, NRM, 1),
            (3, act_y, NRM, 2),
        ),
    )
    grad_phase(
        QKV,
        beside(
            (2, grad_z, OUT, 3),
            (2, act_z, NRM, 0),
            (2, grad_z, UP, 0),
            (2, act_y, NRM, 3),
            (2, act_z, NRM, 1),
            (3, grad_z, QKV, 3),
        ),
    )
    act_y(BLK, 3)
    grad_z(QKV, 2)
    grad_last(UP)
    grad_z(DOWN, 0)
    act_gathered(TOK, tok_at)
    act_gathered(GRD, grd_at)
    for w in ws:
        w_sent(w)
    nrm_last()
    grad_z(OUT, 1)
    grad_z(QKV, 1)
    grad_z(OUT, 2)
    grad_z(QKV, 0)
    small_send()
    input_last()
    grad_z(OUT, 0)
    grad_last(DOWN)
    grad_last(QKV)
    blk_last()
    for w in (QKV, OUT, DOWN):
        grad_sent(w)
    for name in (BLK, NRM):
        act_sent(name)
    grad_last(OUT)
    small_last()
    grad_sent(UP)
    for k, where in enumerate(stat_where):
        send(m_["ST"], m_["STR"].at[k], sem_st + k, where).wait_send()
    for k, where in enumerate(sv_where):
        send(m_["SV"], m_["SVR"].at[k], sem_sv + k, where).wait_send()
    assert counter[0] <= N_REMOTE


def finish_kernel(*refs):
    whole, small = refs[:6], refs[6]
    outs, (gain, shift, out_bias, qkv_bias, up_bias) = refs[7:13], refs[13:18]
    sem = refs[18]
    copies = [pltpu.make_async_copy(whole[i], outs[i], sem.at[i]) for i in range(6)]
    for copy in copies:
        copy.start()
    for k, ref in enumerate((gain, shift, out_bias)):
        ref[...] = small[2 * k : 2 * k + 2, :]
    for k in range(3):
        for j in range(2):
            ref = qkv_bias.at[k : k + 1, j * 128 : (j + 1) * 128]
            ref[...] = small[6 + 2 * k + j : 7 + 2 * k + j, :]
    up_bias[...] = small[12 : 12 + up_bias.shape[0], :]
    for copy in copies:
        copy.wait()


def on_device_fused(
    dp_count,
    feat_count,
    tokens,
    doc_lengths,
    norm_gain,
    norm_shift,
    qkv_weight,
    qkv_bias,
    omega,
    qmc_weights,
    out_weight,
    out_bias,
    up_weight,
    up_bias,
    down_weight,
    out_grad,
):
    rows, width = tokens.shape
    s = Sizes(rows, width, up_weight.shape[1], dp_count, feat_count)
    ones16 = np.kron(np.eye(4), np.full((HD, HD), 1.0 / 16.0)).astype(ml_dtypes.bfloat16)
    rep = np.tile(np.eye(HD, dtype=np.float32), (1, 4))
    shapes = scratch_list(s)
    names = list(shapes) + ["lsem", "ssem", "rsem"]
    scratch = [pltpu.VMEM(shape, kind) for shape, kind in shapes.values()]
    scratch += [
        pltpu.SemaphoreType.DMA((N_LOCAL,)),
        pltpu.SemaphoreType.DMA((N_REMOTE,)),
        pltpu.SemaphoreType.DMA((N_REMOTE,)),
    ]
    results = [
        ((rows, width), bf16),
        ((rows, width), bf16),
        ((3, s.block, width), f32),
        (up_weight.shape, f32),
        (out_weight.shape, f32),
        (down_weight.shape, f32),
        ((24, 128), f32),
    ]
    raw = pl.BlockSpec(memory_space=pl.ANY)
    vm = pl.BlockSpec(memory_space=pltpu.VMEM)
    outs = pl.pallas_call(
        functools.partial(fused_kernel, s, names),
        out_shape=tuple(pltpu.VMEM(shape, kind) for shape, kind in results),
        in_specs=[raw] * (6 + len(SMALL)),
        out_specs=[vm] * 7,
        scratch_shapes=scratch,
        compiler_params=pltpu.CompilerParams(
            collective_id=0, has_side_effects=True, vmem_limit_bytes=56 * 2**20
        ),
    )(
        tokens,
        out_grad,
        jnp.transpose(qkv_weight, (1, 0, 2)),
        up_weight,
        out_weight,
        down_weight,
        doc_lengths,
        norm_gain,
        norm_shift,
        qkv_bias,
        out_bias,
        up_bias,
        qmc_weights,
        jnp.asarray(rotary_table(rows // MB // 2)),
        jnp.asarray(rotary_swap()),
        jnp.asarray(ones16),
        jnp.asarray(dct_rows()),
        jnp.asarray(rep),
        omega,
    )
    whole = [jax.ShapeDtypeStruct(shape, kind) for shape, kind in results[:6]]
    full = up_bias.shape[0]
    short = [(width // 128, 128)] * 3 + [(3, width), (full // 128, 128)]
    done = pl.pallas_call(
        finish_kernel,
        out_shape=tuple(whole) + tuple(jax.ShapeDtypeStruct(shape, f32) for shape in short),
        in_specs=[vm] * 7,
        out_specs=[raw] * 6 + [vm] * 5,
        scratch_shapes=[pltpu.SemaphoreType.DMA((6,))],
        compiler_params=pltpu.CompilerParams(vmem_limit_bytes=4 * 2**20),
    )(*(pltpu.with_memory_space_constraint(out, pltpu.VMEM) for out in outs))
    o_blk, o_inp, o_qkv, o_up, o_out, o_down, gain, shift, out_bias_grad, qkv_bias_grad, up_bias_grad = done
    return (
        o_blk,
        o_inp,
        gain.reshape(-1),
        shift.reshape(-1),
        jnp.transpose(o_qkv, (1, 0, 2)),
        qkv_bias_grad,
        o_out,
        out_bias_grad.reshape(-1),
        o_up,
        up_bias_grad.reshape(-1),
        o_down,
    )


def solution(mesh):
    in_specs = (
        P(DP, FEAT),
        P(DP, None),
        P(FEAT),
        P(FEAT),
        P(DP, None, FEAT),
        P(None, FEAT),
        P(),
        P(),
        P(FEAT, DP),
        P(FEAT),
        P(DP, FEAT),
        P(FEAT),
        P(FEAT, DP),
        P(DP, FEAT),
    )
    out_specs = (
        P(DP, FEAT),
        P(DP, FEAT),
        P(FEAT),
        P(FEAT),
        P(DP, None, FEAT),
        P(None, FEAT),
        P(FEAT, DP),
        P(FEAT),
        P(DP, FEAT),
        P(FEAT),
        P(FEAT, DP),
    )
    dp_count, feat_count = mesh.shape[DP], mesh.shape[FEAT]
    if (dp_count, feat_count) == (8, 4):
        per_device = functools.partial(on_device_fused, dp_count, feat_count)
    else:
        per_device = on_device
    return jax.shard_map(
        per_device, mesh=mesh, in_specs=in_specs, out_specs=out_specs, check_vma=False
    )
```

```python
import functools
import math

import jax
import jax.numpy as jnp
import ml_dtypes
import numpy as np
from jax import lax
from jax.experimental import pallas as pl
from jax.experimental.pallas import tpu as pltpu
from jax.sharding import PartitionSpec as P

D = 1024
HD = 64
ROT = 16
M = 64
SPAN = 64
MB = 2
SEQS = 3


FEAT = "feat"
DP = "dp"
QKV = "qkv"
OUT = "out"
UP = "up"
DOWN = "down"
TOK = "tok"
GRD = "grd"
NRM = "nrm"
BLK = "blk"


epsilon = 1e-05
highest = lax.Precision.HIGHEST


def row_layout(lengths, row_count):
    seq_ends = jnp.cumsum(lengths)
    starts = seq_ends - lengths
    row_ids = jnp.arange(row_count, dtype=jnp.int32)
    segment = jnp.sum((row_ids[:, None] >= seq_ends[None, :]).astype(jnp.int32), 1)
    belongs = segment[:, None] == jnp.arange(lengths.shape[0], dtype=jnp.int32)[None, :]
    row_begin = jnp.sum(jnp.where(belongs, starts[None, :], 0), 1)
    return (segment, (row_ids - row_begin).astype(jnp.float32))


def rotate(vectors, positions):
    half_rot = ROT // 2
    inv_freq = jnp.exp(-jnp.arange(half_rot, dtype=jnp.float32) * (2.0 / ROT) * math.log(10000.0))
    angles = positions[:, None] * inv_freq[None, :]
    cosine = jnp.cos(angles)[:, None, :]
    sine = jnp.sin(angles)[:, None, :]
    lower_part = vectors[..., :half_rot]
    upper_part = vectors[..., half_rot:ROT]
    return jnp.concatenate(
        [
            lower_part * cosine - upper_part * sine,
            upper_part * cosine + lower_part * sine,
            vectors[..., ROT:],
        ],
        -1,
    )


def dct_table():
    ramp_vals = jnp.arange(HD, dtype=jnp.float32)
    weights_row = jnp.where(ramp_vals == 0.0, jnp.sqrt(1.0 / HD), jnp.sqrt(2.0 / HD))
    return (
        jnp.cos(math.pi * (2.0 * ramp_vals[None, :] + 1.0) * ramp_vals[:, None] / (2.0 * HD))
        * weights_row[:, None]
    )


def feature_map(vectors, positions, omega):
    turned = rotate(vectors, positions) * HD ** (-0.25)
    spectrum = jnp.einsum("rhn,kn->rhk", turned, dct_table(), precision=highest)
    scores = jnp.einsum("rhk,kj->rhj", spectrum, omega, precision=highest)
    return jnp.exp(scores - 0.5 * jnp.sum(turned * turned, -1, keepdims=True))


def both_maps(queries, keys_raw, positions, omega_used, weights_used):
    return (
        weights_used * feature_map(queries, positions, omega_used),
        feature_map(keys_raw, positions, omega_used),
    )


def gelu_exact(pre_act):
    return jax.nn.gelu(pre_act, approximate=False)


def block_masks(segment):
    nblocks = segment.shape[0] // SPAN
    blocks = segment.reshape(nblocks, SPAN)
    head_seg = blocks[:, 0]
    following = jnp.concatenate([head_seg[1:], jnp.full((1,), -1, jnp.int32)])
    carry_keep = (head_seg == following).astype(jnp.float32)
    row_gate = (blocks == head_seg[:, None]).astype(jnp.float32)
    chosen = (blocks == following[:, None]).astype(jnp.float32)
    offsets_in = jnp.arange(SPAN, dtype=jnp.int32)
    causal = offsets_in[:, None] >= offsets_in[None, :]
    same_seq = blocks[:, :, None] == blocks[:, None, :]
    block_mask = (causal[None] & same_seq).astype(jnp.float32)
    return (carry_keep, row_gate, chosen, block_mask)


def carry_chain(carry_keep, increments):

    def combine(earlier, latter):
        return (earlier[0] * latter[0], latter[0] * earlier[1] + latter[1])

    factors = jnp.broadcast_to(carry_keep[:, None, None, None], increments.shape)
    return lax.associative_scan(combine, (factors, increments))[1]


def block_states(carry_keep, picked, block_v):
    increments = jnp.einsum("bshj,bshe->bhje", picked, block_v, precision=highest)
    totals = carry_chain(carry_keep, increments)
    return jnp.concatenate([jnp.zeros_like(totals[:1]), totals[:-1]], 0)


def attend(query_feat, key_feat, extended, masks):
    carry_keep, row_gate, chosen, block_mask = masks
    nblocks, span_len = row_gate.shape
    head_count = query_feat.shape[1]
    block_q = query_feat.reshape(nblocks, span_len, head_count, -1)
    block_k = key_feat.reshape(nblocks, span_len, head_count, -1)
    block_v = extended.reshape(nblocks, span_len, head_count, -1)
    scores = (
        jnp.einsum("bthj,bshj->bhts", block_q, block_k, precision=highest) * block_mask[:, None]
    )
    inside = jnp.einsum("bhts,bshe->bthe", scores, block_v, precision=highest)
    states = block_states(carry_keep, block_k * chosen[:, :, None, None], block_v)
    outside = jnp.einsum(
        "bthj,bhje->bthe", block_q * row_gate[:, :, None, None], states, precision=highest
    )
    return (inside + outside).reshape(nblocks * span_len, head_count, -1)


def attend_back(query_feat, key_feat, extended, masks, upstream):
    carry_keep, row_gate, chosen, block_mask = masks
    nblocks, span_len = row_gate.shape
    head_count = query_feat.shape[1]
    block_q = query_feat.reshape(nblocks, span_len, head_count, -1)
    block_k = key_feat.reshape(nblocks, span_len, head_count, -1)
    block_v = extended.reshape(nblocks, span_len, head_count, -1)
    block_g = upstream.reshape(nblocks, span_len, head_count, -1)
    picked = block_k * chosen[:, :, None, None]
    gated = block_q * row_gate[:, :, None, None]
    scores = (
        jnp.einsum("bthj,bshj->bhts", block_q, block_k, precision=highest) * block_mask[:, None]
    )
    states = block_states(carry_keep, picked, block_v)
    score_grad = (
        jnp.einsum("bthe,bshe->bhts", block_g, block_v, precision=highest) * block_mask[:, None]
    )
    query_grad = jnp.einsum("bhts,bshj->bthj", score_grad, block_k, precision=highest)
    query_grad = query_grad + row_gate[:, :, None, None] * jnp.einsum(
        "bthe,bhje->bthj", block_g, states, precision=highest
    )
    key_grad = jnp.einsum("bhts,bthj->bshj", score_grad, block_q, precision=highest)
    value_grad = jnp.einsum("bhts,bthe->bshe", scores, block_g, precision=highest)
    state_grad = jnp.einsum("bthj,bthe->bhje", gated, block_g, precision=highest)
    later_total = jnp.flip(carry_chain(jnp.flip(carry_keep, 0), jnp.flip(state_grad, 0)), 0)
    incr_grad = jnp.concatenate([later_total[1:], jnp.zeros_like(later_total[:1])], 0)
    key_grad = key_grad + chosen[:, :, None, None] * jnp.einsum(
        "bhje,bshe->bshj", incr_grad, block_v, precision=highest
    )
    value_grad = value_grad + jnp.einsum("bshj,bhje->bshe", picked, incr_grad, precision=highest)
    row_total = nblocks * span_len
    return (
        query_grad.reshape(row_total, head_count, -1),
        key_grad.reshape(row_total, head_count, -1),
        value_grad.reshape(row_total, head_count, -1),
    )


def on_device(
    tokens,
    doc_lengths,
    norm_gain,
    norm_shift,
    qkv_weight,
    qkv_bias,
    omega,
    qmc_weights,
    out_weight,
    out_bias,
    up_weight,
    up_bias,
    down_weight,
    out_grad,
):
    feat_parts = lax.axis_size(FEAT)
    feat_index = lax.axis_index(FEAT)
    qkv_full, up_full, out_rows, down_rows = (
        lax.all_gather(qkv_weight, DP, axis=0, tiled=True),
        lax.all_gather(up_weight, DP, axis=0, tiled=True),
        lax.all_gather(out_weight, DP, axis=1, tiled=True),
        lax.all_gather(down_weight, DP, axis=1, tiled=True),
    )
    gain_vec = norm_gain.astype(jnp.float32)
    shift_vec = norm_shift.astype(jnp.float32)
    inputs = tokens.astype(jnp.float32)
    row_sums = lax.psum((jnp.sum(inputs, 1), jnp.sum(inputs * inputs, 1)), FEAT)
    center = row_sums[0] / D
    spread = row_sums[1] / D - center * center
    inv_root = lax.rsqrt(spread + epsilon)
    standard = (inputs - center[:, None]) * inv_root[:, None]
    normed_all = lax.all_gather(
        (standard * gain_vec + shift_vec).astype(jnp.bfloat16), FEAT, axis=1, tiled=True
    )
    local_width = tokens.shape[1]
    local_heads = local_width // HD
    feat_count = M // feat_parts
    omega_used = lax.dynamic_slice_in_dim(omega, feat_index * feat_count, feat_count, 1)
    weights_used = lax.dynamic_slice_in_dim(qmc_weights, feat_index * feat_count, feat_count, 0)
    row_count = tokens.shape[0] // MB
    qkv_bias_f = qkv_bias.astype(jnp.float32)
    up_bias_f = up_bias.astype(jnp.float32)
    out_bias_f = out_bias.astype(jnp.float32)
    block_outs = []
    saved_state = []
    for micro_idx in range(MB):
        offset = micro_idx * row_count
        normed_rows = normed_all[offset : offset + row_count]
        segment, positions = row_layout(doc_lengths[micro_idx], row_count)
        masks = block_masks(segment)
        projected = (
            jnp.einsum("rd,dcf->rcf", normed_rows, qkv_full, preferred_element_type=jnp.float32)
            + qkv_bias_f
        ).astype(jnp.bfloat16)
        pre_act = jnp.dot(normed_rows, up_full, preferred_element_type=jnp.float32) + up_bias_f
        hidden = gelu_exact(pre_act).astype(jnp.bfloat16)
        projected_used = lax.all_gather(projected, FEAT, axis=2, tiled=True)
        heads_used = projected_used.shape[2] // HD
        heads_view = projected_used.astype(jnp.float32).reshape(row_count, 3, heads_used, HD)
        queries = heads_view[:, 0]
        keys_raw = heads_view[:, 1]
        query_map, key_map = both_maps(queries, keys_raw, positions, omega_used, weights_used)
        query_feat = query_map.astype(jnp.bfloat16).astype(jnp.float32)
        key_feat = key_map.astype(jnp.bfloat16).astype(jnp.float32)
        extended = jnp.concatenate(
            [heads_view[:, 2], jnp.ones((row_count, heads_used, 1), jnp.float32)], 2
        )
        mixed = attend(query_feat, key_feat, extended, masks)
        numerator = mixed[..., :HD]
        denominator = mixed[..., HD]
        numerator, denominator = (
            lax.psum_scatter(numerator, FEAT, scatter_dimension=1, tiled=True),
            lax.psum_scatter(denominator, FEAT, scatter_dimension=1, tiled=True),
        )
        attended = (
            (numerator / denominator[..., None])
            .reshape(row_count, local_width)
            .astype(jnp.bfloat16)
        )
        branch = jnp.dot(attended, out_rows, preferred_element_type=jnp.float32)
        branch = branch + jnp.dot(hidden, down_rows, preferred_element_type=jnp.float32)
        summed = lax.psum_scatter(
            branch.astype(jnp.bfloat16), FEAT, scatter_dimension=1, tiled=True
        ).astype(jnp.float32)
        block_outs.append(
            (inputs[offset : offset + row_count] + summed + out_bias_f).astype(jnp.bfloat16)
        )
        saved_state.append(
            (
                normed_rows,
                positions,
                masks,
                pre_act,
                hidden,
                queries,
                keys_raw,
                extended,
                query_feat,
                key_feat,
                numerator,
                denominator,
                attended,
            )
        )
    qkv_acc = jnp.zeros(qkv_full.shape, jnp.float32)
    up_acc = jnp.zeros(up_full.shape, jnp.float32)
    outw_acc = jnp.zeros(out_rows.shape, jnp.float32)
    down_acc = jnp.zeros(down_rows.shape, jnp.float32)
    qkv_bias_acc = jnp.zeros((3, local_width), jnp.float32)
    up_bias_acc = jnp.zeros((up_full.shape[1],), jnp.float32)
    normed_grads = []
    for micro_idx in range(MB):
        offset = micro_idx * row_count
        (
            normed_rows,
            positions,
            masks,
            pre_act,
            hidden,
            queries,
            keys_raw,
            extended,
            query_feat,
            key_feat,
            numerator,
            denominator,
            attended,
        ) = saved_state[micro_idx]
        cotangent = lax.all_gather(
            out_grad[offset : offset + row_count], FEAT, axis=1, tiled=True
        )
        outw_acc = outw_acc + jnp.einsum(
            "rk,rd->kd", attended, cotangent, preferred_element_type=jnp.float32
        )
        down_acc = down_acc + jnp.einsum(
            "rk,rd->kd", hidden, cotangent, preferred_element_type=jnp.float32
        )
        att_grad = jnp.einsum("rd,kd->rk", cotangent, out_rows, preferred_element_type=jnp.float32)
        hidden_grad = jnp.einsum(
            "rd,kd->rk", cotangent, down_rows, preferred_element_type=jnp.float32
        )
        _, gelu_pull = jax.vjp(gelu_exact, pre_act)
        pre_grad = gelu_pull(hidden_grad)[0].astype(jnp.bfloat16)
        up_acc = up_acc + jnp.einsum(
            "rd,rk->dk", normed_rows, pre_grad, preferred_element_type=jnp.float32
        )
        up_bias_acc = up_bias_acc + jnp.sum(pre_grad.astype(jnp.float32), 0)
        att_grad = att_grad.reshape(row_count, local_heads, HD)
        numer_grad = (att_grad / denominator[..., None]).astype(jnp.bfloat16)
        denom_grad = (-jnp.sum(att_grad * numerator, 2) / (denominator * denominator)).astype(
            jnp.bfloat16
        )
        numer_grad, denom_grad = (
            lax.all_gather(numer_grad, FEAT, axis=1, tiled=True),
            lax.all_gather(denom_grad, FEAT, axis=1, tiled=True),
        )
        upstream = jnp.concatenate(
            [numer_grad.astype(jnp.float32), denom_grad.astype(jnp.float32)[..., None]], 2
        )
        query_feat_grad, key_feat_grad, extended_grad = attend_back(
            query_feat, key_feat, extended, masks, upstream
        )

        def map_local(query_in, key_in):
            return both_maps(query_in, key_in, positions, omega_used, weights_used)

        _, map_pull = jax.vjp(map_local, queries, keys_raw)
        query_grad, key_grad = map_pull((query_feat_grad, key_feat_grad))
        proj_rows = jnp.stack([query_grad, key_grad, extended_grad[..., :HD]], 1).reshape(
            row_count, 3, -1
        )
        proj_rows = lax.psum_scatter(proj_rows, FEAT, scatter_dimension=2, tiled=True)
        proj_grad = proj_rows.astype(jnp.bfloat16)
        qkv_acc = qkv_acc + jnp.einsum(
            "rd,rcf->dcf", normed_rows, proj_grad, preferred_element_type=jnp.float32
        )
        qkv_bias_acc = qkv_bias_acc + jnp.sum(proj_grad.astype(jnp.float32), 0)
        normed_part = jnp.einsum(
            "rcf,dcf->rd", proj_grad, qkv_full, preferred_element_type=jnp.float32
        )
        normed_part = normed_part + jnp.einsum(
            "rk,dk->rd", pre_grad, up_full, preferred_element_type=jnp.float32
        )
        normed_grads.append(
            lax.psum_scatter(
                normed_part.astype(jnp.bfloat16), FEAT, scatter_dimension=1, tiled=True
            ).astype(jnp.float32)
        )
    normed_grad = jnp.concatenate(normed_grads, 0)
    scaled = normed_grad * gain_vec
    grad_sums = lax.psum((jnp.sum(scaled, 1), jnp.sum(scaled * standard, 1)), FEAT)
    out_grad_f = out_grad.astype(jnp.float32)
    input_grad = out_grad_f + inv_root[:, None] * (
        scaled - grad_sums[0][:, None] / D - standard * grad_sums[1][:, None] / D
    )
    gain_part = jnp.sum(normed_grad * standard, 0)
    shift_part = jnp.sum(normed_grad, 0)
    out_bias_part = jnp.sum(out_grad_f, 0)
    qkv_grad, up_grad, outw_grad, down_grad = (
        lax.psum_scatter(
            qkv_acc.astype(jnp.bfloat16), DP, scatter_dimension=0, tiled=True
        ).astype(jnp.float32),
        lax.psum_scatter(up_acc.astype(jnp.bfloat16), DP, scatter_dimension=0, tiled=True).astype(
            jnp.float32
        ),
        lax.psum_scatter(
            outw_acc.astype(jnp.bfloat16), DP, scatter_dimension=1, tiled=True
        ).astype(jnp.float32),
        lax.psum_scatter(
            down_acc.astype(jnp.bfloat16), DP, scatter_dimension=1, tiled=True
        ).astype(jnp.float32),
    )
    gain_grad, shift_grad, qkv_bias_grad, out_bias_grad, up_bias_grad = lax.psum(
        (gain_part, shift_part, qkv_bias_acc, out_bias_part, up_bias_acc), DP
    )
    return (
        jnp.concatenate(block_outs, 0),
        input_grad.astype(jnp.bfloat16),
        gain_grad,
        shift_grad,
        qkv_grad,
        qkv_bias_grad,
        outw_grad,
        out_bias_grad,
        up_grad,
        up_bias_grad,
        down_grad,
    )


MESH = pl.DeviceIdType.MESH
f32, bf16 = jnp.float32, jnp.bfloat16
NT = ((1,), (1,))
TN = ((0,), (0,))
EXTRA = 16


def dot(a, b, dims=((1,), (0,)), precision=None):
    return lax.dot_general(
        a, b, (dims, ((), ())), precision=precision, preferred_element_type=f32
    )


def rotary_table(longest):
    half_rot = ROT // 2
    inv_freq = np.exp(
        -np.arange(half_rot, dtype=np.float32)
        * np.float32(2.0 / ROT)
        * np.float32(math.log(10000.0))
    ).astype(np.float32)
    angles = np.arange(longest, dtype=np.float32)[:, None] * inv_freq[None, :]
    cosine = np.ones((longest, HD), np.float32)
    sine = np.zeros((longest, HD), np.float32)
    for part in range(2):
        cosine[:, part * half_rot : (part + 1) * half_rot] = np.cos(angles)
        sine[:, part * half_rot : (part + 1) * half_rot] = np.sin(angles)
    rest = np.concatenate([cosine, cosine, sine, sine], 1).astype(np.float32)
    terms = []
    for _ in range(3):
        term = rest.astype(ml_dtypes.bfloat16)
        terms.append(term)
        rest = rest - term.astype(np.float32)
    return np.concatenate(terms, 0)


def rotary_swap():
    half_rot = ROT // 2
    one = np.zeros((HD, HD), np.float32)
    for i in range(half_rot):
        one[i + half_rot, i] = -1.0
        one[i, i + half_rot] = 1.0
    return np.kron(np.eye(4, dtype=np.float32), one).astype(ml_dtypes.bfloat16)


def dct_rows():
    ramp = np.arange(HD, dtype=np.float32)
    scale = np.where(ramp == 0.0, np.sqrt(1.0 / HD), np.sqrt(2.0 / HD))
    table = np.cos(math.pi * (2.0 * ramp[None, :] + 1.0) * ramp[:, None] / (2.0 * HD)) * scale[:, None]
    return np.tile(table.T, (4, 1)).astype(np.float32)


class Sizes:
    def __init__(self, rows, width, hidden, dp_count, feat_count):
        self.rows = rows
        self.width = width
        self.model = width * feat_count
        self.span = rows // MB
        self.total = 2 * rows
        self.micro = 2 * MB
        self.half = width // 2
        self.hidden = hidden // 2
        self.block = self.model // dp_count
        self.planes = dp_count // 2


def scratch_list(s):
    pl_, bl, hf, hd, tt, md = s.planes, s.block, s.half, s.hidden, s.total, s.model
    grads = {
        QKV: (3, bl, hf),
        OUT: (hf, bl),
        UP: (bl, hd),
        DOWN: (hd, bl),
    }
    shapes = dict(
        XG=((2, s.rows + EXTRA, md), bf16),
        G=((tt, md), bf16),
        WQ=((3, md, hf), bf16),
        WU=((md, hd), bf16),
        WO=((hf, md), bf16),
        WD=((hd, md), bf16),
        NB=((tt, md), bf16),
        MU=((tt, 1), f32),
        IV=((tt, 1), f32),
        A2=((2 * s.width // 2, s.width), f32),
        WB=((tt, 2 * hf), bf16),
        VB=((tt, hf), bf16),
        PHF=((tt, 2 * hf), f32),
        PHB=((tt, 2 * hf), bf16),
        ROTV=((tt, 2 * hf), f32),
        CSB=((tt, 2 * hf), f32),
        SB=((s.micro, 2, s.span, s.span), bf16),
        ND=((tt, 2 * hf), f32),
        AT=((tt, hf), bf16),
        PG=((tt, 3 * hf), bf16),
        HB=((tt, hd), bf16),
        GP=((tt, hd), f32),
        PRE=((tt, hd), bf16),
        QBG=((1, 3 * hf), f32),
        UBG=((1, hd), f32),
        NGF=((s.rows, s.width), f32),
        ST=((16, s.rows), f32),
        STR=((3, 16, s.rows), f32),
        SV=((24, 128), f32),
        SMALL=((3, max(2 * hd, 4 * s.width)), f32),
        IN_lens=((MB, SEQS), jnp.int32),
        IN_gain=((s.width,), bf16),
        IN_shift=((s.width,), bf16),
        IN_qkv_bias=((3, s.width), bf16),
        IN_out_bias=((s.width,), bf16),
        IN_up_bias=((2 * hd,), bf16),
        IN_qmc=((M,), f32),
        IN_tab=((3 * (s.span // 2), 2 * hf), bf16),
        IN_swap=((2 * hf, 2 * hf), bf16),
        IN_ones16=((2 * hf, 2 * hf), bf16),
        IN_dct=((2 * hf, HD), f32),
        IN_rep=((HD, 2 * hf), f32),
        IN_omega=((HD, M), f32),
        SVR=((7, 24, 128), f32),
    )
    for name, shape in grads.items():
        shapes["SX" + name] = ((pl_,) + shape, bf16)
        shapes["RX" + name] = ((pl_,) + shape, bf16)
        shapes["KX" + name] = ((pl_,) + shape, f32)
        shapes["ZS" + name] = ((3,) + shape, bf16)
        shapes["ZR" + name] = ((3,) + shape, bf16)
        shapes["ZM" + name] = (shape, bf16)
    for name in (BLK, NRM):
        shapes["CS" + name] = ((tt, 2 * s.width), bf16)
        shapes["CR" + name] = ((tt, 2 * s.width), bf16)
        shapes["KC" + name] = ((tt, 2 * s.width), f32)
        shapes["KY" + name] = ((tt, s.width), f32)
        shapes["YS" + name] = ((tt, s.width), bf16)
        shapes["YR" + name] = ((tt, s.width), bf16)
        shapes["AS" + name] = ((s.rows, s.width), bf16)
        shapes["AR" + name] = ((s.rows, s.width), bf16)
    return shapes


SMALL = ("lens", "gain", "shift", "qkv_bias", "out_bias", "up_bias", "qmc", "tab", "swap", "ones16", "dct", "rep", "omega")
N_LOCAL = 6 + len(SMALL)
N_REMOTE = 120


def fused_kernel(s, names, *refs):
    (tok, grd, wq_in, wu_in, wo_in, wd_in) = refs[:6]
    small_in = refs[6 : 6 + len(SMALL)]
    o_blk, o_inp, o_qkv, o_up, o_out, o_down, o_small = refs[6 + len(SMALL) : 13 + len(SMALL)]
    m_ = dict(zip(names, refs[13 + len(SMALL) :]))
    small, tab, swap, ones16 = m_["SMALL"], m_["IN_tab"], m_["IN_swap"], m_["IN_ones16"]
    dct, rep, omega = m_["IN_dct"], m_["IN_rep"], m_["IN_omega"]
    lsem, ssem, rsem = m_["lsem"], m_["ssem"], m_["rsem"]
    XG, G, WQ, WU, WO, WD = (m_[k] for k in ("XG", "G", "WQ", "WU", "WO", "WD"))
    NB, MU, IV = m_["NB"], m_["MU"], m_["IV"]

    dp = lax.axis_index(DP)
    ft = lax.axis_index(FEAT)
    z, x = dp // 2, dp % 2
    zl = z % 2
    y, c = ft // 2, ft % 2
    zd = (z, z + 1 - 2 * zl, (z + 2) % 4, 3 - z)
    hl = (zl, 1 - zl, zl, 1 - zl)
    inner = zl != z // 2

    def partner(d):
        if isinstance(d, int):
            return zd[d]
        return (z // 2 + d // 2) % 2 * 2 + (z + d) % 2

    counter = [0]

    def new(n=1):
        counter[0] += n
        return counter[0] - n

    def device(d=0, fx=False, fy=False, fc=False):
        return {
            DP: partner(d) * 2 + (1 - x if fx else x),
            FEAT: (1 - y if fy else y) * 2 + (1 - c if fc else c),
        }

    def send(src, dst, sem, where, arrival=None):
        copy = pltpu.make_async_remote_copy(
            src_ref=src,
            dst_ref=dst,
            send_sem=ssem.at[sem],
            recv_sem=rsem.at[sem if arrival is None else arrival],
            device_id=where,
            device_id_type=MESH,
        )
        return copy

    def go(src, dst, sem, where):
        send(src, dst, sem, where).start()

    def arrived(ref, sem, where):
        send(ref, ref, sem, where).wait_recv()

    mo = pl.multiple_of

    def lanes(index, size):
        return pl.ds(mo(index * size, size), size)

    def tok_at(b, f):
        return XG.at[b, :, lanes(f, s.width)]

    def grd_at(b, f):
        return G.at[lanes(b, s.rows), lanes(f, s.width)]

    def own_half(w, h):
        if w == QKV:
            return wq_in.at[:, :, lanes(h, s.half)]
        if w == UP:
            return wu_in.at[:, lanes(h, s.hidden)]
        if w == OUT:
            return wo_in.at[lanes(h, s.half), :]
        return wd_in.at[lanes(h, s.hidden), :]

    def weight_at(w, block):
        if w == QKV:
            return WQ.at[:, lanes(block, s.block), :]
        if w == UP:
            return WU.at[lanes(block, s.block), :]
        if w == OUT:
            return WO.at[:, lanes(block, s.block)]
        return WD.at[:, lanes(block, s.block)]

    ws = (QKV, OUT, UP, DOWN)

    local = [
        pltpu.make_async_copy(tok, XG.at[zl, pl.ds(0, s.rows), lanes(ft, s.width)], lsem.at[0]),
        pltpu.make_async_copy(grd, grd_at(zl, ft), lsem.at[1]),
    ]
    for i, w in enumerate(ws):
        local.append(pltpu.make_async_copy(own_half(w, zl), weight_at(w, dp), lsem.at[2 + i]))
    for i, name in enumerate(SMALL):
        local.append(pltpu.make_async_copy(small_in[i], m_["IN_" + name], lsem.at[6 + i]))
    for copy in local:
        copy.start()

    barrier = pltpu.get_barrier_semaphore()
    partners = [device(d) for d in (1, 2, 3)] + [device(d, fx=True) for d in (0, 1, 2, 3)]
    partners += [device(fy=True), device(fc=True), device(fy=True, fc=True)]
    for where in partners:
        pl.semaphore_signal(barrier, inc=1, device_id=where, device_id_type=MESH)
    pl.semaphore_wait(barrier, len(partners))
    local_grd, local_weight, local_table = local[1], dict(zip(ws, local[2:6])), local[-6:]
    for copy in local[:1] + local[6:-6]:
        copy.wait()

    def row_of(name):
        value = m_["IN_" + name][...].astype(f32)
        return value.reshape(1, value.shape[0])

    lens = m_["IN_lens"][...].astype(f32)
    rows = [row_of("gain"), row_of("shift")]
    for i in range(MB):
        for j in range(SEQS):
            rows.append(jnp.broadcast_to(lens[i : i + 1, j : j + 1], (1, s.width)))
    rows.append(jnp.zeros((EXTRA - len(rows), s.width), f32))
    XG[zl, s.rows : s.rows + EXTRA, lanes(ft, s.width)] = jnp.concatenate(rows, 0).astype(bf16)
    small[0:1, 0 : 2 * s.hidden] = row_of("up_bias")
    for k in range(3):
        small[1:2, k * s.width : (k + 1) * s.width] = m_["IN_qkv_bias"][k : k + 1, :].astype(f32)
    small[1:2, 3 * s.width : 4 * s.width] = row_of("out_bias")
    qmc = row_of("qmc")
    small[2:3, 0 : 2 * s.half] = jnp.concatenate([qmc, qmc, jnp.ones((1, s.half), f32)], 1)

    sem_act = {TOK: new(7), GRD: new(7)}

    def act_own(name, at, axis):
        k, where = {"c": (0, device(fc=True)), "y": (1, device(fy=True)), "z": (2, device(1))}[axis]
        go(at(zl, ft) if name == TOK else grd, at(zl, ft), sem_act[name] + k, where)

    def act_arrive(name, at, k):
        base = sem_act[name]
        fy = (1 - y) * 2 + c
        zb = 1 - zl
        if k == 0:
            arrived(at(zb, ft), base + 2, device(1))
            go(at(zb, ft), at(zb, ft), base + 3, device(fy=True))
            go(at(zb, ft), at(zb, ft), base + 4, device(fc=True))
        elif k == 1:
            arrived(at(zl, fy), base + 1, device(fy=True))
            go(at(zl, fy), at(zl, fy), base + 5, device(fc=True))
        else:
            arrived(at(zb, fy), base + 3, device(fy=True))
            go(at(zb, fy), at(zb, fy), base + 6, device(fc=True))

    def act_rest(name, at):
        base = sem_act[name]
        if name == GRD:
            local_grd.wait()
        fc = y * 2 + 1 - c
        fyc = (1 - y) * 2 + 1 - c
        for k, b, f in ((0, zl, fc), (4, 1 - zl, fc), (5, zl, fyc), (6, 1 - zl, fyc)):
            arrived(at(b, f), base + k, device(fc=True))

    def act_gathered(name, at):
        base = sem_act[name]
        fy = (1 - y) * 2 + c
        zb = 1 - zl
        to_c, to_y = device(fc=True), device(fy=True)
        for k, b, f, where in (
            (0, zl, ft, to_c),
            (1, zl, ft, to_y),
            (2, zl, ft, device(1)),
            (3, zb, ft, to_y),
            (4, zb, ft, to_c),
            (5, zl, fy, to_c),
            (6, zb, fy, to_c),
        ):
            send(at(b, f), at(b, f), base + k, where).wait_send()

    sem_z = {w: new(3) for w in ws}
    sem_x = {w: new(4) for w in ws}
    sem_r = {w: new() for w in ws}
    sem_m = {w: new() for w in ws}

    waited = set()

    def w_z(w, d):
        def start():
            go(own_half(w, hl[d]), weight_at(w, dp), sem_z[w] + d - 1, device(d))

        if d == 3:
            pl.when(inner)(start)
        else:
            start()

    def w_near(w):
        at = weight_at(w, zd[1] * 2 + x)
        arrived(at, sem_z[w], device(1))

    def relay(w):
        at = weight_at(w, zd[1] * 2 + x)
        return send(at, at, sem_r[w], device(2), sem_z[w] + 2)

    def w_relay(w):
        first = w not in waited
        waited.add(w)

        @pl.when(inner)
        def _():
            if first:
                w_near(w)
            relay(w).start()

    def w_own(w):
        go(own_half(w, zl), weight_at(w, dp), sem_x[w], device(fx=True))

    def w_forward(w, d):
        at = weight_at(w, partner(d) * 2 + x)
        if d > 1:
            arrived(at, sem_z[w] + d - 1, device(d))
        elif w in waited:
            pl.when(jnp.logical_not(inner))(lambda: w_near(w))
        else:
            waited.add(w)
            w_near(w)
        go(at, at, sem_x[w] + d, device(fx=True))

    def w_sent(w):
        for d in range(4):
            at = weight_at(w, zd[d] * 2 + x)
            send(at, at, sem_x[w] + d, device(fx=True)).wait_send()
            if d in (1, 2):
                send(own_half(w, hl[d]), weight_at(w, dp), sem_z[w] + d - 1, device(d)).wait_send()

        @pl.when(inner)
        def _():
            send(own_half(w, hl[3]), weight_at(w, dp), sem_z[w] + 2, device(3)).wait_send()
            relay(w).wait_send()

    def w_rest(w):
        local_weight[w].wait()
        for d in range(4):
            arrived(weight_at(w, zd[d] * 2 + 1 - x), sem_x[w] + d, device(fx=True))

    sem_gx = {w: new(4) for w in ws}
    sem_gz = {w: new(3) for w in ws}

    def put_grad(w, zp, mine, theirs):
        m_["KX" + w][zp] = mine
        m_["SX" + w][zp] = theirs.astype(bf16)
        src, dst = m_["SX" + w].at[zp], m_["RX" + w].at[zp]
        send(src, dst, sem_gx[w] + zp, device(fx=True)).start()

    def grad_copy(w, d):
        return send(m_["ZS" + w].at[d - 1], m_["ZR" + w].at[d - 1], sem_gz[w] + d - 1, device(d))

    def grad_pass(w):
        return send(m_["ZS" + w].at[2], m_["ZM" + w], sem_m[w], device(2))

    def grad_z(w, d):
        zp = zd[d]
        arrived(m_["RX" + w].at[zp], sem_gx[w] + zp, device(fx=True))
        both = m_["KX" + w][zp] + m_["RX" + w][zp].astype(f32)
        if d == 0:
            m_["KX" + w][zp] = both
            return
        if d == 1:

            @pl.when(inner)
            def _():
                arrived(m_["ZM" + w], sem_m[w], device(2))
                m_["ZS" + w][0] = (both + m_["ZM" + w][...].astype(f32)).astype(bf16)

            @pl.when(jnp.logical_not(inner))
            def _():
                m_["ZS" + w][0] = both.astype(bf16)

        else:
            m_["ZS" + w][d - 1] = both.astype(bf16)
        if d < 3:
            grad_copy(w, d).start()
        else:
            pl.when(inner)(lambda: grad_copy(w, 3).start())
            pl.when(jnp.logical_not(inner))(lambda: grad_pass(w).start())

    def grad_last(w):
        for d in (1, 2):
            arrived(m_["ZR" + w].at[d - 1], sem_gz[w] + d - 1, device(d))
        got = m_["ZR" + w]
        same = m_["KX" + w][z] + got[1].astype(f32)
        other = got[0].astype(f32)
        def put(half, value):
            if w == QKV:
                o_qkv[:, :, lanes(half, s.half)] = value
            elif w == UP:
                o_up[:, lanes(half, s.hidden)] = value
            elif w == OUT:
                o_out[lanes(half, s.half), :] = value
            else:
                o_down[lanes(half, s.hidden), :] = value

        put(zl, same)

        @pl.when(inner)
        def _():
            arrived(m_["ZR" + w].at[2], sem_gz[w] + 2, device(3))
            put(1 - zl, other + got[2].astype(f32))

        pl.when(jnp.logical_not(inner))(lambda: put(1 - zl, other))

    def grad_sent(w):
        for zp in range(4):
            send(m_["SX" + w].at[zp], m_["RX" + w].at[zp], sem_gx[w] + zp, device(fx=True)).wait_send()
        for d in (1, 2):
            grad_copy(w, d).wait_send()
        pl.when(inner)(lambda: grad_copy(w, 3).wait_send())
        pl.when(jnp.logical_not(inner))(lambda: grad_pass(w).wait_send())

    def pick(flag, a, b):
        return jnp.where(flag == 0, a, b)

    def halves(value, axis):
        n = value.shape[axis] // 2
        lo, hi = lax.slice_in_dim(value, 0, n, axis=axis), lax.slice_in_dim(value, n, 2 * n, axis=axis)
        return pick(x, lo, hi), pick(x, hi, lo)

    sem_c = {k: new(4) for k in (BLK, NRM)}
    sem_y = {k: new(4) for k in (BLK, NRM)}
    sem_a = {k: new(2) for k in (BLK, NRM)}

    def rows_of(i):
        block = (1 - zl) + (i // MB) * (2 * zl - 1)
        return pl.ds(mo(block * s.rows + (i % MB) * s.span, s.span), s.span)

    def act_put(name, i, value):
        r = rows_of(i)
        w_ = s.width
        v = [value[:, k * w_ : (k + 1) * w_] for k in range(4)]
        m_["KC" + name][r, 0:w_] = pick(c, v[0], v[1])
        m_["KC" + name][r, w_ : 2 * w_] = pick(c, v[2], v[3])
        m_["CS" + name][r, 0:w_] = pick(c, v[1], v[0]).astype(bf16)
        m_["CS" + name][r, w_ : 2 * w_] = pick(c, v[3], v[2]).astype(bf16)
        send(m_["CS" + name].at[r], m_["CR" + name].at[r], sem_c[name] + i, device(fc=True)).start()

    def act_y(name, i):
        r = rows_of(i)
        w_ = s.width
        arrived(m_["CR" + name].at[r], sem_c[name] + i, device(fc=True))
        both = m_["KC" + name][r, :] + m_["CR" + name][r, :].astype(f32)
        lo, hi = both[:, :w_], both[:, w_:]
        m_["KY" + name][r, :] = pick(y, lo, hi)
        m_["YS" + name][r, :] = pick(y, hi, lo).astype(bf16)
        send(m_["YS" + name].at[r], m_["YR" + name].at[r], sem_y[name] + i, device(fy=True)).start()

    def act_z(name, i):
        r = rows_of(i)
        q = pl.ds(i * s.span, s.span)
        arrived(m_["YR" + name].at[r], sem_y[name] + i, device(fy=True))
        both = m_["KY" + name][r, :] + m_["YR" + name][r, :].astype(f32)
        m_["AS" + name][q, :] = both.astype(bf16)
        go(m_["AS" + name].at[q], m_["AR" + name].at[q], sem_a[name] + i, device(1))

    def act_last(name, i):
        r = rows_of(MB + i)
        q = pl.ds(i * s.span, s.span)
        arrived(m_["YR" + name].at[r], sem_y[name] + MB + i, device(fy=True))
        arrived(m_["AR" + name].at[q], sem_a[name] + i, device(1))
        return (
            m_["KY" + name][r, :]
            + m_["YR" + name][r, :].astype(f32)
            + m_["AR" + name][q, :].astype(f32)
        )

    def act_sent(name):
        for i in range(4):
            r = rows_of(i)
            send(m_["CS" + name].at[r], m_["CR" + name].at[r], sem_c[name] + i, device(fc=True)).wait_send()
            send(m_["YS" + name].at[r], m_["YR" + name].at[r], sem_y[name] + i, device(fy=True)).wait_send()
        for i in range(MB):
            q = pl.ds(i * s.span, s.span)
            send(m_["AS" + name].at[q], m_["AR" + name].at[q], sem_a[name] + i, device(1)).wait_send()

    def beside(*steps):
        def side(i):
            for at in sorted(set(step[0] for step in steps)):

                @pl.when(i == at)
                def _():
                    for when, do, *args in steps:
                        if when == at:
                            do(*args)

        return side

    def loop(n, body, side=None):
        def step(i, carry):
            if side is not None:
                side(i)
            body(i)
            return carry

        lax.fori_loop(0, n, step, 0)

    def at_micro(m):
        return pl.ds(mo(m * s.span, s.span), s.span)

    def norm_phase(side=None):
        extra = XG[0, s.rows : s.rows + EXTRA, :].astype(f32)
        gain, shift = extra[0:1], extra[1:2]

        def body(m):
            xv = XG[m // MB, pl.ds(mo((m % MB) * s.span, s.span), s.span), :].astype(f32)
            mu = jnp.sum(xv, 1, keepdims=True) * (1.0 / s.model)
            var = jnp.sum(xv * xv, 1, keepdims=True) * (1.0 / s.model) - mu * mu
            inv = lax.rsqrt(var + epsilon)
            r = at_micro(m)
            MU[r, :] = mu
            IV[r, :] = inv
            NB[r, :] = ((xv - mu) * inv * gain + shift).astype(bf16)

        loop(s.micro, body, side)

    def masks(m):
        extra = XG[m // MB, s.rows : s.rows + EXTRA, 0 : s.span].astype(f32)
        row_id = lax.broadcasted_iota(jnp.int32, extra.shape, 0)
        first = 2 + SEQS * (m % MB)

        def length(k):
            return jnp.sum(jnp.where(row_id == first + k, extra, 0.0), 0, keepdims=True)

        end0 = length(0)
        end1 = end0 + length(1)
        t = lax.broadcasted_iota(jnp.int32, (s.span, s.span), 0).astype(f32)
        u = lax.broadcasted_iota(jnp.int32, (s.span, s.span), 1).astype(f32)
        start = jnp.where(t >= end1, end1, jnp.where(t >= end0, end0, 0.0))
        return jnp.logical_and(u <= t, u >= start), t, u, start

    def head_rows():
        lane = lax.broadcasted_iota(jnp.int32, (1, s.half), 1)
        return [jnp.where(lane // HD == h, 1.0, 0.0).astype(bf16) for h in range(2)], [
            jnp.where(lane == h * HD, 1.0, 0.0).astype(bf16) for h in range(2)
        ]

    HIGH = lax.Precision.HIGH
    HIGHEST = lax.Precision.HIGHEST
    hf = s.half

    def table_phase():
        for copy in local_table:
            copy.wait()
        wide = dot(dot(dct[...], omega[...], precision=HIGHEST), rep[...], precision=HIGHEST)
        m_["A2"][...] = wide * (ones16[...].astype(f32) * (16.0 * HD ** (-0.25)))

    def fwd_phase(side=None):
        def body(m):
            r = at_micro(m)
            wq = jnp.concatenate([WQ[0], WQ[1], WQ[2]], 1)
            bias = jnp.concatenate(
                [small[1:2, pl.ds(mo(k * s.width + zl * hf, hf), hf)] for k in range(3)], 1
            )
            p = (dot(NB[r, :], wq) + bias).astype(bf16)
            w, v = p[:, : 2 * hf], p[:, 2 * hf :]
            m_["VB"][r, :] = v
            mask, t, u, start = masks(m)
            pos = t[:, :hf] - start[:, :hf]
            hot = jnp.where(pos == u[:, :hf], 1.0, 0.0).astype(bf16)
            cs = dot(jnp.concatenate([hot, hot, hot], 1), tab[...])
            m_["CSB"][r, :] = cs
            cc = jnp.concatenate([cs[:, :hf], cs[:, :hf]], 1)
            ss = jnp.concatenate([cs[:, hf:], cs[:, hf:]], 1)
            wf = w.astype(f32)
            rot = wf * cc + dot(w, swap[...]) * ss
            m_["ROTV"][r, :] = rot
            score = dot(rot, m_["A2"][...], precision=HIGH)
            norm2 = dot(wf * wf, ones16[...].astype(f32), precision=HIGH)
            ph = jnp.exp(score - norm2) * small[2:3, 0 : 2 * hf]
            m_["PHF"][r, :] = ph
            pb = ph.astype(bf16)
            m_["PHB"][r, :] = pb
            hm, _ = head_rows()
            acc = jnp.zeros((s.span, 2 * hf), f32)
            for h in range(2):
                sc = dot(pb[:, :hf] * hm[h], pb[:, hf:], NT)
                sm = jnp.where(mask, sc, 0.0).astype(bf16)
                m_["SB"][m, h] = sm
                rhs = jnp.concatenate([v * hm[h], jnp.broadcast_to(hm[h], v.shape)], 1)
                acc = acc + dot(sm, rhs)
            m_["ND"][r, :] = acc
            m_["AT"][r, :] = (acc[:, :hf] / acc[:, hf:]).astype(bf16)

        loop(s.micro, body, side)

    def bwd_phase(side=None):
        m_["QBG"][...] = jnp.zeros_like(m_["QBG"])

        def body(m):
            r = at_micro(m)
            mask = masks(m)[0]
            hm, hot = head_rows()
            ag = dot(G[r, :], WO[...], NT)
            nd = m_["ND"][r, :]
            num, den = nd[:, :hf], nd[:, hf:]
            ng = (ag / den).astype(bf16)
            sums = dot(ag * num, ones16[0:hf, 0:hf].astype(f32), precision=HIGH) * 16.0
            dg = (-sums / (den * den)).astype(bf16)
            v = m_["VB"][r, :]
            pb = m_["PHB"][r, :]
            v1 = jnp.concatenate([v, jnp.ones(v.shape, bf16)], 1)
            dq = dk = dv = jnp.zeros((s.span, hf), f32)
            for h in range(2):
                e = dot(jnp.concatenate([ng * hm[h], dg * hot[h]], 1), v1, NT)
                em = jnp.where(mask, e, 0.0).astype(bf16)
                dq = dq + dot(em, pb[:, hf:] * hm[h])
                dk = dk + dot(em, pb[:, :hf] * hm[h], TN)
                dv = dv + dot(m_["SB"][m, h], ng * hm[h], TN)
            dph = jnp.concatenate([dq, dk], 1) * m_["PHF"][r, :]
            rot = m_["ROTV"][r, :]
            both = dot(dph, ones16[...].astype(f32), precision=HIGH) * 2.0
            drot = dot(dph, m_["A2"][...], NT, precision=HIGH) - rot * both
            cs = m_["CSB"][r, :]
            cc = jnp.concatenate([cs[:, :hf], cs[:, :hf]], 1)
            ss = jnp.concatenate([cs[:, hf:], cs[:, hf:]], 1)
            dw = drot * cc + dot(drot * ss, swap[...].astype(f32), NT, precision=HIGH)
            pg = jnp.concatenate([dw, dv], 1).astype(bf16)
            m_["PG"][r, :] = pg
            m_["QBG"][...] += jnp.sum(pg.astype(f32), 0, keepdims=True)

        loop(s.micro, body, side)

    def up_phase(side=None):
        bias = small[0:1, lanes(zl, s.hidden)]

        def body(m):
            r = at_micro(m)
            pre = dot(NB[r, :], WU[...]) + bias
            cdf = 0.5 * (1.0 + lax.erf(pre * math.sqrt(0.5)))
            m_["HB"][r, :] = (pre * cdf).astype(bf16)
            m_["GP"][r, :] = cdf + pre * jnp.exp(-0.5 * pre * pre) * (1.0 / math.sqrt(2.0 * math.pi))

        loop(s.micro, body, side)

    def pre_phase(side=None):
        m_["UBG"][...] = jnp.zeros_like(m_["UBG"])

        def body(m):
            r = at_micro(m)
            pre = (dot(G[r, :], WD[...], NT) * m_["GP"][r, :]).astype(bf16)
            m_["PRE"][r, :] = pre
            m_["UBG"][...] += jnp.sum(pre.astype(f32), 0, keepdims=True)

        loop(s.micro, body, side)

    def nrm_phase(side=None):
        def body(i):
            r = rows_of(i)
            wq = jnp.concatenate([WQ[0], WQ[1], WQ[2]], 1)
            act_put(NRM, i, dot(m_["PG"][r, :], wq, NT) + dot(m_["PRE"][r, :], WU[...], NT))

        loop(4, body, side)

    def blk_phase(side=None):
        def body(i):
            r = rows_of(i)
            act_put(BLK, i, dot(m_["AT"][r, :], WO[...]) + dot(m_["HB"][r, :], WD[...]))

        loop(4, body, side)

    two = 2 * s.block

    def grad_phase(w, side=None):
        def body(i):
            zp = partner(3 - i)
            cols = lanes(zp, two)
            if w == QKV:
                value = dot(NB[:, cols], m_["PG"][...], TN)
                mine, theirs = halves(value, 0)
                mine = jnp.stack([mine[:, k * hf : (k + 1) * hf] for k in range(3)], 0)
                theirs = jnp.stack([theirs[:, k * hf : (k + 1) * hf] for k in range(3)], 0)
            elif w == UP:
                mine, theirs = halves(dot(NB[:, cols], m_["PRE"][...], TN), 0)
            elif w == OUT:
                mine, theirs = halves(dot(m_["AT"][...], G[:, cols], TN), 1)
            else:
                mine, theirs = halves(dot(m_["HB"][...], G[:, cols], TN), 1)
            put_grad(w, zp, mine, theirs)

        loop(s.planes, body, side)

    def out_rows(i):
        return pl.ds(i * s.span, s.span)

    def blk_last():
        for i in range(MB):
            own = XG[zl, i * s.span : (i + 1) * s.span, lanes(ft, s.width)].astype(f32)
            bias = small[1:2, 3 * s.width : 4 * s.width]
            o_blk[out_rows(i), :] = (own + act_last(BLK, i) + bias).astype(bf16)

    sem_st = new(3)
    stat_where = [device(fc=True), device(fy=True), device(fy=True, fc=True)]

    def own_parts():
        extra = XG[0, s.rows : s.rows + EXTRA, lanes(ft, s.width)].astype(f32)
        r = lanes(zl, s.rows)
        own = XG[zl, 0 : s.rows, lanes(ft, s.width)].astype(f32)
        xhat = (own - MU[r, :]) * IV[r, :]
        return extra[0:1], xhat

    def nrm_last():
        for i in range(MB):
            m_["NGF"][out_rows(i), :] = act_last(NRM, i)
        gain, xhat = own_parts()
        ngrad = m_["NGF"][...]
        scaled = ngrad * gain
        ones = jnp.ones((8, s.width), f32)
        m_["ST"][0:8, :] = dot(ones, scaled, NT, precision=HIGHEST)
        m_["ST"][8:16, :] = dot(ones, scaled * xhat, NT, precision=HIGHEST)
        for k, where in enumerate(stat_where):
            go(m_["ST"], m_["STR"].at[k], sem_st + k, where)
        own_g = G[lanes(zl, s.rows), lanes(ft, s.width)].astype(f32)
        rows = [
            jnp.sum(ngrad * xhat, 0, keepdims=True),
            jnp.sum(ngrad, 0, keepdims=True),
            jnp.sum(own_g, 0, keepdims=True),
        ]
        sv = m_["SV"]
        sv[...] = jnp.zeros_like(sv)
        for k, row in enumerate(rows):
            for j in range(2):
                sv[2 * k + j : 2 * k + j + 1, :] = row[:, j * 128 : (j + 1) * 128]
        for k in range(3):
            sv[pl.ds(6 + 2 * k + zl, 1), :] = m_["QBG"][0:1, k * hf : (k + 1) * hf]
        for j in range(s.hidden // 128):
            sv[pl.ds(12 + zl * (s.hidden // 128) + j, 1), :] = m_["UBG"][0:1, j * 128 : (j + 1) * 128]

    sem_sv = new(7)
    sv_where = [device(d) for d in (1, 2, 3)] + [device(d, fx=True) for d in (0, 1, 2, 3)]

    def small_send():
        for k, where in enumerate(sv_where):
            go(m_["SV"], m_["SVR"].at[k], sem_sv + k, where)

    def small_last():
        total = m_["SV"][...]
        for k, where in enumerate(sv_where):
            arrived(m_["SVR"].at[k], sem_sv + k, where)
            total = total + m_["SVR"][k]
        o_small[...] = total

    def input_last():
        total = m_["ST"][...]
        for k, where in enumerate(stat_where):
            arrived(m_["STR"].at[k], sem_st + k, where)
            total = total + m_["STR"][k]
        spread = jnp.full((8, s.width), 1.0 / (8.0 * s.model), f32)
        mean1 = dot(total[0:8, :], spread, TN, precision=HIGHEST)
        mean2 = dot(total[8:16, :], spread, TN, precision=HIGHEST)
        gain, xhat = own_parts()
        own_g = G[lanes(zl, s.rows), lanes(ft, s.width)].astype(f32)
        scaled = m_["NGF"][...] * gain
        inv = IV[lanes(zl, s.rows), :]
        o_inp[...] = (own_g + inv * (scaled - mean1 - xhat * mean2)).astype(bf16)

    w_own(OUT)
    act_own(TOK, tok_at, "z")
    w_z(OUT, 3)
    act_own(TOK, tok_at, "y")
    w_z(DOWN, 3)
    w_z(OUT, 1)
    act_own(TOK, tok_at, "c")
    w_z(QKV, 2)
    w_own(UP)
    w_relay(OUT)
    w_z(QKV, 3)
    w_own(QKV)
    act_arrive(TOK, tok_at, 1)
    w_z(DOWN, 1)
    act_arrive(TOK, tok_at, 0)
    w_own(DOWN)
    act_own(GRD, grd_at, "y")
    w_forward(QKV, 2)
    w_z(QKV, 1)
    w_z(UP, 1)
    w_forward(OUT, 3)
    w_z(UP, 3)
    w_forward(DOWN, 1)
    w_forward(OUT, 1)
    act_own(GRD, grd_at, "z")
    w_z(UP, 2)
    act_arrive(TOK, tok_at, 2)
    w_relay(QKV)
    w_forward(QKV, 1)
    act_own(GRD, grd_at, "c")
    w_forward(UP, 1)
    w_forward(QKV, 3)
    act_arrive(GRD, grd_at, 1)
    act_rest(TOK, tok_at)
    w_z(OUT, 2)
    table_phase()
    w_forward(UP, 2)
    w_relay(UP)
    w_z(DOWN, 2)
    act_arrive(GRD, grd_at, 0)
    norm_phase(
        beside(
            (1, w_forward, OUT, 2),
            (1, w_rest, QKV),
            (2, w_relay, DOWN),
        ),
    )
    fwd_phase(
        beside(
            (1, w_forward, UP, 3),
            (3, w_forward, DOWN, 2),
        ),
    )
    act_arrive(GRD, grd_at, 2)
    w_rest(UP)
    up_phase(
        beside(
            (1, w_forward, DOWN, 3),
        ),
    )
    act_rest(GRD, grd_at)
    grad_phase(DOWN)
    w_rest(DOWN)
    pre_phase()
    w_rest(OUT)
    blk_phase(
        beside(
            (1, grad_z, DOWN, 3),
        ),
    )
    act_y(BLK, 0)
    grad_phase(
        UP,
        beside(
            (1, grad_z, DOWN, 2),
        ),
    )
    act_y(BLK, 2)
    grad_z(DOWN, 1)
    act_z(BLK, 0)
    act_y(BLK, 1)
    bwd_phase(
        beside(
            (2, grad_z, UP, 3),
            (3, act_z, BLK, 1),
        ),
    )
    nrm_phase(
        beside(
            (2, grad_z, UP, 2),
            (3, act_y, NRM, 0),
        ),
    )
    grad_z(UP, 1)
    grad_phase(
        OUT,
        beside(
            (1, act_y, NRM, 1),
            (3, act_y, NRM, 2),
        ),
    )
    grad_phase(
        QKV,
        beside(
            (2, grad_z, OUT, 3),
            (2, act_z, NRM, 0),
            (2, grad_z, UP, 0),
            (2, act_y, NRM, 3),
            (2, act_z, NRM, 1),
            (3, grad_z, QKV, 3),
        ),
    )
    act_y(BLK, 3)
    grad_z(QKV, 2)
    grad_last(UP)
    grad_z(DOWN, 0)
    act_gathered(TOK, tok_at)
    act_gathered(GRD, grd_at)
    for w in ws:
        w_sent(w)
    nrm_last()
    grad_z(OUT, 1)
    grad_z(QKV, 1)
    grad_z(OUT, 2)
    grad_z(QKV, 0)
    small_send()
    input_last()
    grad_z(OUT, 0)
    grad_last(DOWN)
    grad_last(QKV)
    blk_last()
    for w in (QKV, OUT, DOWN):
        grad_sent(w)
    for name in (BLK, NRM):
        act_sent(name)
    grad_last(OUT)
    small_last()
    grad_sent(UP)
    for k, where in enumerate(stat_where):
        send(m_["ST"], m_["STR"].at[k], sem_st + k, where).wait_send()
    for k, where in enumerate(sv_where):
        send(m_["SV"], m_["SVR"].at[k], sem_sv + k, where).wait_send()
    assert counter[0] <= N_REMOTE


def finish_kernel(*refs):
    whole, small = refs[:6], refs[6]
    outs, (gain, shift, out_bias, qkv_bias, up_bias) = refs[7:13], refs[13:18]
    sem = refs[18]
    copies = [pltpu.make_async_copy(whole[i], outs[i], sem.at[i]) for i in range(6)]
    for copy in copies:
        copy.start()
    for k, ref in enumerate((gain, shift, out_bias)):
        ref[...] = small[2 * k : 2 * k + 2, :]
    for k in range(3):
        for j in range(2):
            ref = qkv_bias.at[k : k + 1, j * 128 : (j + 1) * 128]
            ref[...] = small[6 + 2 * k + j : 7 + 2 * k + j, :]
    up_bias[...] = small[12 : 12 + up_bias.shape[0], :]
    for copy in copies:
        copy.wait()


def on_device_fused(
    dp_count,
    feat_count,
    tokens,
    doc_lengths,
    norm_gain,
    norm_shift,
    qkv_weight,
    qkv_bias,
    omega,
    qmc_weights,
    out_weight,
    out_bias,
    up_weight,
    up_bias,
    down_weight,
    out_grad,
):
    rows, width = tokens.shape
    s = Sizes(rows, width, up_weight.shape[1], dp_count, feat_count)
    ones16 = np.kron(np.eye(4), np.full((HD, HD), 1.0 / 16.0)).astype(ml_dtypes.bfloat16)
    rep = np.tile(np.eye(HD, dtype=np.float32), (1, 4))
    shapes = scratch_list(s)
    names = list(shapes) + ["lsem", "ssem", "rsem"]
    scratch = [pltpu.VMEM(shape, kind) for shape, kind in shapes.values()]
    scratch += [
        pltpu.SemaphoreType.DMA((N_LOCAL,)),
        pltpu.SemaphoreType.DMA((N_REMOTE,)),
        pltpu.SemaphoreType.DMA((N_REMOTE,)),
    ]
    results = [
        ((rows, width), bf16),
        ((rows, width), bf16),
        ((3, s.block, width), f32),
        (up_weight.shape, f32),
        (out_weight.shape, f32),
        (down_weight.shape, f32),
        ((24, 128), f32),
    ]
    raw = pl.BlockSpec(memory_space=pl.ANY)
    vm = pl.BlockSpec(memory_space=pltpu.VMEM)
    outs = pl.pallas_call(
        functools.partial(fused_kernel, s, names),
        out_shape=tuple(pltpu.VMEM(shape, kind) for shape, kind in results),
        in_specs=[raw] * (6 + len(SMALL)),
        out_specs=[vm] * 7,
        scratch_shapes=scratch,
        compiler_params=pltpu.CompilerParams(
            collective_id=0, has_side_effects=True, vmem_limit_bytes=56 * 2**20
        ),
    )(
        tokens,
        out_grad,
        jnp.transpose(qkv_weight, (1, 0, 2)),
        up_weight,
        out_weight,
        down_weight,
        doc_lengths,
        norm_gain,
        norm_shift,
        qkv_bias,
        out_bias,
        up_bias,
        qmc_weights,
        jnp.asarray(rotary_table(rows // MB // 2)),
        jnp.asarray(rotary_swap()),
        jnp.asarray(ones16),
        jnp.asarray(dct_rows()),
        jnp.asarray(rep),
        omega,
    )
    whole = [jax.ShapeDtypeStruct(shape, kind) for shape, kind in results[:6]]
    full = up_bias.shape[0]
    short = [(width // 128, 128)] * 3 + [(3, width), (full // 128, 128)]
    done = pl.pallas_call(
        finish_kernel,
        out_shape=tuple(whole) + tuple(jax.ShapeDtypeStruct(shape, f32) for shape in short),
        in_specs=[vm] * 7,
        out_specs=[raw] * 6 + [vm] * 5,
        scratch_shapes=[pltpu.SemaphoreType.DMA((6,))],
        compiler_params=pltpu.CompilerParams(vmem_limit_bytes=4 * 2**20),
    )(*(pltpu.with_memory_space_constraint(out, pltpu.VMEM) for out in outs))
    o_blk, o_inp, o_qkv, o_up, o_out, o_down, gain, shift, out_bias_grad, qkv_bias_grad, up_bias_grad = done
    return (
        o_blk,
        o_inp,
        gain.reshape(-1),
        shift.reshape(-1),
        jnp.transpose(o_qkv, (1, 0, 2)),
        qkv_bias_grad,
        o_out,
        out_bias_grad.reshape(-1),
        o_up,
        up_bias_grad.reshape(-1),
        o_down,
    )


def solution(mesh):
    in_specs = (
        P(DP, FEAT),
        P(DP, None),
        P(FEAT),
        P(FEAT),
        P(DP, None, FEAT),
        P(None, FEAT),
        P(),
        P(),
        P(FEAT, DP),
        P(FEAT),
        P(DP, FEAT),
        P(FEAT),
        P(FEAT, DP),
        P(DP, FEAT),
    )
    out_specs = (
        P(DP, FEAT),
        P(DP, FEAT),
        P(FEAT),
        P(FEAT),
        P(DP, None, FEAT),
        P(None, FEAT),
        P(FEAT, DP),
        P(FEAT),
        P(DP, FEAT),
        P(FEAT),
        P(FEAT, DP),
    )
    dp_count, feat_count = mesh.shape[DP], mesh.shape[FEAT]
    if (dp_count, feat_count) == (8, 4):
        per_device = functools.partial(on_device_fused, dp_count, feat_count)
    else:
        per_device = on_device
    return jax.shard_map(
        per_device, mesh=mesh, in_specs=in_specs, out_specs=out_specs, check_vma=False
    )
```
